32 devices in a mesh: row: 4 (over y, x), col: 8 (over z, core).
Axes of the slice: x: 2, y: 2, z: 4, core: 2. Of those that a mesh axis runs over, the one named last changes fastest.
Arguments:
- object_field: float32 [2, 2048, 4096], P(None, 'row', 'col'), may hold values from -6 to 6
- probe_field: float32 [2, 128, 128], replicated, may hold values from -1 to 1
- amplitudes: float32 [96, 128, 1024], P('row', None, 'col'), may hold values from 0 to 2
- positions: int32 [4, 8, 2, 24], P('row', 'col'), may hold values from -32 to 416
- counts: int32 [4, 8], P('row', 'col'), may hold values from 8 to 24, as said below
Outputs:
- estimate: float32 [2, 2048, 4096], P(None, 'row', 'col')
- correction: float32 [2, 2048, 4096], P(None, 'row', 'col')
The draws below stay inside these ranges and needn't reach their ends.
Inputs may be any that keep to these rules, and one draw needn't show every extreme that they name: `counts`: between 8 and 24 live slots per tile; some tile has exactly 24 and some exactly 8; slots at or beyond a tile's count carry data that is not used.
All inputs are finite; a program needn't handle non-finite values.
Results may differ from the reference program's by a relative error of at most 0.0001.
Values sent between devices are 32-bit elements; how exact they have to be, the bound alone decides.
No kernel may reach another device: no remote copies, remote signals or barrier semaphores. Data moves between devices by JAX's collectives and lax.ppermute only.
A program may use at most 128 MiB of HBM per device.

```python
import jax
import jax.numpy as jnp
from jax import lax

TILE = 512
PROBE = 128
BORDER = 32
PMAX = 24
PMIN = 8
ITERS = 2
TILE_ROWS = 4
TILE_COLS = 8
HEIGHT = 2048
WIDTH = 4096


def draw_counts(key, part):
    key_first, key_second, key_full, key_light = jax.random.split(key, 4)
    device_total = TILE_ROWS * TILE_COLS
    spread = PMAX - PMIN
    first_draw = jax.random.randint(key_first, (device_total,), 0, spread + 1)
    second_draw = jax.random.randint(key_second, (device_total,), 0, spread + 1)
    counts_flat = PMIN + first_draw * second_draw // spread
    fullest = jax.random.randint(key_full, (), 0, device_total)
    lightest = (fullest + 1 + jax.random.randint(key_light, (), 0, device_total - 1)) % device_total
    counts_flat = counts_flat.at[fullest].set(PMAX).at[lightest].set(PMIN)
    return counts_flat.reshape(TILE_ROWS, TILE_COLS).astype(jnp.int32)


def touch_ends(array, key, least, high):
    longest = array.shape.index(max(array.shape))
    spots = []
    for shift in (0, 1):
        where = [jax.random.randint(jax.random.fold_in(key, axis), (), 0, length) for axis, length in enumerate(array.shape)]
        where[longest] = (where[longest] + shift) % array.shape[longest]
        spots.append(tuple(where))
    return array.at[spots[0]].set(least).at[spots[1]].set(high)


def level_of(key, shape, pieces, low, high):
    gain, own = 1.0, jax.random.fold_in(key, 6)
    for dim, shards_of in pieces:
        heights = jnp.exp(jax.random.uniform(jax.random.fold_in(own, dim), (shards_of,), jnp.float32, low / len(pieces), high / len(pieces)))
        gain = gain * jnp.repeat(heights, shape[dim] // shards_of).reshape([-1 if axis == dim else 1 for axis in range(len(shape))])
    return gain


def centred(own_key, extent, scale, bound, pieces=(), held_as=jnp.bfloat16):
    array = jax.random.normal(own_key, extent, jnp.float32) * scale
    if len(pieces) > 0:
        array = level_of(own_key, extent, pieces, -0.22, 0.18) * array
    return jnp.clip(array, min=-bound, max=bound).astype(held_as)


def setup_inputs(seed: int = 0) -> dict:
    splits = jax.random.split(jax.random.key(seed), 6)
    return {
        "object_field": centred(splits[0], (2, HEIGHT, WIDTH), 1.0, 6.0, ((1, 4), (2, 8)), jnp.float32),
        "probe_field": jnp.clip(jax.random.uniform(splits[1], (2, PROBE, PROBE), jnp.float32, -1.0, 1.0), -1.0, 1.0),
        "amplitudes": jnp.clip(2.0 * jax.random.uniform(splits[2], (TILE_ROWS * PMAX, PROBE, TILE_COLS * PROBE), jnp.float32) ** level_of(splits[2], (TILE_ROWS * PMAX, PROBE, TILE_COLS * PROBE), ((0, 4), (2, 8)), -0.2, 0.2), 0.0, 2.0),
        "positions": touch_ends(jax.random.randint(splits[3], (TILE_ROWS, TILE_COLS, 2, PMAX), -BORDER, TILE - PROBE + BORDER + 1), jax.random.fold_in(splits[3], 1), -BORDER, TILE - PROBE + BORDER).astype(jnp.int32),
        "counts": draw_counts(jax.random.fold_in(splits[5], 71), 0),
    }


smoothing = 0.5
step_gain = 0.5
highest = lax.Precision.HIGHEST

def dft_tables(length):
    counter = jnp.arange(length, dtype=jnp.int32)
    product = counter[:, None] * counter[None, :] % length
    angles = 2.0 * jnp.pi / length * product.astype(jnp.float32)
    factor = 1.0 / jnp.sqrt(jnp.float32(length))
    return (jnp.cos(angles) * factor, -jnp.sin(angles) * factor)

def transform(real_part, imag_part, table_real, table_imag):
    left_real = jnp.einsum('kp,spq->skq', table_real, real_part, precision=highest) - jnp.einsum('kp,spq->skq', table_imag, imag_part, precision=highest)
    left_imag = jnp.einsum('kp,spq->skq', table_real, imag_part, precision=highest) + jnp.einsum('kp,spq->skq', table_imag, real_part, precision=highest)
    right_real = jnp.einsum('spq,qk->spk', left_real, table_real, precision=highest) - jnp.einsum('spq,qk->spk', left_imag, table_imag, precision=highest)
    right_imag = jnp.einsum('spq,qk->spk', left_real, table_imag, precision=highest) + jnp.einsum('spq,qk->spk', left_imag, table_real, precision=highest)
    return (right_real, right_imag)

def probe_gradient(patch_real, patch_imag, probe_field, amplitude, table_real, table_imag):
    probe_real = probe_field[0]
    probe_imag = probe_field[1]
    exit_real = probe_real * patch_real - probe_imag * patch_imag
    exit_imag = probe_real * patch_imag + probe_imag * patch_real
    wave_real, wave_imag = transform(exit_real, exit_imag, table_real, table_imag)
    modulus = jnp.sqrt(wave_real * wave_real + wave_imag * wave_imag + smoothing)
    shrink = amplitude / modulus - 1.0
    back_real, back_imag = transform(wave_real * shrink, wave_imag * shrink, table_real, -table_imag)
    grad_real = probe_real * back_real + probe_imag * back_imag
    grad_imag = probe_real * back_imag - probe_imag * back_real
    return (grad_real, grad_imag)

def reference(object_field, probe_field, amplitudes, positions, counts):
    table_real, table_imag = dft_tables(PROBE)
    step_rate = step_gain / (jnp.max(probe_field[0] * probe_field[0] + probe_field[1] * probe_field[1]) + 1e-06)
    row_base = jnp.arange(TILE_ROWS, dtype=jnp.int32)[:, None, None] * TILE
    col_base = jnp.arange(TILE_COLS, dtype=jnp.int32)[None, :, None] * TILE
    row_start = (positions[:, :, 0, :] + row_base + BORDER).astype(jnp.int32)
    col_start = (positions[:, :, 1, :] + col_base + BORDER).astype(jnp.int32)
    slot_ids = jnp.arange(PMAX, dtype=jnp.int32)[None, None, :]
    live_mask = (slot_ids < counts[:, :, None]).astype(jnp.float32)
    measured = amplitudes.reshape(TILE_ROWS, PMAX, PROBE, TILE_COLS, PROBE).transpose(0, 3, 1, 2, 4)
    zero_index = jnp.zeros((), jnp.int32)
    correction = jnp.zeros_like(object_field)
    for iteration in range(ITERS):
        padded = jnp.pad(object_field + correction, ((0, 0), (BORDER, BORDER), (BORDER, BORDER)))

        def cut_patch(start_row, start_col):
            return lax.dynamic_slice(padded, (zero_index, start_row, start_col), (2, PROBE, PROBE))

        def row_block(gradient_sum, block_items):
            block_rows, block_cols, block_mask, block_measured = block_items
            block_rows = block_rows.reshape(-1)
            block_cols = block_cols.reshape(-1)
            block_mask = block_mask.reshape(-1, 1, 1)
            block_measured = block_measured.reshape(-1, PROBE, PROBE)
            patches = jax.vmap(cut_patch)(block_rows, block_cols)
            grad_real, grad_imag = probe_gradient(patches[:, 0], patches[:, 1], probe_field, block_measured, table_real, table_imag)
            gradient = jnp.stack([grad_real * block_mask, grad_imag * block_mask], axis=1)

            def accumulate(slot_index, running):
                corner = (zero_index, block_rows[slot_index], block_cols[slot_index])
                current = lax.dynamic_slice(running, corner, (2, PROBE, PROBE))
                return lax.dynamic_update_slice(running, current + gradient[slot_index], corner)
            return (lax.fori_loop(0, gradient.shape[0], accumulate, gradient_sum), None)
        gradient_sum, unused = lax.scan(row_block, jnp.zeros_like(padded), (row_start, col_start, live_mask, measured))
        correction = correction + step_rate * gradient_sum[:, BORDER:BORDER + HEIGHT, BORDER:BORDER + WIDTH]
    return (object_field + correction, correction)
```

```python
import functools

import jax
import jax.numpy as jnp
import numpy as np
from jax import lax
from jax.experimental import pallas as pl
from jax.experimental.pallas import tpu as pltpu
from jax.sharding import PartitionSpec as P

BORDER = 32
BAND = 2 * BORDER
ITERS = 2
LANES = 128
SUBLANES = 8
GROUP = 4

smoothing = 0.5
step_gain = 0.5


def split_host(table):
    high = table.astype(jnp.bfloat16)
    low = (table - high.astype(np.float64)).astype(jnp.bfloat16)
    return high, low


def dft_blocks(length):
    counter = np.arange(length)
    angles = 2.0 * np.pi * (np.outer(counter, counter) % length) / length
    real, imag = np.cos(angles) / np.sqrt(length), -np.sin(angles) / np.sqrt(length)
    blocks = []
    for sign in (1.0, -1.0):
        right = np.block([[real, sign * imag], [-sign * imag, real]])
        high, low = split_host(right)
        blocks.append(np.concatenate([high, high, low], axis=0))
        left = np.block([[real, -sign * imag], [sign * imag, real]])
        high, low = split_host(left)
        blocks.append(np.concatenate([high, high, low], axis=1))
    return blocks


def split(value):
    high = value.astype(jnp.bfloat16)
    low = (value - high.astype(jnp.float32)).astype(jnp.bfloat16)
    return high, low


def dot(left, right):
    return jnp.dot(left, right, preferred_element_type=jnp.float32)


def times_right(rows, block):
    high, low = split(rows)
    return dot(jnp.concatenate([high, low, high], axis=1), block)


def times_left(block, columns):
    high, low = split(columns)
    return dot(block, jnp.concatenate([high, low, high], axis=0))


def lane_iota(rows):
    return lax.broadcasted_iota(jnp.int32, (rows, LANES), 1)


def edge_lanes(rows):
    lane = lane_iota(rows)
    return (lane < BORDER) | (lane >= LANES - BORDER)


def pack_planes(real, imag):
    return jnp.where(edge_lanes(real.shape[0]), real, pltpu.roll(imag, LANES // 2, 1))


def unpack_planes(packed):
    return packed, pltpu.roll(packed, LANES // 2, 1)


def gradient_slots(cur, acc, doubled, amplitudes, positions, live, tables):
    right_f, left_f, right_b, left_b = tables
    probe = doubled.shape[1] // 2
    frame = probe + SUBLANES
    lane = lane_iota(frame)
    sub = lax.broadcasted_iota(jnp.int32, (SUBLANES, LANES), 0)
    slot_total = amplitudes.shape[0]

    def group_body(group, carry):
        places, probes, exits = [], [], []
        for member in range(GROUP):
            slot = group * GROUP + member
            at = jnp.minimum(slot, slot_total - 1)
            row = positions[0, at] + BORDER
            col = positions[1, at] + LANES
            row_at = pl.multiple_of(row // SUBLANES * SUBLANES, SUBLANES)
            col_at = pl.multiple_of(col // LANES * LANES, LANES)
            row_off, col_off = row - row_at, col - col_at
            from_left = lane >= col_off
            from_top = sub >= row_off
            planes, rolled = [], []
            for plane in range(2):
                wide = jnp.where(
                    from_left,
                    cur[plane, pl.ds(row_at, frame), pl.ds(col_at, LANES)],
                    cur[plane, pl.ds(row_at, frame), pl.ds(col_at + LANES, LANES)],
                )
                first = jnp.where(from_top, wide[:SUBLANES], wide[probe:])
                planes.append(jnp.concatenate([first, wide[SUBLANES:probe]], axis=0))
                shifted = doubled[plane, pl.ds(probe - row_off, probe), :]
                rolled.append(pltpu.roll(shifted, col_off, 1))
            places.append((at, slot, row_at, col_at, from_left, from_top))
            probes.append(rolled)
            exits.append(
                jnp.concatenate(
                    [
                        rolled[0] * planes[0] - rolled[1] * planes[1],
                        rolled[0] * planes[1] + rolled[1] * planes[0],
                    ],
                    axis=1,
                )
            )
        half = times_right(jnp.concatenate(exits, axis=0), right_f[...])
        shrunk = []
        for pair in range(0, GROUP, 2):
            first = half[pair * probe : (pair + 1) * probe]
            second = half[(pair + 1) * probe : (pair + 2) * probe]
            stacked = jnp.concatenate(
                [
                    jnp.concatenate([first[:, :probe], second[:, :probe]], axis=1),
                    jnp.concatenate([first[:, probe:], second[:, probe:]], axis=1),
                ],
                axis=0,
            )
            wave = times_left(left_f[...], stacked)
            for member in range(2):
                at = places[pair + member][0]
                real = wave[:probe, member * probe : (member + 1) * probe]
                imag = wave[probe:, member * probe : (member + 1) * probe]
                shrink = amplitudes[at] * lax.rsqrt(real * real + imag * imag + smoothing) - 1.0
                shrunk.append(jnp.concatenate([real * shrink, imag * shrink], axis=1))
        half = times_right(jnp.concatenate(shrunk, axis=0), right_b[...])
        for pair in range(0, GROUP, 2):
            first = half[pair * probe : (pair + 1) * probe]
            second = half[(pair + 1) * probe : (pair + 2) * probe]
            stacked = jnp.concatenate(
                [
                    jnp.concatenate([first[:, :probe], second[:, :probe]], axis=1),
                    jnp.concatenate([first[:, probe:], second[:, probe:]], axis=1),
                ],
                axis=0,
            )
            back = times_left(left_b[...], stacked)
            for member in range(2):
                at, slot, row_at, col_at, from_left, from_top = places[pair + member]
                real = back[:probe, member * probe : (member + 1) * probe]
                imag = back[probe:, member * probe : (member + 1) * probe]
                rolled = probes[pair + member]
                grads = (
                    rolled[0] * real + rolled[1] * imag,
                    rolled[0] * imag - rolled[1] * real,
                )
                is_live = slot < live
                keep_left = from_left & is_live
                keep_right = jnp.logical_not(from_left) & is_live
                for plane in range(2):
                    grad = grads[plane]
                    frame_grad = jnp.concatenate(
                        [
                            jnp.where(from_top, grad[:SUBLANES], 0.0),
                            grad[SUBLANES:],
                            jnp.where(from_top, 0.0, grad[:SUBLANES]),
                        ],
                        axis=0,
                    )
                    rows = pl.ds(row_at, frame)
                    acc[plane, rows, pl.ds(col_at, LANES)] += jnp.where(keep_left, frame_grad, 0.0)
                    acc[plane, rows, pl.ds(col_at + LANES, LANES)] += jnp.where(
                        keep_right, frame_grad, 0.0
                    )
        return carry

    lax.fori_loop(0, (live + GROUP - 1) // GROUP, group_body, 0)


def double_probe(probe, doubled):
    size = probe.shape[1]
    for plane in range(2):
        doubled[plane, :size, :] = probe[plane]
        doubled[plane, size:, :] = probe[plane]


def step_of(probe):
    return step_gain / (jnp.max(probe[0] * probe[0] + probe[1] * probe[1]) + 1e-06)


def pack_row_band(acc, row, count, out):
    rows = slice(row, row + count)
    width = acc.shape[2] - 2 * LANES
    halo = []
    for plane in range(2):
        out[:, plane * width : (plane + 1) * width] = acc[plane, rows, LANES : LANES + width]
        halo.append(
            jnp.where(
                lane_iota(count) < BORDER,
                acc[plane, rows, LANES + width :],
                acc[plane, rows, :LANES],
            )
        )
    out[:, 2 * width :] = pack_planes(*halo)


def pack_side_bands(acc, height, to_left, to_right):
    width = acc.shape[2] - 2 * LANES
    is_low = lane_iota(height) < BORDER
    for out, high_block in ((to_left, 0), (to_right, width)):
        out[...] = pack_planes(
            *[
                jnp.where(
                    is_low,
                    acc[plane, :height, high_block + LANES : high_block + 2 * LANES],
                    acc[plane, :height, high_block : high_block + LANES],
                )
                for plane in range(2)
            ]
        )


def add_row_band(acc, row, band):
    count = band.shape[0]
    rows = slice(row, row + count)
    width = acc.shape[2] - 2 * LANES
    lane = lane_iota(count)
    halo = unpack_planes(band[:, 2 * width :])
    for plane in range(2):
        acc[plane, rows, LANES : LANES + width] += band[:, plane * width : (plane + 1) * width]
        acc[plane, rows, :LANES] += jnp.where(lane >= LANES - BORDER, halo[plane], 0.0)
        acc[plane, rows, LANES + width :] += jnp.where(lane < BORDER, halo[plane], 0.0)


def add_side_band(acc, block, band):
    height = band.shape[0]
    lane = lane_iota(height)
    both = unpack_planes(band[...])
    for plane in range(2):
        acc[plane, :height, block : block + LANES] += jnp.where(
            lane >= LANES - BORDER, both[plane], 0.0
        )
        acc[plane, :height, block + LANES : block + 2 * LANES] += jnp.where(
            lane < BORDER, both[plane], 0.0
        )


def object_pack_kernel(left, right, up_left, up_right, down_left, down_right, out):
    tile = left.shape[1]
    for row, low, high in (
        (0, up_left, up_right),
        (BORDER, left, right),
        (BORDER + tile, down_left, down_right),
    ):
        count = low.shape[1]
        is_low = lane_iota(count) < BORDER
        out[row : row + count, :] = pack_planes(
            *[jnp.where(is_low, low[plane], high[plane]) for plane in range(2)]
        )


def load_object(cur, objects, up, down, left, right):
    tile, width = objects.shape[1], objects.shape[2]
    extent = tile + BAND
    lane = lane_iota(extent)
    lefts, rights = unpack_planes(left[...]), unpack_planes(right[...])
    for plane in range(2):
        cur[plane, :extent, :LANES] = jnp.where(lane >= LANES - BORDER, lefts[plane], 0.0)
        cur[plane, :extent, LANES + width :] = jnp.where(lane < BORDER, rights[plane], 0.0)
        inner = slice(LANES, LANES + width)
        cur[plane, :BORDER, inner] = up[plane]
        cur[plane, BORDER : BORDER + tile, inner] = objects[plane]
        cur[plane, BORDER + tile : extent, inner] = down[plane]
        cur[plane, extent:, :] = jnp.zeros_like(cur[plane, extent:, :])


def first_kernel(
    positions, counts, objects, up, down, left, right, probe, amplitudes,
    right_f, left_f, right_b, left_b,
    acc, to_up, to_down, to_left, to_right, cur, doubled,
):
    tile = objects.shape[1]
    double_probe(probe, doubled)
    load_object(cur, objects, up, down, left, right)
    acc[...] = jnp.zeros_like(acc)
    gradient_slots(
        cur, acc, doubled, amplitudes, positions, counts[0, 0], (right_f, left_f, right_b, left_b)
    )
    pack_row_band(acc, 0, BAND, to_up)
    pack_row_band(acc, tile, BAND, to_down)
    pack_side_bands(acc, tile + BAND, to_left, to_right)


def corner_kernel(inset, up, down, left, right, to_left, to_right):
    count = up.shape[0]
    width = (up.shape[1] - LANES) // 2
    is_low = lane_iota(count) < BORDER
    for source, out, low_block, high_block in (
        (left, to_left, 0, None),
        (right, to_right, None, width - LANES),
    ):
        out[...] = source[...]
        for band, row in ((up, inset), (down, source.shape[0] - inset - count)):
            halo = unpack_planes(band[:, 2 * width :])
            parts = []
            for plane in range(2):
                if low_block is not None:
                    low = band[:, plane * width + low_block : plane * width + low_block + LANES]
                    parts.append(jnp.where(is_low, low, halo[plane]))
                else:
                    high = band[:, plane * width + high_block : plane * width + high_block + LANES]
                    parts.append(jnp.where(is_low, halo[plane], high))
            out[row : row + count, :] += pack_planes(*parts)


def second_kernel(
    row_count, col_count, positions, counts, objects, up, down, left, right, probe, amplitudes,
    right_f, left_f, right_b, left_b, first, band_up, band_down, band_left, band_right,
    base, to_up, to_down, to_left, to_right, cur, acc, doubled,
):
    tile, width = objects.shape[1], objects.shape[2]
    extent = tile + BAND
    rate = step_of(probe)
    double_probe(probe, doubled)
    load_object(cur, objects, up, down, left, right)
    acc[...] = first[...]
    add_row_band(acc, 0, band_up)
    add_row_band(acc, tile, band_down)
    add_side_band(acc, 0, band_left)
    add_side_band(acc, width, band_right)
    row_at, row_last = lax.axis_index("row"), row_count - 1
    col_at, col_last = lax.axis_index("col"), col_count - 1

    def rate_if(inside):
        return jnp.where(inside, rate, 0.0)

    inner = slice(LANES, LANES + width)
    middle = slice(BORDER, BORDER + tile)
    for plane in range(2):
        base[plane] = rate * acc[plane, middle, inner]
        cur[plane, middle, inner] += base[plane]
        for rows, row_in in (
            (slice(0, BORDER), row_at > 0),
            (middle, True),
            (slice(BORDER + tile, extent), row_at < row_last),
        ):
            for lanes, col_in in (
                (slice(0, LANES), col_at > 0),
                (inner, True),
                (slice(LANES + width, None), col_at < col_last),
            ):
                if row_in is True and col_in is True:
                    continue
                inside = col_in if row_in is True else row_in if col_in is True else row_in & col_in
                cur[plane, rows, lanes] += rate_if(inside) * acc[plane, rows, lanes]
    acc[...] = jnp.zeros_like(acc)
    gradient_slots(
        cur, acc, doubled, amplitudes, positions, counts[0, 0], (right_f, left_f, right_b, left_b)
    )
    for plane in range(2):
        base[plane] += rate * acc[plane, middle, inner]
    pack_row_band(acc, 0, BORDER, to_up)
    pack_row_band(acc, BORDER + tile, BORDER, to_down)
    pack_side_bands(acc, extent, to_left, to_right)


def last_kernel(objects, base, probe, up, down, left, right, estimate, correction):
    tile, width = objects.shape[1], objects.shape[2]
    rate = step_of(probe)
    lane = lane_iota(tile)
    lefts = unpack_planes(left[BORDER : BORDER + tile, :])
    rights = unpack_planes(right[BORDER : BORDER + tile, :])
    for plane in range(2):
        correction[plane] = base[plane]
        correction[plane, :BORDER, :] += rate * up[:, plane * width : (plane + 1) * width]
        correction[plane, tile - BORDER :, :] += rate * down[:, plane * width : (plane + 1) * width]
        correction[plane, :, :LANES] += rate * jnp.where(lane < BORDER, lefts[plane], 0.0)
        correction[plane, :, width - LANES :] += rate * jnp.where(
            lane >= LANES - BORDER, rights[plane], 0.0
        )
        estimate[plane] = objects[plane] + correction[plane]


VMEM = pl.BlockSpec(memory_space=pltpu.VMEM)
SMEM = pl.BlockSpec(memory_space=pltpu.SMEM)


def f32(*shape):
    return jax.ShapeDtypeStruct(shape, jnp.float32)


def swap_along(axis, to_before, to_after):
    count = lax.axis_size(axis)
    forth = [(i, i + 1) for i in range(count - 1)]
    back = [(i + 1, i) for i in range(count - 1)]
    return lax.ppermute(to_after, axis, forth), lax.ppermute(to_before, axis, back)


def on_device(object_field, probe_field, amplitudes, positions, counts):
    tile, width = object_field.shape[1:]
    probe = probe_field.shape[1]
    extent = tile + BAND
    padded = (2, extent + SUBLANES, width + 2 * LANES)
    row_band = 2 * width + LANES
    tables = dft_blocks(probe)
    places = positions[0, 0]
    last_block = width // LANES - 1

    up, down = swap_along(
        "row", object_field[:, :BORDER, :], object_field[:, tile - BORDER :, :]
    )

    def block_of(rows, index):
        return pl.BlockSpec((2, rows, LANES), lambda i: (0, 0, index))

    sides = pl.pallas_call(
        object_pack_kernel,
        grid=(1,),
        out_shape=f32(extent, LANES),
        in_specs=[
            block_of(rows, index) for rows in (tile, BORDER, BORDER) for index in (0, last_block)
        ],
        out_specs=pl.BlockSpec((extent, LANES), lambda i: (0, 0)),
        name="object_pack",
    )(object_field, object_field, up, up, down, down)
    left, right = swap_along("col", sides, sides)

    common = (object_field, up, down, left, right, probe_field, amplitudes, *tables)
    acc, to_up, to_down, to_left, to_right = pl.pallas_call(
        first_kernel,
        out_shape=(
            f32(*padded), f32(BAND, row_band), f32(BAND, row_band),
            f32(extent, LANES), f32(extent, LANES),
        ),
        in_specs=[SMEM, SMEM] + [VMEM] * len(common),
        out_specs=(VMEM,) * 5,
        scratch_shapes=[
            pltpu.VMEM(padded, jnp.float32), pltpu.VMEM((2, 2 * probe, probe), jnp.float32),
        ],
        name="first_iteration",
    )(places, counts, *common)
    band_up, band_down = swap_along("row", to_up, to_down)
    to_left, to_right = pl.pallas_call(
        functools.partial(corner_kernel, 0),
        out_shape=(f32(extent, LANES), f32(extent, LANES)),
        in_specs=[VMEM] * 4,
        out_specs=(VMEM,) * 2,
        name="corners",
    )(band_up, band_down, to_left, to_right)
    band_left, band_right = swap_along("col", to_left, to_right)

    bands = (acc, band_up, band_down, band_left, band_right)
    base, to_up, to_down, to_left, to_right = pl.pallas_call(
        functools.partial(second_kernel, lax.axis_size("row"), lax.axis_size("col")),
        out_shape=(
            f32(2, tile, width), f32(BORDER, row_band), f32(BORDER, row_band),
            f32(extent, LANES), f32(extent, LANES),
        ),
        in_specs=[SMEM, SMEM] + [VMEM] * (len(common) + len(bands)),
        out_specs=(VMEM,) * 5,
        scratch_shapes=[
            pltpu.VMEM(padded, jnp.float32), pltpu.VMEM(padded, jnp.float32),
            pltpu.VMEM((2, 2 * probe, probe), jnp.float32),
        ],
        name="second_iteration",
    )(places, counts, *common, *bands)
    band_up, band_down = swap_along("row", to_up, to_down)
    to_left, to_right = pl.pallas_call(
        functools.partial(corner_kernel, BORDER),
        out_shape=(f32(extent, LANES), f32(extent, LANES)),
        in_specs=[VMEM] * 4,
        out_specs=(VMEM,) * 2,
        name="last_corners",
    )(band_up, band_down, to_left, to_right)
    band_left, band_right = swap_along("col", to_left, to_right)
    estimate, correction = pl.pallas_call(
        last_kernel,
        out_shape=(f32(2, tile, width), f32(2, tile, width)),
        in_specs=[VMEM] * 7,
        out_specs=(VMEM,) * 2,
        name="finish",
    )(object_field, base, probe_field, band_up, band_down, band_left, band_right)
    return estimate, correction


def solution(mesh):
    placed = (
        P(None, "row", "col"),
        P(),
        P("row", None, "col"),
        P("row", "col", None, None),
        P("row", "col"),
    )
    return jax.shard_map(
        on_device,
        mesh=mesh,
        in_specs=placed,
        out_specs=(P(None, "row", "col"), P(None, "row", "col")),
        check_vma=False,
    )
```

```python
import functools

import jax
import jax.numpy as jnp
import numpy as np
from jax import lax
from jax.experimental import pallas as pl
from jax.experimental.pallas import tpu as pltpu
from jax.sharding import PartitionSpec as P

BORDER = 32
BAND = 2 * BORDER
ITERS = 2
LANES = 128
SUBLANES = 8
GROUP = 8
RIGHT = 4

smoothing = 0.5
step_gain = 0.5


def split_host(table):
    high = table.astype(jnp.bfloat16)
    low = (table - high.astype(np.float64)).astype(jnp.bfloat16)
    return high, low


def dft_blocks(length):
    counter = np.arange(length)
    angles = 2.0 * np.pi * (np.outer(counter, counter) % length) / length
    real, imag = np.cos(angles) / np.sqrt(length), -np.sin(angles) / np.sqrt(length)
    blocks = []
    for sign in (1.0, -1.0):
        right = np.block([[real, sign * imag], [-sign * imag, real]])
        high, low = split_host(right)
        blocks.append(np.concatenate([high, high, low], axis=0))
        left = np.block([[real, -sign * imag], [sign * imag, real]])
        high, low = split_host(left)
        blocks.append(np.concatenate([high, high, low], axis=1))
    return blocks


def split(value):
    high = value.astype(jnp.bfloat16)
    low = (value - high.astype(jnp.float32)).astype(jnp.bfloat16)
    return high, low


def dot(left, right):
    return jnp.dot(left, right, preferred_element_type=jnp.float32)


def times_right(rows, block):
    high, low = split(rows)
    return dot(jnp.concatenate([high, low, high], axis=1), block)


def right_groups(members, block):
    rows = members[0].shape[0]
    results = []
    for start in range(0, len(members), RIGHT):
        product = times_right(jnp.concatenate(members[start : start + RIGHT], axis=0), block[...])
        results += [product[i * rows : (i + 1) * rows] for i in range(RIGHT)]
    return results


def times_left(block, columns):
    high, low = split(columns)
    return dot(block, jnp.concatenate([high, low, high], axis=0))


def lane_iota(rows):
    return lax.broadcasted_iota(jnp.int32, (rows, LANES), 1)


def edge_lanes(rows):
    lane = lane_iota(rows)
    return (lane < BORDER) | (lane >= LANES - BORDER)


def pack_planes(real, imag):
    return jnp.where(edge_lanes(real.shape[0]), real, pltpu.roll(imag, LANES // 2, 1))


def unpack_planes(packed):
    return packed, pltpu.roll(packed, LANES // 2, 1)


def list_slots(order, positions, live, low, high, inside):
    def visit(slot, found):
        row, col = positions[0, slot], positions[1, slot]
        within = (row >= low) & (row <= high) & (col >= low) & (col <= high)
        order[found] = slot
        return found + jnp.where(within == inside, 1, 0)

    return lax.fori_loop(0, live, visit, 0)


def gradient_slots(cur, acc, doubled, amplitudes, positions, order, begin, stop, tables):
    right_f, left_f, right_b, left_b = tables
    probe = doubled.shape[1] // 2
    frame = probe + SUBLANES
    lane = lane_iota(frame)
    sub = lax.broadcasted_iota(jnp.int32, (SUBLANES, LANES), 0)

    def group_body(group, carry):
        places, probes, exits = [], [], []
        for member in range(GROUP):
            slot = begin + group * GROUP + member
            at = order[jnp.minimum(slot, stop - 1)]
            row = positions[0, at] + BORDER
            col = positions[1, at] + LANES
            row_at = pl.multiple_of(row // SUBLANES * SUBLANES, SUBLANES)
            col_at = pl.multiple_of(col // LANES * LANES, LANES)
            row_off, col_off = row - row_at, col - col_at
            from_left = lane >= col_off
            from_top = sub >= row_off
            planes, rolled = [], []
            for plane in range(2):
                wide = jnp.where(
                    from_left,
                    cur[plane, pl.ds(row_at, frame), pl.ds(col_at, LANES)],
                    cur[plane, pl.ds(row_at, frame), pl.ds(col_at + LANES, LANES)],
                )
                first = jnp.where(from_top, wide[:SUBLANES], wide[probe:])
                planes.append(jnp.concatenate([first, wide[SUBLANES:probe]], axis=0))
                shifted = doubled[plane, pl.ds(probe - row_off, probe), :]
                rolled.append(pltpu.roll(shifted, col_off, 1))
            places.append((at, slot, row_at, col_at, from_left, from_top))
            probes.append(rolled)
            exits.append(
                jnp.concatenate(
                    [
                        rolled[0] * planes[0] - rolled[1] * planes[1],
                        rolled[0] * planes[1] + rolled[1] * planes[0],
                    ],
                    axis=1,
                )
            )
        half = right_groups(exits, right_f)
        shrunk = []
        for pair in range(0, GROUP, 2):
            first, second = half[pair], half[pair + 1]
            stacked = jnp.concatenate(
                [
                    jnp.concatenate([first[:, :probe], second[:, :probe]], axis=1),
                    jnp.concatenate([first[:, probe:], second[:, probe:]], axis=1),
                ],
                axis=0,
            )
            wave = times_left(left_f[...], stacked)
            for member in range(2):
                at = places[pair + member][0]
                real = wave[:probe, member * probe : (member + 1) * probe]
                imag = wave[probe:, member * probe : (member + 1) * probe]
                shrink = amplitudes[at] * lax.rsqrt(real * real + imag * imag + smoothing) - 1.0
                shrunk.append(jnp.concatenate([real * shrink, imag * shrink], axis=1))
        half = right_groups(shrunk, right_b)
        for pair in range(0, GROUP, 2):
            first, second = half[pair], half[pair + 1]
            stacked = jnp.concatenate(
                [
                    jnp.concatenate([first[:, :probe], second[:, :probe]], axis=1),
                    jnp.concatenate([first[:, probe:], second[:, probe:]], axis=1),
                ],
                axis=0,
            )
            back = times_left(left_b[...], stacked)
            for member in range(2):
                at, slot, row_at, col_at, from_left, from_top = places[pair + member]
                real = back[:probe, member * probe : (member + 1) * probe]
                imag = back[probe:, member * probe : (member + 1) * probe]
                rolled = probes[pair + member]
                grads = (
                    rolled[0] * real + rolled[1] * imag,
                    rolled[0] * imag - rolled[1] * real,
                )
                is_live = slot < stop
                keep_left = from_left & is_live
                keep_right = jnp.logical_not(from_left) & is_live
                for plane in range(2):
                    grad = grads[plane]
                    frame_grad = jnp.concatenate(
                        [
                            jnp.where(from_top, grad[:SUBLANES], 0.0),
                            grad[SUBLANES:],
                            jnp.where(from_top, 0.0, grad[:SUBLANES]),
                        ],
                        axis=0,
                    )
                    rows = pl.ds(row_at, frame)
                    acc[plane, rows, pl.ds(col_at, LANES)] += jnp.where(keep_left, frame_grad, 0.0)
                    acc[plane, rows, pl.ds(col_at + LANES, LANES)] += jnp.where(
                        keep_right, frame_grad, 0.0
                    )
        return carry

    lax.fori_loop(0, (stop - begin + GROUP - 1) // GROUP, group_body, 0)


def double_probe(probe, doubled):
    size = probe.shape[1]
    for plane in range(2):
        doubled[plane, :size, :] = probe[plane]
        doubled[plane, size:, :] = probe[plane]


def step_of(probe):
    return step_gain / (jnp.max(probe[0] * probe[0] + probe[1] * probe[1]) + 1e-06)


def pack_row_band(acc, row, count, out):
    rows = slice(row, row + count)
    width = acc.shape[2] - 2 * LANES
    halo = []
    for plane in range(2):
        out[:, plane * width : (plane + 1) * width] = acc[plane, rows, LANES : LANES + width]
        halo.append(
            jnp.where(
                lane_iota(count) < BORDER,
                acc[plane, rows, LANES + width :],
                acc[plane, rows, :LANES],
            )
        )
    out[:, 2 * width :] = pack_planes(*halo)


def pack_side_bands(acc, height, to_left, to_right):
    width = acc.shape[2] - 2 * LANES
    is_low = lane_iota(height) < BORDER
    for out, high_block in ((to_left, 0), (to_right, width)):
        out[...] = pack_planes(
            *[
                jnp.where(
                    is_low,
                    acc[plane, :height, high_block + LANES : high_block + 2 * LANES],
                    acc[plane, :height, high_block : high_block + LANES],
                )
                for plane in range(2)
            ]
        )


def add_row_band(acc, row, band):
    count = band.shape[0]
    rows = slice(row, row + count)
    width = acc.shape[2] - 2 * LANES
    lane = lane_iota(count)
    halo = unpack_planes(band[:, 2 * width :])
    for plane in range(2):
        acc[plane, rows, LANES : LANES + width] += band[:, plane * width : (plane + 1) * width]
        acc[plane, rows, :LANES] += jnp.where(lane >= LANES - BORDER, halo[plane], 0.0)
        acc[plane, rows, LANES + width :] += jnp.where(lane < BORDER, halo[plane], 0.0)


def add_side_band(acc, block, band):
    height = band.shape[0]
    lane = lane_iota(height)
    both = unpack_planes(band[...])
    for plane in range(2):
        acc[plane, :height, block : block + LANES] += jnp.where(
            lane >= LANES - BORDER, both[plane], 0.0
        )
        acc[plane, :height, block + LANES : block + 2 * LANES] += jnp.where(
            lane < BORDER, both[plane], 0.0
        )


def inner_start_kernel(
    positions, counts, objects, probe, amplitudes, right_f, left_f, right_b, left_b,
    cur, acc, doubled, held, order, sems,
):
    tile, width = objects.shape[1:]
    loads = [
        pltpu.make_async_copy(
            objects.at[plane],
            cur.at[plane, pl.ds(BORDER, tile), pl.ds(LANES, width)],
            sems.at[plane],
        )
        for plane in range(2)
    ]
    loads.append(pltpu.make_async_copy(amplitudes, held, sems.at[2]))
    for load in loads:
        load.start()
    double_probe(probe, doubled)
    acc[...] = jnp.zeros_like(acc)
    found = list_slots(order, positions, counts[0, 0], 0, tile - probe.shape[1], True)
    for load in loads:
        load.wait()
    gradient_slots(
        cur, acc, doubled, held, positions, order, 0, jnp.minimum(found, GROUP),
        (right_f, left_f, right_b, left_b),
    )


def inner_rest_kernel(
    positions, counts, cur, doubled, amplitudes, right_f, left_f, right_b, left_b, acc_in,
    acc, order,
):
    tile = cur.shape[1] - SUBLANES - BAND
    found = list_slots(order, positions, counts[0, 0], 0, tile - doubled.shape[2], True)
    gradient_slots(
        cur, acc, doubled, amplitudes, positions, order, jnp.minimum(found, GROUP), found,
        (right_f, left_f, right_b, left_b),
    )


def object_pack_kernel(cur, up, down, out):
    count = up.shape[0]
    width = up.shape[1] // 2
    tile = out.shape[0] - 2 * count
    is_low = lane_iota(count) < BORDER
    for row, band in ((0, up), (count + tile, down)):
        out[row : row + count, :] = pack_planes(
            *[
                jnp.where(
                    is_low,
                    band[:, plane * width : plane * width + LANES],
                    band[:, (plane + 1) * width - LANES : (plane + 1) * width],
                )
                for plane in range(2)
            ]
        )
    rows = slice(count, count + tile)
    is_low = lane_iota(tile) < BORDER
    out[rows, :] = pack_planes(
        *[
            jnp.where(is_low, cur[plane, rows, LANES : 2 * LANES], cur[plane, rows, width : width + LANES])
            for plane in range(2)
        ]
    )


def outer_kernel(
    positions, counts, up, down, left, right, doubled, amplitudes,
    right_f, left_f, right_b, left_b, cur_in, acc_in,
    cur, acc, to_up, to_down, to_left, to_right, order,
):
    extent = left.shape[0]
    tile, width = extent - BAND, up.shape[1] // 2
    lane = lane_iota(extent)
    lefts, rights = unpack_planes(left[...]), unpack_planes(right[...])
    for plane in range(2):
        cur[plane, :extent, :LANES] = jnp.where(lane >= LANES - BORDER, lefts[plane], 0.0)
        cur[plane, :extent, LANES + width :] = jnp.where(lane < BORDER, rights[plane], 0.0)
        inner = slice(LANES, LANES + width)
        cur[plane, :BORDER, inner] = up[:, plane * width : (plane + 1) * width]
        cur[plane, BORDER + tile : extent, inner] = down[:, plane * width : (plane + 1) * width]
        cur[plane, extent:, :] = jnp.zeros_like(cur[plane, extent:, :])
    found = list_slots(order, positions, counts[0, 0], 0, tile - doubled.shape[2], False)
    gradient_slots(
        cur, acc, doubled, amplitudes, positions, order, 0, found, (right_f, left_f, right_b, left_b)
    )
    pack_row_band(acc, 0, BAND, to_up)
    pack_row_band(acc, tile, BAND, to_down)
    pack_side_bands(acc, extent, to_left, to_right)


def corner_kernel(inset, up, down, left, right, to_left, to_right):
    count = up.shape[0]
    width = (up.shape[1] - LANES) // 2
    is_low = lane_iota(count) < BORDER
    for source, out in ((left, to_left), (right, to_right)):
        out[...] = source[...]
        for band, row in ((up, inset), (down, source.shape[0] - inset - count)):
            halo = unpack_planes(band[:, 2 * width :])
            parts = []
            for plane in range(2):
                if out is to_left:
                    low = band[:, plane * width : plane * width + LANES]
                    parts.append(jnp.where(is_low, low, halo[plane]))
                else:
                    high = band[:, (plane + 1) * width - LANES : (plane + 1) * width]
                    parts.append(jnp.where(is_low, halo[plane], high))
            out[row : row + count, :] += pack_planes(*parts)


def deep_kernel(
    positions, counts, probe, doubled, amplitudes, right_f, left_f, right_b, left_b, cur_in, acc_in,
    cur, acc, order,
):
    tile, width = cur.shape[1] - SUBLANES - BAND, cur.shape[2] - 2 * LANES
    rate = step_of(probe)
    middle, inner = slice(BORDER, BORDER + tile), slice(LANES, LANES + width)
    for plane in range(2):
        cur[plane, middle, inner] += rate * acc[plane, middle, inner]
    found = list_slots(
        order, positions, counts[0, 0], BORDER, tile - doubled.shape[2] - BORDER, True
    )
    gradient_slots(
        cur, acc, doubled, amplitudes, positions, order, 0, found, (right_f, left_f, right_b, left_b)
    )


def second_kernel(
    row_count, col_count,
    positions, counts, probe, doubled, amplitudes, right_f, left_f, right_b, left_b,
    up, down, left, right, cur_in, acc_in,
    cur, acc, to_up, to_down, to_left, to_right, order,
):
    tile, width = cur.shape[1] - SUBLANES - BAND, cur.shape[2] - 2 * LANES
    extent = tile + BAND
    rate = step_of(probe)
    row_at, row_last = lax.axis_index("row"), row_count - 1
    col_at, col_last = lax.axis_index("col"), col_count - 1
    top = jnp.where(row_at > 0, 1.0, 0.0)
    bottom = jnp.where(row_at < row_last, 1.0, 0.0)
    before = jnp.where(col_at > 0, 1.0, 0.0)
    after = jnp.where(col_at < col_last, 1.0, 0.0)
    found = list_slots(
        order, positions, counts[0, 0], BORDER, tile - doubled.shape[2] - BORDER, False
    )
    inner = slice(LANES, LANES + width)
    lane = lane_iota(extent)
    is_low, is_high = lane < BORDER, lane >= LANES - BORDER
    lefts, rights = unpack_planes(left[...]), unpack_planes(right[...])
    row_id = lax.broadcasted_iota(jnp.int32, (extent, LANES), 0)
    row_gain = rate * jnp.where(
        row_id < BORDER, top, jnp.where(row_id >= BORDER + tile, bottom, 1.0)
    )
    for plane in range(2):
        for row, band, on_grid in ((0, up, top), (tile, down, bottom)):
            halo_first = row == 0
            values = band[:, plane * width : (plane + 1) * width]
            own, out = (BORDER, 0) if halo_first else (0, BORDER)
            own_rows = slice(row + own, row + own + BORDER)
            out_rows = slice(row + out, row + out + BORDER)
            cur[plane, own_rows, inner] += rate * values[own : own + BORDER]
            acc[plane, own_rows, inner] += values[own : own + BORDER]
            cur[plane, out_rows, inner] += (rate * on_grid) * (
                acc[plane, out_rows, inner] + values[out : out + BORDER]
            )
            acc[plane, out_rows, inner] = jnp.zeros_like(acc[plane, out_rows, inner])
            halo = unpack_planes(band[:, 2 * width :])[plane]
            for lanes, keep in (
                (slice(0, LANES), is_high[:BAND]),
                (slice(LANES + width, None), is_low[:BAND]),
            ):
                acc[plane, row : row + BAND, lanes] += jnp.where(keep, halo, 0.0)
        for block, band, on_grid, own_first in (
            (0, lefts[plane], before, False),
            (width, rights[plane], after, True),
        ):
            low_block = slice(block, block + LANES)
            high_block = slice(block + LANES, block + 2 * LANES)
            own, out = (low_block, high_block) if own_first else (high_block, low_block)
            keep_own, keep_out = (is_high, is_low) if own_first else (is_low, is_high)
            own_band = jnp.where(keep_own, band, 0.0)
            cur[plane, :extent, own] += row_gain * own_band
            acc[plane, BORDER : BORDER + tile, own] += own_band[BORDER : BORDER + tile]
            cur[plane, :extent, out] += (row_gain * on_grid) * (
                acc[plane, :extent, out] + jnp.where(keep_out, band, 0.0)
            )
            acc[plane, :extent, out] = jnp.zeros_like(acc[plane, :extent, out])
    gradient_slots(
        cur, acc, doubled, amplitudes, positions, order, 0, found, (right_f, left_f, right_b, left_b)
    )
    pack_row_band(acc, 0, BORDER, to_up)
    pack_row_band(acc, BORDER + tile, BORDER, to_down)
    pack_side_bands(acc, extent, to_left, to_right)


CHUNKS = 4


def last_kernel(
    objects, probe, up, down, left, right, acc, estimate, correction,
    held, estimated, corrected, load_sems, store_sems,
):
    tile, width = objects.shape[1:]
    step = tile // CHUNKS

    def rows_of(ref, chunk):
        return ref.at[:, pl.ds(chunk * step, step), :]

    loads = [
        pltpu.make_async_copy(rows_of(objects, i), rows_of(held, i), load_sems.at[i])
        for i in range(CHUNKS)
    ]
    for load in loads:
        load.start()
    rate = step_of(probe)
    lane = lane_iota(tile)
    rows = slice(BORDER, BORDER + tile)
    lefts, rights = unpack_planes(left[rows, :]), unpack_planes(right[rows, :])
    for plane in range(2):
        lanes = slice(plane * width, (plane + 1) * width)
        corrected[plane] = acc[plane, rows, LANES : LANES + width]
        corrected[plane, :BORDER, :] += up[:, lanes]
        corrected[plane, tile - BORDER :, :] += down[:, lanes]
        corrected[plane, :, :LANES] += jnp.where(lane < BORDER, lefts[plane], 0.0)
        corrected[plane, :, width - LANES :] += jnp.where(
            lane >= LANES - BORDER, rights[plane], 0.0
        )
    stores = []
    for i in range(CHUNKS):
        loads[i].wait()
        part = slice(i * step, (i + 1) * step)
        corrected[:, part, :] = rate * corrected[:, part, :]
        estimated[:, part, :] = held[:, part, :] + corrected[:, part, :]
        for number, (source, target) in enumerate(
            ((corrected, correction), (estimated, estimate))
        ):
            store = pltpu.make_async_copy(
                rows_of(source, i), rows_of(target, i), store_sems.at[number, i]
            )
            store.start()
            stores.append(store)
    for store in stores:
        store.wait()


VMEM = pl.BlockSpec(memory_space=pltpu.VMEM)
SMEM = pl.BlockSpec(memory_space=pltpu.SMEM)
ANY = pl.BlockSpec(memory_space=pl.ANY)
PARAMS = pltpu.CompilerParams(vmem_limit_bytes=32 * 1024 * 1024)


def f32(*shape):
    return pltpu.VMEM(shape, jnp.float32)


def in_vmem(array):
    return pltpu.with_memory_space_constraint(array, pltpu.VMEM)


def swap_along(axis, to_before, to_after):
    count = lax.axis_size(axis)
    forth = [(i, i + 1) for i in range(count - 1)]
    back = [(i + 1, i) for i in range(count - 1)]
    return (
        in_vmem(lax.ppermute(to_after, axis, forth)),
        in_vmem(lax.ppermute(to_before, axis, back)),
    )


def on_device(object_field, probe_field, amplitudes, positions, counts):
    tile, width = object_field.shape[1:]
    probe = probe_field.shape[1]
    extent = tile + BAND
    padded = f32(2, extent + SUBLANES, width + 2 * LANES)
    doubled_shape = f32(2, 2 * probe, probe)
    tables = tuple(in_vmem(jnp.asarray(table)) for table in dft_blocks(probe))
    places = positions[0, 0]
    order = pltpu.SMEM((amplitudes.shape[0],), jnp.int32)
    sides = (f32(extent, LANES), f32(extent, LANES))

    def row_bands(count):
        band = f32(count, 2 * width + LANES)
        return (band, band)

    def call(kernel, name, scalars, arrays, outs, scratch=(), aliases=None):
        return pl.pallas_call(
            kernel,
            out_shape=outs,
            in_specs=[SMEM] * len(scalars) + [VMEM] * len(arrays),
            out_specs=jax.tree.map(lambda out: VMEM, outs),
            scratch_shapes=list(scratch),
            input_output_aliases=aliases or {},
            compiler_params=PARAMS,
            name=name,
        )(*scalars, *arrays)

    slots = (places, counts)
    strips = [
        jnp.concatenate([object_field[0, rows], object_field[1, rows]], axis=1)
        for rows in (slice(0, BORDER), slice(tile - BORDER, tile))
    ]
    up, down = swap_along("row", *strips)
    cur, acc, doubled, held = pl.pallas_call(
        inner_start_kernel,
        out_shape=(padded, padded, doubled_shape, f32(*amplitudes.shape)),
        in_specs=[SMEM, SMEM, ANY, VMEM, ANY] + [VMEM] * 4,
        out_specs=(VMEM,) * 4,
        scratch_shapes=[order, pltpu.SemaphoreType.DMA((3,))],
        compiler_params=PARAMS,
        name="inner_start",
    )(*slots, object_field, probe_field, amplitudes, *tables)
    packed = call(object_pack_kernel, "object_pack", (), (cur, up, down), sides[0])
    left, right = swap_along("col", packed, packed)
    acc = call(
        inner_rest_kernel, "inner_rest", slots, (cur, doubled, held, *tables, acc),
        padded, (order,), {9: 0},
    )
    cur, acc, to_up, to_down, to_left, to_right = call(
        outer_kernel, "outer", slots, (up, down, left, right, doubled, held, *tables, cur, acc),
        (padded, padded, *row_bands(BAND), *sides), (order,), {12: 0, 13: 1},
    )
    up, down = swap_along("row", to_up, to_down)
    cur, acc = call(
        deep_kernel, "deep", slots, (probe_field, doubled, held, *tables, cur, acc),
        (padded, padded), (order,), {9: 0, 10: 1},
    )
    to_left, to_right = call(
        functools.partial(corner_kernel, 0), "corners", (), (up, down, to_left, to_right), sides
    )
    left, right = swap_along("col", to_left, to_right)
    cur, acc, to_up, to_down, to_left, to_right = call(
        functools.partial(second_kernel, lax.axis_size("row"), lax.axis_size("col")),
        "second", slots,
        (probe_field, doubled, held, *tables, up, down, left, right, cur, acc),
        (padded, padded, *row_bands(BORDER), *sides), (order,), {13: 0, 14: 1},
    )
    up, down = swap_along("row", to_up, to_down)
    to_left, to_right = call(
        functools.partial(corner_kernel, BORDER), "last_corners", (),
        (up, down, to_left, to_right), sides,
    )
    left, right = swap_along("col", to_left, to_right)
    whole = pltpu.VMEM((2, tile, width), jnp.float32)
    result = jax.ShapeDtypeStruct((2, tile, width), jnp.float32)
    estimate, correction = pl.pallas_call(
        last_kernel,
        out_shape=(result, result),
        in_specs=[ANY] + [VMEM] * 6,
        out_specs=(ANY, ANY),
        scratch_shapes=[
            whole, whole, whole,
            pltpu.SemaphoreType.DMA((CHUNKS,)), pltpu.SemaphoreType.DMA((2, CHUNKS)),
        ],
        compiler_params=PARAMS,
        name="finish",
    )(object_field, probe_field, up, down, left, right, acc)
    return estimate, correction


def solution(mesh):
    placed = (
        P(None, "row", "col"),
        P(),
        P("row", None, "col"),
        P("row", "col", None, None),
        P("row", "col"),
    )
    return jax.shard_map(
        on_device,
        mesh=mesh,
        in_specs=placed,
        out_specs=(P(None, "row", "col"), P(None, "row", "col")),
        check_vma=False,
    )
```

```python
import functools

import jax
import jax.numpy as jnp
import numpy as np
from jax import lax
from jax.experimental import pallas as pl
from jax.experimental.pallas import tpu as pltpu
from jax.sharding import PartitionSpec as P

BORDER = 32
BAND = 2 * BORDER
LANES = 128
SUBLANES = 8
GROUP = 8
RIGHT = 4

smoothing = 0.5
step_gain = 0.5


def split_host(table):
    high = table.astype(jnp.bfloat16)
    low = (table - high.astype(np.float64)).astype(jnp.bfloat16)
    return high, low


def dft_blocks(length):
    counter = np.arange(length)
    angles = 2.0 * np.pi * (np.outer(counter, counter) % length) / length
    real, imag = np.cos(angles) / np.sqrt(length), -np.sin(angles) / np.sqrt(length)
    blocks = []
    for sign in (1.0, -1.0):
        right = np.block([[real, sign * imag], [-sign * imag, real]])
        high, low = split_host(right)
        blocks.append(np.concatenate([high, high, low], axis=0))
        left = np.block([[real, -sign * imag], [sign * imag, real]])
        high, low = split_host(left)
        blocks.append(np.concatenate([high, high, low], axis=1))
    return blocks


def split(value):
    high = value.astype(jnp.bfloat16)
    low = (value - high.astype(jnp.float32)).astype(jnp.bfloat16)
    return high, low


def dot(left, right):
    return jnp.dot(left, right, preferred_element_type=jnp.float32)


def times_right(rows, block):
    high, low = split(rows)
    return dot(jnp.concatenate([high, low, high], axis=1), block)


def right_groups(members, block):
    rows = members[0].shape[0]
    results = []
    for start in range(0, len(members), RIGHT):
        product = times_right(jnp.concatenate(members[start : start + RIGHT], axis=0), block[...])
        results += [product[i * rows : (i + 1) * rows] for i in range(RIGHT)]
    return results


def times_left(block, columns):
    high, low = split(columns)
    return dot(block, jnp.concatenate([high, low, high], axis=0))


def lane_iota(rows):
    return lax.broadcasted_iota(jnp.int32, (rows, LANES), 1)


def edge_lanes(rows):
    lane = lane_iota(rows)
    return (lane < BORDER) | (lane >= LANES - BORDER)


def pack_planes(real, imag):
    return jnp.where(edge_lanes(real.shape[0]), real, pltpu.roll(imag, LANES // 2, 1))


def unpack_planes(packed):
    return packed, pltpu.roll(packed, LANES // 2, 1)


def list_slots(order, positions, live, low, high, inside):
    def visit(slot, found):
        row, col = positions[0, slot], positions[1, slot]
        within = (row >= low) & (row <= high) & (col >= low) & (col <= high)
        order[found] = slot
        return found + jnp.where(within == inside, 1, 0)

    return lax.fori_loop(0, live, visit, 0)


def gradient_slots(cur, acc, doubled, amplitudes, positions, order, begin, stop, tables):
    right_f, left_f, right_b, left_b = tables
    probe = doubled.shape[1] // 2
    frame = probe + SUBLANES
    lane = lane_iota(frame)
    sub = lax.broadcasted_iota(jnp.int32, (SUBLANES, LANES), 0)

    def group_body(group, carry):
        places, probes, exits = [], [], []
        for member in range(GROUP):
            slot = begin + group * GROUP + member
            at = order[jnp.minimum(slot, stop - 1)]
            row = positions[0, at] + BORDER
            col = positions[1, at] + LANES
            row_at = pl.multiple_of(row // SUBLANES * SUBLANES, SUBLANES)
            col_at = pl.multiple_of(col // LANES * LANES, LANES)
            row_off, col_off = row - row_at, col - col_at
            from_left = lane >= col_off
            from_top = sub >= row_off
            planes, rolled = [], []
            for plane in range(2):
                wide = jnp.where(
                    from_left,
                    cur[plane, pl.ds(row_at, frame), pl.ds(col_at, LANES)],
                    cur[plane, pl.ds(row_at, frame), pl.ds(col_at + LANES, LANES)],
                )
                first = jnp.where(from_top, wide[:SUBLANES], wide[probe:])
                planes.append(jnp.concatenate([first, wide[SUBLANES:probe]], axis=0))
                shifted = doubled[plane, pl.ds(probe - row_off, probe), :]
                rolled.append(pltpu.roll(shifted, col_off, 1))
            places.append((at, slot, row_at, col_at, from_left, from_top))
            probes.append(rolled)
            exits.append(
                jnp.concatenate(
                    [
                        rolled[0] * planes[0] - rolled[1] * planes[1],
                        rolled[0] * planes[1] + rolled[1] * planes[0],
                    ],
                    axis=1,
                )
            )
        half = right_groups(exits, right_f)
        shrunk = []
        for pair in range(0, GROUP, 2):
            first, second = half[pair], half[pair + 1]
            stacked = jnp.concatenate(
                [
                    jnp.concatenate([first[:, :probe], second[:, :probe]], axis=1),
                    jnp.concatenate([first[:, probe:], second[:, probe:]], axis=1),
                ],
                axis=0,
            )
            wave = times_left(left_f[...], stacked)
            for member in range(2):
                at = places[pair + member][0]
                real = wave[:probe, member * probe : (member + 1) * probe]
                imag = wave[probe:, member * probe : (member + 1) * probe]
                shrink = amplitudes[at] * lax.rsqrt(real * real + imag * imag + smoothing) - 1.0
                shrunk.append(jnp.concatenate([real * shrink, imag * shrink], axis=1))
        half = right_groups(shrunk, right_b)
        for pair in range(0, GROUP, 2):
            first, second = half[pair], half[pair + 1]
            stacked = jnp.concatenate(
                [
                    jnp.concatenate([first[:, :probe], second[:, :probe]], axis=1),
                    jnp.concatenate([first[:, probe:], second[:, probe:]], axis=1),
                ],
                axis=0,
            )
            back = times_left(left_b[...], stacked)
            for member in range(2):
                at, slot, row_at, col_at, from_left, from_top = places[pair + member]
                real = back[:probe, member * probe : (member + 1) * probe]
                imag = back[probe:, member * probe : (member + 1) * probe]
                rolled = probes[pair + member]
                grads = (
                    rolled[0] * real + rolled[1] * imag,
                    rolled[0] * imag - rolled[1] * real,
                )
                is_live = slot < stop
                keep_left = from_left & is_live
                keep_right = jnp.logical_not(from_left) & is_live
                for plane in range(2):
                    grad = grads[plane]
                    frame_grad = jnp.concatenate(
                        [
                            jnp.where(from_top, grad[:SUBLANES], 0.0),
                            grad[SUBLANES:],
                            jnp.where(from_top, 0.0, grad[:SUBLANES]),
                        ],
                        axis=0,
                    )
                    rows = pl.ds(row_at, frame)
                    acc[plane, rows, pl.ds(col_at, LANES)] += jnp.where(keep_left, frame_grad, 0.0)
                    acc[plane, rows, pl.ds(col_at + LANES, LANES)] += jnp.where(
                        keep_right, frame_grad, 0.0
                    )
        return carry

    lax.fori_loop(0, (stop - begin + GROUP - 1) // GROUP, group_body, 0)


def step_of(probe):
    return step_gain / (jnp.max(probe[0] * probe[0] + probe[1] * probe[1]) + 1e-06)


def pack_row_band(acc, row, count, out):
    rows = slice(row, row + count)
    width = acc.shape[2] - 2 * LANES
    halo = []
    for plane in range(2):
        out[:, plane * width : (plane + 1) * width] = acc[plane, rows, LANES : LANES + width]
        halo.append(
            jnp.where(
                lane_iota(count) < BORDER,
                acc[plane, rows, LANES + width :],
                acc[plane, rows, :LANES],
            )
        )
    out[:, 2 * width :] = pack_planes(*halo)


def pack_side_bands(acc, height, to_left, to_right):
    width = acc.shape[2] - 2 * LANES
    is_low = lane_iota(height) < BORDER
    for out, high_block in ((to_left, 0), (to_right, width)):
        out[...] = pack_planes(
            *[
                jnp.where(
                    is_low,
                    acc[plane, :height, high_block + LANES : high_block + 2 * LANES],
                    acc[plane, :height, high_block : high_block + LANES],
                )
                for plane in range(2)
            ]
        )


def inner_start_kernel(
    positions, counts, objects, probe_in, amplitudes, *refs
):
    table_count = (len(refs) - 6) // 2
    tables_in, refs = refs[:table_count], refs[table_count:]
    cur, acc, doubled, held = refs[:4]
    tables, (order, sems) = refs[4:-2], refs[-2:]
    tile, width = objects.shape[1:]
    probe = probe_in.shape[1]
    sources = [(amplitudes, held)] + list(zip(tables_in, tables))
    for plane in range(2):
        sources.append(
            (
                objects.at[plane],
                cur.at[plane, pl.ds(BORDER, tile), pl.ds(LANES, width)],
            )
        )
        for row in (0, probe):
            sources.append((probe_in.at[plane], doubled.at[plane, pl.ds(row, probe), :]))
    loads = [
        pltpu.make_async_copy(source, target, sems.at[i])
        for i, (source, target) in enumerate(sources)
    ]
    for load in loads:
        load.start()
    acc[...] = jnp.zeros_like(acc)
    found = list_slots(order, positions, counts[0, 0], 0, tile - probe, True)
    for load in loads:
        load.wait()
    gradient_slots(
        cur, acc, doubled, held, positions, order, 0, jnp.minimum(found, GROUP), tables
    )


def inner_rest_kernel(
    positions, counts, cur, doubled, amplitudes, right_f, left_f, right_b, left_b, acc_in,
    acc, order,
):
    tile = cur.shape[1] - SUBLANES - BAND
    found = list_slots(order, positions, counts[0, 0], 0, tile - doubled.shape[2], True)
    gradient_slots(
        cur, acc, doubled, amplitudes, positions, order, jnp.minimum(found, GROUP), found,
        (right_f, left_f, right_b, left_b),
    )


def object_pack_kernel(cur, up, down, out):
    count = up.shape[0]
    width = up.shape[1] // 2
    tile = out.shape[0] - 2 * count
    is_low = lane_iota(count) < BORDER
    for row, band in ((0, up), (count + tile, down)):
        out[row : row + count, :] = pack_planes(
            *[
                jnp.where(
                    is_low,
                    band[:, plane * width : plane * width + LANES],
                    band[:, (plane + 1) * width - LANES : (plane + 1) * width],
                )
                for plane in range(2)
            ]
        )
    rows = slice(count, count + tile)
    is_low = lane_iota(tile) < BORDER
    out[rows, :] = pack_planes(
        *[
            jnp.where(is_low, cur[plane, rows, LANES : 2 * LANES], cur[plane, rows, width : width + LANES])
            for plane in range(2)
        ]
    )


def outer_kernel(
    positions, counts, up, down, left, right, doubled, amplitudes,
    right_f, left_f, right_b, left_b, cur_in, acc_in,
    cur, acc, to_up, to_down, to_left, to_right, order,
):
    extent = left.shape[0]
    tile, width = extent - BAND, up.shape[1] // 2
    lane = lane_iota(extent)
    lefts, rights = unpack_planes(left[...]), unpack_planes(right[...])
    for plane in range(2):
        cur[plane, :extent, :LANES] = jnp.where(lane >= LANES - BORDER, lefts[plane], 0.0)
        cur[plane, :extent, LANES + width :] = jnp.where(lane < BORDER, rights[plane], 0.0)
        inner = slice(LANES, LANES + width)
        cur[plane, :BORDER, inner] = up[:, plane * width : (plane + 1) * width]
        cur[plane, BORDER + tile : extent, inner] = down[:, plane * width : (plane + 1) * width]
        cur[plane, extent:, :] = jnp.zeros_like(cur[plane, extent:, :])
    found = list_slots(order, positions, counts[0, 0], 0, tile - doubled.shape[2], False)
    gradient_slots(
        cur, acc, doubled, amplitudes, positions, order, 0, found, (right_f, left_f, right_b, left_b)
    )
    pack_row_band(acc, 0, BAND, to_up)
    pack_row_band(acc, tile, BAND, to_down)
    pack_side_bands(acc, extent, to_left, to_right)


def corner_parts(band, width):
    is_low = lane_iota(band.shape[0]) < BORDER
    halo = unpack_planes(band[:, 2 * width :])
    lefts, rights = [], []
    for plane in range(2):
        low = band[:, plane * width : plane * width + LANES]
        high = band[:, (plane + 1) * width - LANES : (plane + 1) * width]
        lefts.append(jnp.where(is_low, low, halo[plane]))
        rights.append(jnp.where(is_low, halo[plane], high))
    return pack_planes(*lefts), pack_planes(*rights)


def corner_kernel(up, down, after, to_left, to_right):
    count = up.shape[0]
    width = (up.shape[1] - LANES) // 2
    for row, band in ((0, up), (count, down)):
        to_left[row : row + count, :], to_right[row : row + count, :] = corner_parts(band, width)


def half_lanes(rows, first):
    low = lane_iota(rows) % (LANES // 2) < BORDER
    return low if first else jnp.logical_not(low)


def last_corner_kernel(up, down, left, right, to_left, to_right, whole):
    count = up.shape[0]
    tile = left.shape[0] - BAND
    width = (up.shape[1] - LANES) // 2
    half = tile // 2
    tops, bottoms = corner_parts(up, width), corner_parts(down, width)
    for side, (source, out) in enumerate(((left, to_left), (right, to_right))):
        whole[...] = source[BORDER : BORDER + tile, :]
        whole[:count, :] += tops[side]
        whole[tile - count :, :] += bottoms[side]
        out[...] = jnp.where(
            half_lanes(half, side == 1), whole[:half, :], pltpu.roll(whole[half:, :], BORDER, 1)
        )


def unfold_side(packed):
    both = jnp.concatenate([packed, pltpu.roll(packed, LANES - BORDER, 1)], axis=0)
    return unpack_planes(both)


def deep_kernel(
    positions, counts, probe, doubled, amplitudes, right_f, left_f, right_b, left_b, cur_in, acc_in,
    cur, acc, order,
):
    tile, width = cur.shape[1] - SUBLANES - BAND, cur.shape[2] - 2 * LANES
    rate = step_of(probe)
    middle, inner = slice(BORDER, BORDER + tile), slice(LANES, LANES + width)
    for plane in range(2):
        cur[plane, middle, inner] += rate * acc[plane, middle, inner]
    found = list_slots(
        order, positions, counts[0, 0], BORDER, tile - doubled.shape[2] - BORDER, True
    )
    gradient_slots(
        cur, acc, doubled, amplitudes, positions, order, 0, found, (right_f, left_f, right_b, left_b)
    )


def second_kernel(
    row_count, col_count,
    positions, counts, probe, doubled, amplitudes, right_f, left_f, right_b, left_b,
    up, down, left, right, left_corners, right_corners, cur_in, acc_in,
    cur, acc, to_up, to_down, to_left, to_right, order,
):
    tile, width = cur.shape[1] - SUBLANES - BAND, cur.shape[2] - 2 * LANES
    extent = tile + BAND
    rate = step_of(probe)
    row_at, row_last = lax.axis_index("row"), row_count - 1
    col_at, col_last = lax.axis_index("col"), col_count - 1
    top = jnp.where(row_at > 0, 1.0, 0.0)
    bottom = jnp.where(row_at < row_last, 1.0, 0.0)
    before = jnp.where(col_at > 0, 1.0, 0.0)
    after = jnp.where(col_at < col_last, 1.0, 0.0)
    found = list_slots(
        order, positions, counts[0, 0], BORDER, tile - doubled.shape[2] - BORDER, False
    )
    inner = slice(LANES, LANES + width)
    lane = lane_iota(extent)
    is_low, is_high = lane < BORDER, lane >= LANES - BORDER
    lefts, rights = (
        unpack_planes(
            jnp.concatenate(
                [
                    side[:BAND, :] + corners[:BAND, :],
                    side[BAND:tile, :],
                    side[tile:, :] + corners[BAND:, :],
                ],
                axis=0,
            )
        )
        for side, corners in ((left, left_corners), (right, right_corners))
    )
    row_id = lax.broadcasted_iota(jnp.int32, (extent, LANES), 0)
    row_gain = rate * jnp.where(
        row_id < BORDER, top, jnp.where(row_id >= BORDER + tile, bottom, 1.0)
    )
    for plane in range(2):
        for row, band, on_grid in ((0, up, top), (tile, down, bottom)):
            halo_first = row == 0
            values = band[:, plane * width : (plane + 1) * width]
            own, out = (BORDER, 0) if halo_first else (0, BORDER)
            own_rows = slice(row + own, row + own + BORDER)
            out_rows = slice(row + out, row + out + BORDER)
            cur[plane, own_rows, inner] += rate * values[own : own + BORDER]
            acc[plane, own_rows, inner] += values[own : own + BORDER]
            cur[plane, out_rows, inner] += (rate * on_grid) * (
                acc[plane, out_rows, inner] + values[out : out + BORDER]
            )
            acc[plane, out_rows, inner] = jnp.zeros_like(acc[plane, out_rows, inner])
            halo = unpack_planes(band[:, 2 * width :])[plane]
            for lanes, keep in (
                (slice(0, LANES), is_high[:BAND]),
                (slice(LANES + width, None), is_low[:BAND]),
            ):
                acc[plane, row : row + BAND, lanes] += jnp.where(keep, halo, 0.0)
        for block, band, on_grid, own_first in (
            (0, lefts[plane], before, False),
            (width, rights[plane], after, True),
        ):
            low_block = slice(block, block + LANES)
            high_block = slice(block + LANES, block + 2 * LANES)
            own, out = (low_block, high_block) if own_first else (high_block, low_block)
            keep_own, keep_out = (is_high, is_low) if own_first else (is_low, is_high)
            own_band = jnp.where(keep_own, band, 0.0)
            cur[plane, :extent, own] += row_gain * own_band
            acc[plane, BORDER : BORDER + tile, own] += own_band[BORDER : BORDER + tile]
            cur[plane, :extent, out] += (row_gain * on_grid) * (
                acc[plane, :extent, out] + jnp.where(keep_out, band, 0.0)
            )
            acc[plane, :extent, out] = jnp.zeros_like(acc[plane, :extent, out])
    gradient_slots(
        cur, acc, doubled, amplitudes, positions, order, 0, found, (right_f, left_f, right_b, left_b)
    )
    pack_row_band(acc, 0, BORDER, to_up)
    pack_row_band(acc, BORDER + tile, BORDER, to_down)
    pack_side_bands(acc, extent, to_left, to_right)


CHUNKS = 4


def last_kernel(
    objects, probe, up, down, left, right, acc, estimate, correction,
    held, estimated, corrected, load_sems, store_sems,
):
    tile, width = objects.shape[1:]
    step = tile // CHUNKS

    def rows_of(ref, chunk):
        return ref.at[:, pl.ds(chunk * step, step), :]

    loads = [
        pltpu.make_async_copy(rows_of(objects, i), rows_of(held, i), load_sems.at[i])
        for i in range(CHUNKS)
    ]
    for load in loads:
        load.start()
    rate = step_of(probe)
    lane = lane_iota(tile)
    rows = slice(BORDER, BORDER + tile)
    lefts, rights = unfold_side(left[...]), unfold_side(right[...])
    for plane in range(2):
        lanes = slice(plane * width, (plane + 1) * width)
        corrected[plane] = acc[plane, rows, LANES : LANES + width]
        corrected[plane, :BORDER, :] += up[:, lanes]
        corrected[plane, tile - BORDER :, :] += down[:, lanes]
        corrected[plane, :, :LANES] += jnp.where(lane < BORDER, lefts[plane], 0.0)
        corrected[plane, :, width - LANES :] += jnp.where(
            lane >= LANES - BORDER, rights[plane], 0.0
        )
    stores = []
    for i in range(CHUNKS):
        loads[i].wait()
        part = slice(i * step, (i + 1) * step)
        corrected[:, part, :] = rate * corrected[:, part, :]
        estimated[:, part, :] = held[:, part, :] + corrected[:, part, :]
        for number, (source, target) in enumerate(
            ((corrected, correction), (estimated, estimate))
        ):
            store = pltpu.make_async_copy(
                rows_of(source, i), rows_of(target, i), store_sems.at[number, i]
            )
            store.start()
            stores.append(store)
    for store in stores:
        store.wait()


VMEM = pl.BlockSpec(memory_space=pltpu.VMEM)
SMEM = pl.BlockSpec(memory_space=pltpu.SMEM)
HBM = pl.BlockSpec(memory_space=pltpu.HBM)
PARAMS = pltpu.CompilerParams(vmem_limit_bytes=32 * 1024 * 1024)


def f32(*shape):
    return pltpu.VMEM(shape, jnp.float32)


def in_hbm(array):
    return pltpu.with_memory_space_constraint(array, pltpu.HBM)


def in_vmem(array):
    return pltpu.with_memory_space_constraint(array, pltpu.VMEM)


def swap_along(axis, to_before, to_after):
    count = lax.axis_size(axis)
    forth = [(i, i + 1) for i in range(count - 1)]
    back = [(i + 1, i) for i in range(count - 1)]
    return (
        in_vmem(lax.ppermute(to_after, axis, forth)),
        in_vmem(lax.ppermute(to_before, axis, back)),
    )


def on_device(object_field, probe_field, amplitudes, positions, counts):
    tile, width = object_field.shape[1:]
    probe = probe_field.shape[1]
    extent = tile + BAND
    padded = f32(2, extent + SUBLANES, width + 2 * LANES)
    doubled_shape = f32(2, 2 * probe, probe)
    tables = tuple(jnp.asarray(table) for table in dft_blocks(probe))
    places = positions[0, 0]
    order = pltpu.SMEM((amplitudes.shape[0],), jnp.int32)
    sides = (f32(extent, LANES), f32(extent, LANES))

    def row_bands(count):
        band = f32(count, 2 * width + LANES)
        return (band, band)

    def call(kernel, scalars, arrays, outs, scratch=(), aliases=None):
        return pl.pallas_call(
            kernel,
            out_shape=outs,
            in_specs=[SMEM] * len(scalars) + [VMEM] * len(arrays),
            out_specs=jax.tree.map(lambda out: VMEM, outs),
            scratch_shapes=list(scratch),
            input_output_aliases=aliases or {},
            compiler_params=PARAMS,
        )(*scalars, *arrays)

    slots = (places, counts)
    strips = [
        jnp.concatenate([object_field[0, rows], object_field[1, rows]], axis=1)
        for rows in (slice(0, BORDER), slice(tile - BORDER, tile))
    ]
    table_shapes = tuple(pltpu.VMEM(table.shape, table.dtype) for table in tables)
    up, down = swap_along("row", *strips)
    cur, acc, doubled, held, *tables = pl.pallas_call(
        inner_start_kernel,
        out_shape=(padded, padded, doubled_shape, f32(*amplitudes.shape), *table_shapes),
        in_specs=[SMEM, SMEM] + [HBM] * (3 + len(tables)),
        out_specs=(VMEM,) * (4 + len(tables)),
        scratch_shapes=[order, pltpu.SemaphoreType.DMA((7 + len(tables),))],
        compiler_params=PARAMS,
        name="inner_start",
    )(*slots, *map(in_hbm, (object_field, probe_field, amplitudes, *tables)))
    packed = call(object_pack_kernel, (), (cur, up, down), sides[0])
    left, right = swap_along("col", packed, packed)
    acc = call(
        inner_rest_kernel, slots, (cur, doubled, held, *tables, acc),
        padded, (order,), {9: 0},
    )
    cur, acc, to_up, to_down, to_left, to_right = call(
        outer_kernel, slots, (up, down, left, right, doubled, held, *tables, cur, acc),
        (padded, padded, *row_bands(BAND), *sides), (order,), {12: 0, 13: 1},
    )
    up, down = swap_along("row", to_up, to_down)
    left, right = swap_along("col", to_left, to_right)
    cur, acc = call(
        deep_kernel, slots, (probe_field, doubled, held, *tables, cur, acc),
        (padded, padded), (order,), {9: 0, 10: 1},
    )
    corners = (f32(2 * BAND, LANES),) * 2
    left_corners, right_corners = swap_along("col", *call(corner_kernel, (), (up, down, acc), corners))
    cur, acc, to_up, to_down, to_left, to_right = call(
        functools.partial(second_kernel, lax.axis_size("row"), lax.axis_size("col")),
        slots,
        (
            probe_field, doubled, held, *tables,
            up, down, left, right, left_corners, right_corners, cur, acc,
        ),
        (padded, padded, *row_bands(BORDER), *sides), (order,), {15: 0, 16: 1},
    )
    up, down = swap_along("row", to_up, to_down)
    folded = f32(tile // 2, LANES)
    to_left, to_right = call(
        last_corner_kernel, (), (up, down, to_left, to_right),
        (folded, folded), (f32(tile, LANES),),
    )
    left, right = swap_along("col", to_left, to_right)
    whole = pltpu.VMEM((2, tile, width), jnp.float32)
    result = jax.ShapeDtypeStruct((2, tile, width), jnp.float32)
    estimate, correction = pl.pallas_call(
        last_kernel,
        out_shape=(result, result),
        in_specs=[HBM] + [VMEM] * 6,
        out_specs=(HBM, HBM),
        scratch_shapes=[
            whole, whole, whole,
            pltpu.SemaphoreType.DMA((CHUNKS,)), pltpu.SemaphoreType.DMA((2, CHUNKS)),
        ],
        compiler_params=PARAMS,
        name="finish",
    )(in_hbm(object_field), probe_field, up, down, left, right, acc)
    return estimate, correction


def solution(mesh):
    placed = (
        P(None, "row", "col"),
        P(),
        P("row", None, "col"),
        P("row", "col", None, None),
        P("row", "col"),
    )
    return jax.shard_map(
        on_device,
        mesh=mesh,
        in_specs=placed,
        out_specs=(P(None, "row", "col"), P(None, "row", "col")),
        check_vma=False,
    )
```

```python
import functools

import jax
import jax.numpy as jnp
import numpy as np
from jax import lax
from jax.experimental import pallas as pl
from jax.experimental.pallas import tpu as pltpu
from jax.sharding import PartitionSpec as P

BORDER = 32
BAND = 2 * BORDER
LANES = 128
SUBLANES = 8
GROUP = 8
RIGHT = 4

smoothing = 0.5
step_gain = 0.5


def split_host(table):
    high = table.astype(jnp.bfloat16)
    low = (table - high.astype(np.float64)).astype(jnp.bfloat16)
    return high, low


def dft_blocks(length):
    counter = np.arange(length)
    angles = 2.0 * np.pi * (np.outer(counter, counter) % length) / length
    real, imag = np.cos(angles) / np.sqrt(length), -np.sin(angles) / np.sqrt(length)
    blocks = []
    for sign in (1.0, -1.0):
        right = np.block([[real, sign * imag], [-sign * imag, real]])
        high, low = split_host(right)
        blocks.append(np.concatenate([high, high, low], axis=0))
        left = np.block([[real, -sign * imag], [sign * imag, real]])
        high, low = split_host(left)
        blocks.append(np.concatenate([high, high, low], axis=1))
    return blocks


def split(value):
    high = value.astype(jnp.bfloat16)
    low = (value - high.astype(jnp.float32)).astype(jnp.bfloat16)
    return high, low


def dot(left, right):
    return jnp.dot(left, right, preferred_element_type=jnp.float32)


def times_right(rows, block):
    high, low = split(rows)
    return dot(jnp.concatenate([high, low, high], axis=1), block)


def right_groups(members, block):
    rows = members[0].shape[0]
    results = []
    for start in range(0, len(members), RIGHT):
        product = times_right(jnp.concatenate(members[start : start + RIGHT], axis=0), block[...])
        results += [product[i * rows : (i + 1) * rows] for i in range(RIGHT)]
    return results


def times_left(block, columns):
    high, low = split(columns)
    return dot(block, jnp.concatenate([high, low, high], axis=0))


def lane_iota(rows):
    return lax.broadcasted_iota(jnp.int32, (rows, LANES), 1)


def edge_lanes(rows):
    lane = lane_iota(rows)
    return (lane < BORDER) | (lane >= LANES - BORDER)


def pack_planes(real, imag):
    return jnp.where(edge_lanes(real.shape[0]), real, pltpu.roll(imag, LANES // 2, 1))


def unpack_planes(packed):
    return packed, pltpu.roll(packed, LANES // 2, 1)


def list_slots(order, positions, live, low, high, inside):
    def visit(slot, found):
        row, col = positions[0, slot], positions[1, slot]
        within = (row >= low) & (row <= high) & (col >= low) & (col <= high)
        order[found] = slot
        return found + jnp.where(within == inside, 1, 0)

    return lax.fori_loop(0, live, visit, 0)


def gradient_slots(cur, acc, doubled, amplitudes, positions, order, begin, stop, tables):
    right_f, left_f, right_b, left_b = tables
    probe = doubled.shape[1] // 2
    frame = probe + SUBLANES
    lane = lane_iota(frame)
    sub = lax.broadcasted_iota(jnp.int32, (SUBLANES, LANES), 0)

    def group_body(group, carry):
        places, probes, exits = [], [], []
        for member in range(GROUP):
            slot = begin + group * GROUP + member
            at = order[jnp.minimum(slot, stop - 1)]
            row = positions[0, at] + BORDER
            col = positions[1, at] + LANES
            row_at = pl.multiple_of(row // SUBLANES * SUBLANES, SUBLANES)
            col_at = pl.multiple_of(col // LANES * LANES, LANES)
            row_off, col_off = row - row_at, col - col_at
            from_left = lane >= col_off
            from_top = sub >= row_off
            planes, rolled = [], []
            for plane in range(2):
                wide = jnp.where(
                    from_left,
                    cur[plane, pl.ds(row_at, frame), pl.ds(col_at, LANES)],
                    cur[plane, pl.ds(row_at, frame), pl.ds(col_at + LANES, LANES)],
                )
                first = jnp.where(from_top, wide[:SUBLANES], wide[probe:])
                planes.append(jnp.concatenate([first, wide[SUBLANES:probe]], axis=0))
                shifted = doubled[plane, pl.ds(probe - row_off, probe), :]
                rolled.append(pltpu.roll(shifted, col_off, 1))
            places.append((at, slot, row_at, col_at, from_left, from_top))
            probes.append(rolled)
            exits.append(
                jnp.concatenate(
                    [
                        rolled[0] * planes[0] - rolled[1] * planes[1],
                        rolled[0] * planes[1] + rolled[1] * planes[0],
                    ],
                    axis=1,
                )
            )
        half = right_groups(exits, right_f)
        shrunk = []
        for pair in range(0, GROUP, 2):
            first, second = half[pair], half[pair + 1]
            stacked = jnp.concatenate(
                [
                    jnp.concatenate([first[:, :probe], second[:, :probe]], axis=1),
                    jnp.concatenate([first[:, probe:], second[:, probe:]], axis=1),
                ],
                axis=0,
            )
            wave = times_left(left_f[...], stacked)
            for member in range(2):
                at = places[pair + member][0]
                real = wave[:probe, member * probe : (member + 1) * probe]
                imag = wave[probe:, member * probe : (member + 1) * probe]
                shrink = amplitudes[at] * lax.rsqrt(real * real + imag * imag + smoothing) - 1.0
                shrunk.append(jnp.concatenate([real * shrink, imag * shrink], axis=1))
        half = right_groups(shrunk, right_b)
        for pair in range(0, GROUP, 2):
            first, second = half[pair], half[pair + 1]
            stacked = jnp.concatenate(
                [
                    jnp.concatenate([first[:, :probe], second[:, :probe]], axis=1),
                    jnp.concatenate([first[:, probe:], second[:, probe:]], axis=1),
                ],
                axis=0,
            )
            back = times_left(left_b[...], stacked)
            for member in range(2):
                at, slot, row_at, col_at, from_left, from_top = places[pair + member]
                real = back[:probe, member * probe : (member + 1) * probe]
                imag = back[probe:, member * probe : (member + 1) * probe]
                rolled = probes[pair + member]
                grads = (
                    rolled[0] * real + rolled[1] * imag,
                    rolled[0] * imag - rolled[1] * real,
                )
                is_live = slot < stop
                keep_left = from_left & is_live
                keep_right = jnp.logical_not(from_left) & is_live
                for plane in range(2):
                    grad = grads[plane]
                    frame_grad = jnp.concatenate(
                        [
                            jnp.where(from_top, grad[:SUBLANES], 0.0),
                            grad[SUBLANES:],
                            jnp.where(from_top, 0.0, grad[:SUBLANES]),
                        ],
                        axis=0,
                    )
                    rows = pl.ds(row_at, frame)
                    acc[plane, rows, pl.ds(col_at, LANES)] += jnp.where(keep_left, frame_grad, 0.0)
                    acc[plane, rows, pl.ds(col_at + LANES, LANES)] += jnp.where(
                        keep_right, frame_grad, 0.0
                    )
        return carry

    lax.fori_loop(0, (stop - begin + GROUP - 1) // GROUP, group_body, 0)


def step_of(probe):
    return step_gain / (jnp.max(probe[0] * probe[0] + probe[1] * probe[1]) + 1e-06)


def pack_row_band(acc, row, count):
    rows = slice(row, row + count)
    width = acc.shape[2] - 2 * LANES
    is_low = lane_iota(count) < BORDER
    halo = [
        jnp.where(is_low, acc[plane, rows, LANES + width :], acc[plane, rows, :LANES])
        for plane in range(2)
    ]
    own = [acc[plane, rows, LANES : LANES + width] for plane in range(2)]
    return jnp.concatenate([*own, pack_planes(*halo)], axis=1)


def pack_side_bands(acc, height):
    width = acc.shape[2] - 2 * LANES
    is_low = lane_iota(height) < BORDER
    return [
        pack_planes(
            *[
                jnp.where(
                    is_low,
                    acc[plane, :height, block + LANES : block + 2 * LANES],
                    acc[plane, :height, block : block + LANES],
                )
                for plane in range(2)
            ]
        )
        for block in (0, width)
    ]


def inner_start_kernel(
    positions, counts, objects, probe_in, amplitudes, *refs
):
    table_count = (len(refs) - 6) // 2
    tables_in, refs = refs[:table_count], refs[table_count:]
    cur, acc, doubled, held = refs[:4]
    tables, (order, sems) = refs[4:-2], refs[-2:]
    tile, width = objects.shape[1:]
    probe = probe_in.shape[1]
    sources = [(amplitudes, held)] + list(zip(tables_in, tables))
    for plane in range(2):
        sources.append(
            (
                objects.at[plane],
                cur.at[plane, pl.ds(BORDER, tile), pl.ds(LANES, width)],
            )
        )
        for row in (0, probe):
            sources.append((probe_in.at[plane], doubled.at[plane, pl.ds(row, probe), :]))
    loads = [
        pltpu.make_async_copy(source, target, sems.at[i])
        for i, (source, target) in enumerate(sources)
    ]
    for load in loads:
        load.start()
    acc[...] = jnp.zeros_like(acc)
    found = list_slots(order, positions, counts[0, 0], 0, tile - probe, True)
    for load in loads:
        load.wait()
    gradient_slots(
        cur, acc, doubled, held, positions, order, 0, jnp.minimum(found, GROUP), tables
    )


def inner_rest_kernel(
    positions, counts, cur, doubled, amplitudes, right_f, left_f, right_b, left_b, acc_in,
    acc, order,
):
    tile = cur.shape[1] - SUBLANES - BAND
    found = list_slots(order, positions, counts[0, 0], 0, tile - doubled.shape[2], True)
    gradient_slots(
        cur, acc, doubled, amplitudes, positions, order, jnp.minimum(found, GROUP), found,
        (right_f, left_f, right_b, left_b),
    )


def by_side(axis, first, second):
    even = lax.axis_index(axis) % 2 == 0
    return jnp.where(even, second, first), jnp.where(even, first, second)


def object_pack_kernel(cur, up, down, out):
    count = up.shape[0]
    width = up.shape[1] // 2
    tile = out.shape[0] - 2 * count
    is_low = lane_iota(count) < BORDER
    up, down = by_side("row", up[...], down[...])
    for row, band in ((0, up), (count + tile, down)):
        out[row : row + count, :] = pack_planes(
            *[
                jnp.where(
                    is_low,
                    band[:, plane * width : plane * width + LANES],
                    band[:, (plane + 1) * width - LANES : (plane + 1) * width],
                )
                for plane in range(2)
            ]
        )
    rows = slice(count, count + tile)
    is_low = lane_iota(tile) < BORDER
    out[rows, :] = pack_planes(
        *[
            jnp.where(is_low, cur[plane, rows, LANES : 2 * LANES], cur[plane, rows, width : width + LANES])
            for plane in range(2)
        ]
    )


def outer_kernel(
    positions, counts, up, down, left, right, doubled, amplitudes,
    right_f, left_f, right_b, left_b, cur_in, acc_in,
    cur, acc, to_up, to_down, to_left, to_right, order,
):
    extent = left.shape[0]
    tile, width = extent - BAND, up.shape[1] // 2
    lane = lane_iota(extent)
    up, down = by_side("row", up[...], down[...])
    lefts, rights = map(unpack_planes, by_side("col", left[...], right[...]))
    for plane in range(2):
        cur[plane, :extent, :LANES] = jnp.where(lane >= LANES - BORDER, lefts[plane], 0.0)
        cur[plane, :extent, LANES + width :] = jnp.where(lane < BORDER, rights[plane], 0.0)
        inner = slice(LANES, LANES + width)
        cur[plane, :BORDER, inner] = up[:, plane * width : (plane + 1) * width]
        cur[plane, BORDER + tile : extent, inner] = down[:, plane * width : (plane + 1) * width]
        cur[plane, extent:, :] = jnp.zeros_like(cur[plane, extent:, :])
    found = list_slots(order, positions, counts[0, 0], 0, tile - doubled.shape[2], False)
    gradient_slots(
        cur, acc, doubled, amplitudes, positions, order, 0, found, (right_f, left_f, right_b, left_b)
    )
    store_bands(acc, 0, tile, BAND, to_up, to_down, to_left, to_right)


def corner_parts(band, width):
    is_low = lane_iota(band.shape[0]) < BORDER
    halo = unpack_planes(band[:, 2 * width :])
    lefts, rights = [], []
    for plane in range(2):
        low = band[:, plane * width : plane * width + LANES]
        high = band[:, (plane + 1) * width - LANES : (plane + 1) * width]
        lefts.append(jnp.where(is_low, low, halo[plane]))
        rights.append(jnp.where(is_low, halo[plane], high))
    return pack_planes(*lefts), pack_planes(*rights)


def corner_kernel(up, down, after, to_left, to_right):
    width = (up.shape[1] - LANES) // 2
    up, down = by_side("row", up[...], down[...])
    tops, bottoms = corner_parts(up, width), corner_parts(down, width)
    to_left[...], to_right[...] = by_side(
        "col", *(jnp.concatenate([tops[i], bottoms[i]], axis=0) for i in range(2))
    )


def half_lanes(rows, first):
    low = lane_iota(rows) % (LANES // 2) < BORDER
    return low if first else jnp.logical_not(low)


def last_corner_kernel(up, down, left, right, after, to_left, to_right, whole):
    count = up.shape[0]
    tile = left.shape[0] - BAND
    width = (up.shape[1] - LANES) // 2
    half = tile // 2
    up, down = by_side("row", up[...], down[...])
    tops, bottoms = corner_parts(up, width), corner_parts(down, width)
    parts = []
    for side, source in enumerate((left, right)):
        whole[...] = source[BORDER : BORDER + tile, :]
        whole[:count, :] += tops[side]
        whole[tile - count :, :] += bottoms[side]
        parts.append(
            jnp.where(
                half_lanes(half, side == 1),
                whole[:half, :],
                pltpu.roll(whole[half:, :], BORDER, 1),
            )
        )
    to_left[...], to_right[...] = by_side("col", *parts)


def unfold_side(packed):
    both = jnp.concatenate([packed, pltpu.roll(packed, LANES - BORDER, 1)], axis=0)
    return unpack_planes(both)


def deep_kernel(
    positions, counts, probe, doubled, amplitudes, right_f, left_f, right_b, left_b, cur_in, acc_in,
    cur, acc, order,
):
    tile, width = cur.shape[1] - SUBLANES - BAND, cur.shape[2] - 2 * LANES
    rate = step_of(probe)
    middle, inner = slice(BORDER, BORDER + tile), slice(LANES, LANES + width)
    for plane in range(2):
        cur[plane, middle, inner] += rate * acc[plane, middle, inner]
    found = list_slots(
        order, positions, counts[0, 0], BORDER, tile - doubled.shape[2] - BORDER, True
    )
    gradient_slots(
        cur, acc, doubled, amplitudes, positions, order, 0, found, (right_f, left_f, right_b, left_b)
    )


def second_kernel(
    row_count, col_count,
    positions, counts, probe, doubled, amplitudes, right_f, left_f, right_b, left_b,
    up, down, left, right, left_corners, right_corners, cur_in, acc_in,
    cur, acc, to_up, to_down, to_left, to_right, order,
):
    tile, width = cur.shape[1] - SUBLANES - BAND, cur.shape[2] - 2 * LANES
    extent = tile + BAND
    rate = step_of(probe)
    row_at, row_last = lax.axis_index("row"), row_count - 1
    col_at, col_last = lax.axis_index("col"), col_count - 1
    top = jnp.where(row_at > 0, 1.0, 0.0)
    bottom = jnp.where(row_at < row_last, 1.0, 0.0)
    before = jnp.where(col_at > 0, 1.0, 0.0)
    after = jnp.where(col_at < col_last, 1.0, 0.0)
    early, _ = list_late_slots(order, positions, counts[0, 0], tile - doubled.shape[2])
    inner = slice(LANES, LANES + width)
    lane = lane_iota(extent)
    is_low, is_high = lane < BORDER, lane >= LANES - BORDER
    lefts, rights = (
        unpack_planes(
            jnp.concatenate(
                [
                    side[:BAND, :] + corners[:BAND, :],
                    side[BAND:tile, :],
                    side[tile:, :] + corners[BAND:, :],
                ],
                axis=0,
            )
        )
        for side, corners in zip(
            by_side("col", left[...], right[...]),
            by_side("col", left_corners[...], right_corners[...]),
        )
    )
    up, down = by_side("row", up[...], down[...])
    row_id = lax.broadcasted_iota(jnp.int32, (extent, LANES), 0)
    row_gain = rate * jnp.where(
        row_id < BORDER, top, jnp.where(row_id >= BORDER + tile, bottom, 1.0)
    )
    for plane in range(2):
        for row, band, on_grid in ((0, up, top), (tile, down, bottom)):
            halo_first = row == 0
            values = band[:, plane * width : (plane + 1) * width]
            own, out = (BORDER, 0) if halo_first else (0, BORDER)
            own_rows = slice(row + own, row + own + BORDER)
            out_rows = slice(row + out, row + out + BORDER)
            cur[plane, own_rows, inner] += rate * values[own : own + BORDER]
            acc[plane, own_rows, inner] += values[own : own + BORDER]
            cur[plane, out_rows, inner] += (rate * on_grid) * (
                acc[plane, out_rows, inner] + values[out : out + BORDER]
            )
            acc[plane, out_rows, inner] = jnp.zeros_like(acc[plane, out_rows, inner])
            halo = unpack_planes(band[:, 2 * width :])[plane]
            for lanes, keep in (
                (slice(0, LANES), is_high[:BAND]),
                (slice(LANES + width, None), is_low[:BAND]),
            ):
                acc[plane, row : row + BAND, lanes] += jnp.where(keep, halo, 0.0)
        for block, band, on_grid, own_first in (
            (0, lefts[plane], before, False),
            (width, rights[plane], after, True),
        ):
            low_block = slice(block, block + LANES)
            high_block = slice(block + LANES, block + 2 * LANES)
            own, out = (low_block, high_block) if own_first else (high_block, low_block)
            keep_own, keep_out = (is_high, is_low) if own_first else (is_low, is_high)
            own_band = jnp.where(keep_own, band, 0.0)
            cur[plane, :extent, own] += row_gain * own_band
            acc[plane, BORDER : BORDER + tile, own] += own_band[BORDER : BORDER + tile]
            cur[plane, :extent, out] += (row_gain * on_grid) * (
                acc[plane, :extent, out] + jnp.where(keep_out, band, 0.0)
            )
            acc[plane, :extent, out] = jnp.zeros_like(acc[plane, :extent, out])
    gradient_slots(
        cur, acc, doubled, amplitudes, positions, order, 0, early, (right_f, left_f, right_b, left_b)
    )
    store_bands(acc, 0, BORDER + tile, BORDER, to_up, to_down, to_left, to_right)


def list_late_slots(order, positions, live, last):
    reaching = list_slots(order, positions, live, 0, last, False)

    def visit(slot, found):
        row, col = positions[0, slot], positions[1, slot]
        inner = (row >= 0) & (row <= last) & (col >= 0) & (col <= last)
        deep = (row >= BORDER) & (row <= last - BORDER) & (col >= BORDER) & (col <= last - BORDER)
        order[found] = slot
        return found + jnp.where(inner & jnp.logical_not(deep), 1, 0)

    found = lax.fori_loop(0, live, visit, reaching)
    return jnp.minimum(found, (reaching + GROUP - 1) // GROUP * GROUP), found


def second_rest_kernel(
    positions, counts, cur, doubled, amplitudes, right_f, left_f, right_b, left_b, acc_in,
    acc, order,
):
    tile = cur.shape[1] - SUBLANES - BAND
    early, found = list_late_slots(order, positions, counts[0, 0], tile - doubled.shape[2])
    gradient_slots(
        cur, acc, doubled, amplitudes, positions, order, early, found,
        (right_f, left_f, right_b, left_b),
    )


def store_bands(acc, top, bottom, count, to_up, to_down, to_left, to_right):
    ups = pack_row_band(acc, top, count), pack_row_band(acc, bottom, count)
    to_up[...], to_down[...] = by_side("row", *ups)
    sides = pack_side_bands(acc, to_left.shape[0])
    if count == BAND:
        sides = by_side("col", *sides)
    to_left[...], to_right[...] = sides


def middle_kernel(objects, probe, acc, held, estimate, correction, estimated, corrected, sems):
    tile, width = objects.shape[1:]
    load = pltpu.make_async_copy(objects, held, sems.at[0])
    load.start()
    rate = step_of(probe)
    rows, lanes = slice(BORDER, tile - BORDER), slice(LANES, width - LANES)
    load.wait()
    for plane in range(2):
        corrected[plane] = rate * acc[plane, 2 * BORDER : tile, 2 * LANES : width]
        estimated[plane] = held[plane, rows, lanes] + corrected[plane]
    stores = [
        pltpu.make_async_copy(
            source,
            target.at[:, pl.ds(BORDER, tile - BAND), pl.ds(LANES, width - 2 * LANES)],
            sems.at[1 + i],
        )
        for i, (source, target) in enumerate(((corrected, correction), (estimated, estimate)))
    ]
    for store in stores:
        store.start()
    for store in stores:
        store.wait()


def last_kernel(
    probe, up, down, left, right, acc, held, estimate_in, correction_in,
    estimate, correction, side_parts, row_parts, sems,
):
    tile, width = held.shape[1:]
    rate = step_of(probe)
    lane = lane_iota(tile)
    rows = slice(BORDER, BORDER + tile)
    lefts, rights = map(unfold_side, by_side("col", left[...], right[...]))
    up, down = by_side("row", up[...], down[...])
    stores = []

    def send(index, source, target):
        store = pltpu.make_async_copy(source, target, sems.at[index])
        store.start()
        stores.append(store)

    for side, (block, bands) in enumerate(((0, lefts), (width - LANES, rights))):
        keep = (lane < BORDER) if side == 0 else (lane >= LANES - BORDER)
        for plane in range(2):
            at = plane * width + block
            total = acc[plane, rows, LANES + block : 2 * LANES + block]
            total += jnp.where(keep, bands[plane], 0.0)
            total = jnp.concatenate(
                [
                    total[:BORDER] + up[:, at : at + LANES],
                    total[BORDER : tile - BORDER],
                    total[tile - BORDER :] + down[:, at : at + LANES],
                ],
                axis=0,
            )
            side_parts[0, side, plane] = rate * total
            side_parts[1, side, plane] = (
                held[plane, :, block : block + LANES] + side_parts[0, side, plane]
            )
        for number, target in enumerate((correction, estimate)):
            send(
                2 * side + number, side_parts.at[number, side],
                target.at[:, :, pl.ds(block, LANES)],
            )
    lanes = slice(LANES, width - LANES)
    for end, (row, band) in enumerate(((0, up), (tile - BORDER, down))):
        for plane in range(2):
            total = acc[plane, BORDER + row : 2 * BORDER + row, 2 * LANES : width]
            total += band[:, plane * width + LANES : (plane + 1) * width - LANES]
            row_parts[0, end, plane] = rate * total
            row_parts[1, end, plane] = (
                held[plane, row : row + BORDER, lanes] + row_parts[0, end, plane]
            )
        for number, target in enumerate((correction, estimate)):
            send(
                4 + 2 * end + number, row_parts.at[number, end],
                target.at[:, pl.ds(row, BORDER), pl.ds(LANES, width - 2 * LANES)],
            )
    for store in stores:
        store.wait()


VMEM = pl.BlockSpec(memory_space=pltpu.VMEM)
SMEM = pl.BlockSpec(memory_space=pltpu.SMEM)
HBM = pl.BlockSpec(memory_space=pltpu.HBM)
PARAMS = pltpu.CompilerParams(vmem_limit_bytes=32 * 1024 * 1024)


def f32(*shape):
    return pltpu.VMEM(shape, jnp.float32)


def in_hbm(array):
    return pltpu.with_memory_space_constraint(array, pltpu.HBM)


def in_vmem(array):
    return pltpu.with_memory_space_constraint(array, pltpu.VMEM)


def swap_pairs(axis, first, second):
    count = lax.axis_size(axis)

    def swap(array, begin):
        ends = [(i, i + 1) for i in range(begin, count - 1, 2)]
        return in_vmem(lax.ppermute(array, axis, ends + [(j, i) for i, j in ends]))

    return swap(first, 0), swap(second, 1)


def on_device(object_field, probe_field, amplitudes, positions, counts):
    tile, width = object_field.shape[1:]
    probe = probe_field.shape[1]
    extent = tile + BAND
    padded = f32(2, extent + SUBLANES, width + 2 * LANES)
    doubled_shape = f32(2, 2 * probe, probe)
    tables = tuple(jnp.asarray(table) for table in dft_blocks(probe))
    places = positions[0, 0]
    order = pltpu.SMEM((amplitudes.shape[0] + 1,), jnp.int32)
    sides = (f32(extent, LANES), f32(extent, LANES))

    def row_bands(count):
        band = f32(count, 2 * width + LANES)
        return (band, band)

    def call(kernel, scalars, arrays, outs, scratch=(), aliases=None):
        return pl.pallas_call(
            kernel,
            out_shape=outs,
            in_specs=[SMEM] * len(scalars) + [VMEM] * len(arrays),
            out_specs=jax.tree.map(lambda out: VMEM, outs),
            scratch_shapes=list(scratch),
            input_output_aliases=aliases or {},
            compiler_params=PARAMS,
        )(*scalars, *arrays)

    slots = (in_hbm(places), counts)
    strips = [
        jnp.concatenate([object_field[0, rows], object_field[1, rows]], axis=1)
        for rows in (slice(0, BORDER), slice(tile - BORDER, tile))
    ]
    table_shapes = tuple(pltpu.VMEM(table.shape, table.dtype) for table in tables)
    up, down = swap_pairs("row", *by_side("row", *strips))
    cur, acc, doubled, held, *tables = pl.pallas_call(
        inner_start_kernel,
        out_shape=(padded, padded, doubled_shape, f32(*amplitudes.shape), *table_shapes),
        in_specs=[SMEM, SMEM] + [HBM] * (3 + len(tables)),
        out_specs=(VMEM,) * (4 + len(tables)),
        scratch_shapes=[order, pltpu.SemaphoreType.DMA((7 + len(tables),))],
        compiler_params=PARAMS,
        name="inner_start",
    )(*slots, *map(in_hbm, (object_field, probe_field, amplitudes, *tables)))
    packed = call(object_pack_kernel, (), (cur, up, down), sides[0])
    left, right = swap_pairs("col", packed, packed)
    acc = call(
        inner_rest_kernel, slots, (cur, doubled, held, *tables, acc),
        padded, (order,), {9: 0},
    )
    cur, acc, to_up, to_down, to_left, to_right = call(
        outer_kernel, slots, (up, down, left, right, doubled, held, *tables, cur, acc),
        (padded, padded, *row_bands(BAND), *sides), (order,), {12: 0, 13: 1},
    )
    up, down = swap_pairs("row", to_up, to_down)
    left, right = swap_pairs("col", to_left, to_right)
    cur, acc = call(
        deep_kernel, slots, (probe_field, doubled, held, *tables, cur, acc),
        (padded, padded), (order,), {9: 0, 10: 1},
    )
    corners = (f32(2 * BAND, LANES),) * 2
    left_corners, right_corners = swap_pairs("col", *call(corner_kernel, (), (up, down, acc), corners))
    cur, acc, to_up, to_down, to_left, to_right = call(
        functools.partial(second_kernel, lax.axis_size("row"), lax.axis_size("col")),
        slots,
        (
            probe_field, doubled, held, *tables,
            up, down, left, right, left_corners, right_corners, cur, acc,
        ),
        (padded, padded, *row_bands(BORDER), *sides), (order,), {15: 0, 16: 1},
    )
    up, down = swap_pairs("row", to_up, to_down)
    acc = call(
        second_rest_kernel, slots, (cur, doubled, held, *tables, acc),
        padded, (order,), {9: 0},
    )
    folded = f32(tile // 2, LANES)
    to_left, to_right = call(
        last_corner_kernel, (), (up, down, to_left, to_right, acc),
        (folded, folded), (f32(tile, LANES),),
    )
    left, right = swap_pairs("col", to_left, to_right)
    result = jax.ShapeDtypeStruct((2, tile, width), jnp.float32)
    middle = f32(2, tile - BAND, width - 2 * LANES)
    tile_held, estimate, correction = pl.pallas_call(
        middle_kernel,
        out_shape=(f32(2, tile, width), result, result),
        in_specs=[HBM, VMEM, VMEM],
        out_specs=(VMEM, HBM, HBM),
        scratch_shapes=[middle, middle, pltpu.SemaphoreType.DMA((3,))],
        compiler_params=PARAMS,
        name="middle",
    )(in_hbm(object_field), probe_field, acc)
    estimate, correction = pl.pallas_call(
        last_kernel,
        out_shape=(result, result),
        in_specs=[VMEM] * 7 + [HBM] * 2,
        out_specs=(HBM, HBM),
        scratch_shapes=[
            f32(2, 2, 2, tile, LANES), f32(2, 2, 2, BORDER, width - 2 * LANES),
            pltpu.SemaphoreType.DMA((8,)),
        ],
        input_output_aliases={7: 0, 8: 1},
        compiler_params=PARAMS,
        name="finish",
    )(probe_field, up, down, left, right, acc, tile_held, estimate, correction)
    return estimate, correction


def solution(mesh):
    placed = (
        P(None, "row", "col"),
        P(),
        P("row", None, "col"),
        P("row", "col", None, None),
        P("row", "col"),
    )
    return jax.shard_map(
        on_device,
        mesh=mesh,
        in_specs=placed,
        out_specs=(P(None, "row", "col"), P(None, "row", "col")),
        check_vma=False,
    )
```

```python
import functools

import jax
import jax.numpy as jnp
import numpy as np
from jax import lax
from jax.experimental import pallas as pl
from jax.experimental.pallas import tpu as pltpu
from jax.sharding import PartitionSpec as P

BORDER = 32
BAND = 2 * BORDER
LANES = 128
SUBLANES = 8
GROUP = 8
RIGHT = 4

smoothing = 0.5
step_gain = 0.5


def split_host(table):
    high = table.astype(jnp.bfloat16)
    low = (table - high.astype(np.float64)).astype(jnp.bfloat16)
    return high, low


def dft_blocks(length):
    counter = np.arange(length)
    angles = 2.0 * np.pi * (np.outer(counter, counter) % length) / length
    real, imag = np.cos(angles) / np.sqrt(length), -np.sin(angles) / np.sqrt(length)
    blocks = []
    for sign in (1.0, -1.0):
        right = np.block([[real, sign * imag], [-sign * imag, real]])
        high, low = split_host(right)
        blocks.append(np.concatenate([high, high, low], axis=0))
        left = np.block([[real, -sign * imag], [sign * imag, real]])
        high, low = split_host(left)
        blocks.append(np.concatenate([high, low], axis=0))
    return blocks


def split(value):
    high = value.astype(jnp.bfloat16)
    low = (value - high.astype(jnp.float32)).astype(jnp.bfloat16)
    return high, low


def dot(left, right):
    return jnp.dot(left, right, preferred_element_type=jnp.float32)


def times_right(rows, block):
    high, low = split(rows)
    return dot(jnp.concatenate([high, low, high], axis=1), block)


def right_groups(members, block):
    rows = members[0].shape[0]
    results = []
    for start in range(0, len(members), RIGHT):
        product = times_right(jnp.concatenate(members[start : start + RIGHT], axis=0), block[...])
        results += [product[i * rows : (i + 1) * rows] for i in range(RIGHT)]
    return results


def times_left(block, columns):
    high, low = split(columns)
    count = block.shape[0] // 2
    both = dot(block, high)
    return both[:count] + (both[count:] + dot(block[:count], low))


def lane_iota(rows):
    return lax.broadcasted_iota(jnp.int32, (rows, LANES), 1)


def edge_lanes(rows):
    lane = lane_iota(rows)
    return (lane < BORDER) | (lane >= LANES - BORDER)


def pack_planes(real, imag):
    return jnp.where(edge_lanes(real.shape[0]), real, pltpu.roll(imag, LANES // 2, 1))


def unpack_planes(packed):
    return packed, pltpu.roll(packed, LANES // 2, 1)


def list_slots(order, positions, live, low, high, inside):
    def visit(slot, found):
        row, col = positions[0, slot], positions[1, slot]
        within = (row >= low) & (row <= high) & (col >= low) & (col <= high)
        order[found] = slot
        return found + jnp.where(within == inside, 1, 0)

    return lax.fori_loop(0, live, visit, 0)


def gradient_slots(cur, acc, doubled, amplitudes, positions, order, begin, stop, tables):
    right_f, left_f, right_b, left_b = tables
    probe = doubled.shape[1] // 2
    frame = probe + SUBLANES
    lane = lane_iota(frame)
    sub = lax.broadcasted_iota(jnp.int32, (SUBLANES, LANES), 0)

    def group_body(group, carry):
        places, probes, exits = [], [], []
        for member in range(GROUP):
            slot = begin + group * GROUP + member
            at = order[jnp.minimum(slot, stop - 1)]
            row = positions[0, at] + BORDER
            col = positions[1, at] + LANES
            row_at = pl.multiple_of(row // SUBLANES * SUBLANES, SUBLANES)
            col_at = pl.multiple_of(col // LANES * LANES, LANES)
            row_off, col_off = row - row_at, col - col_at
            from_left = lane >= col_off
            from_top = sub >= row_off
            planes, rolled = [], []
            for plane in range(2):
                wide = jnp.where(
                    from_left,
                    cur[plane, pl.ds(row_at, frame), pl.ds(col_at, LANES)],
                    cur[plane, pl.ds(row_at, frame), pl.ds(col_at + LANES, LANES)],
                )
                first = jnp.where(from_top, wide[:SUBLANES], wide[probe:])
                planes.append(jnp.concatenate([first, wide[SUBLANES:probe]], axis=0))
                shifted = doubled[plane, pl.ds(probe - row_off, probe), :]
                rolled.append(pltpu.roll(shifted, col_off, 1))
            places.append((at, slot, row_at, col_at, from_left, from_top))
            probes.append(rolled)
            exits.append(
                jnp.concatenate(
                    [
                        rolled[0] * planes[0] - rolled[1] * planes[1],
                        rolled[0] * planes[1] + rolled[1] * planes[0],
                    ],
                    axis=1,
                )
            )
        half = right_groups(exits, right_f)
        shrunk = []
        for pair in range(0, GROUP, 2):
            first, second = half[pair], half[pair + 1]
            stacked = jnp.concatenate(
                [
                    jnp.concatenate([first[:, :probe], second[:, :probe]], axis=1),
                    jnp.concatenate([first[:, probe:], second[:, probe:]], axis=1),
                ],
                axis=0,
            )
            wave = times_left(left_f[...], stacked)
            for member in range(2):
                at = places[pair + member][0]
                real = wave[:probe, member * probe : (member + 1) * probe]
                imag = wave[probe:, member * probe : (member + 1) * probe]
                shrink = amplitudes[at] * lax.rsqrt(real * real + imag * imag + smoothing) - 1.0
                shrunk.append(jnp.concatenate([real * shrink, imag * shrink], axis=1))
        half = right_groups(shrunk, right_b)
        for pair in range(0, GROUP, 2):
            first, second = half[pair], half[pair + 1]
            stacked = jnp.concatenate(
                [
                    jnp.concatenate([first[:, :probe], second[:, :probe]], axis=1),
                    jnp.concatenate([first[:, probe:], second[:, probe:]], axis=1),
                ],
                axis=0,
            )
            back = times_left(left_b[...], stacked)
            for member in range(2):
                at, slot, row_at, col_at, from_left, from_top = places[pair + member]
                real = back[:probe, member * probe : (member + 1) * probe]
                imag = back[probe:, member * probe : (member + 1) * probe]
                rolled = probes[pair + member]
                grads = (
                    rolled[0] * real + rolled[1] * imag,
                    rolled[0] * imag - rolled[1] * real,
                )
                is_live = slot < stop
                keep_left = from_left & is_live
                keep_right = jnp.logical_not(from_left) & is_live
                for plane in range(2):
                    grad = grads[plane]
                    frame_grad = jnp.concatenate(
                        [
                            jnp.where(from_top, grad[:SUBLANES], 0.0),
                            grad[SUBLANES:],
                            jnp.where(from_top, 0.0, grad[:SUBLANES]),
                        ],
                        axis=0,
                    )
                    rows = pl.ds(row_at, frame)
                    acc[plane, rows, pl.ds(col_at, LANES)] += jnp.where(keep_left, frame_grad, 0.0)
                    acc[plane, rows, pl.ds(col_at + LANES, LANES)] += jnp.where(
                        keep_right, frame_grad, 0.0
                    )
        return carry

    lax.fori_loop(0, (stop - begin + GROUP - 1) // GROUP, group_body, 0)


def step_of(probe):
    return step_gain / (jnp.max(probe[0] * probe[0] + probe[1] * probe[1]) + 1e-06)


def pack_row_band(acc, row, count):
    rows = slice(row, row + count)
    width = acc.shape[2] - 2 * LANES
    is_low = lane_iota(count) < BORDER
    halo = [
        jnp.where(is_low, acc[plane, rows, LANES + width :], acc[plane, rows, :LANES])
        for plane in range(2)
    ]
    own = [acc[plane, rows, LANES : LANES + width] for plane in range(2)]
    return jnp.concatenate([*own, pack_planes(*halo)], axis=1)


def pack_side_bands(acc, height):
    width = acc.shape[2] - 2 * LANES
    is_low = lane_iota(height) < BORDER
    return [
        pack_planes(
            *[
                jnp.where(
                    is_low,
                    acc[plane, :height, block + LANES : block + 2 * LANES],
                    acc[plane, :height, block : block + LANES],
                )
                for plane in range(2)
            ]
        )
        for block in (0, width)
    ]


def inner_start_kernel(
    positions, counts, objects, probe_in, amplitudes, *refs
):
    table_count = (len(refs) - 6) // 2
    tables_in, refs = refs[:table_count], refs[table_count:]
    cur, acc, doubled, held = refs[:4]
    tables, (order, sems) = refs[4:-2], refs[-2:]
    tile, width = objects.shape[1:]
    probe = probe_in.shape[1]
    sources = [(amplitudes, held)] + list(zip(tables_in, tables))
    for plane in range(2):
        sources.append(
            (
                objects.at[plane],
                cur.at[plane, pl.ds(BORDER, tile), pl.ds(LANES, width)],
            )
        )
        for row in (0, probe):
            sources.append((probe_in.at[plane], doubled.at[plane, pl.ds(row, probe), :]))
    loads = [
        pltpu.make_async_copy(source, target, sems.at[i])
        for i, (source, target) in enumerate(sources)
    ]
    for load in loads:
        load.start()
    acc[...] = jnp.zeros_like(acc)
    found = list_slots(order, positions, counts[0, 0], 0, tile - probe, True)
    for load in loads:
        load.wait()
    gradient_slots(
        cur, acc, doubled, held, positions, order, 0, jnp.minimum(found, GROUP), tables
    )


def inner_rest_kernel(
    positions, counts, cur, doubled, amplitudes, right_f, left_f, right_b, left_b, acc_in,
    acc, order,
):
    tile = cur.shape[1] - SUBLANES - BAND
    found = list_slots(order, positions, counts[0, 0], 0, tile - doubled.shape[2], True)
    gradient_slots(
        cur, acc, doubled, amplitudes, positions, order, jnp.minimum(found, GROUP), found,
        (right_f, left_f, right_b, left_b),
    )


def fold_side(whole, is_low):
    half = whole.shape[0] // 2
    low = lane_iota(half) % (LANES // 2) < BORDER
    keep = low if is_low else jnp.logical_not(low)
    return jnp.where(keep, whole[:half, :], pltpu.roll(whole[half:, :], BORDER, 1))


def unfold_side(packed):
    return unpack_planes(
        jnp.concatenate([packed, pltpu.roll(packed, LANES - BORDER, 1)], axis=0)
    )


def by_side(axis, first, second):
    even = lax.axis_index(axis) % 2 == 0
    return jnp.where(even, second, first), jnp.where(even, first, second)


def object_pack_kernel(cur, up, down, to_left, to_right, whole):
    count = up.shape[0]
    width = up.shape[1] // 2
    extent = whole.shape[0]
    rows = slice(count, extent - count)
    up, down = by_side("row", up[...], down[...])
    parts = []
    for side in range(2):
        block = side * (width - LANES)
        for row, band in ((0, up), (extent - count, down)):
            whole[row : row + count, :] = pack_planes(
                *[
                    band[:, plane * width + block : plane * width + block + LANES]
                    for plane in range(2)
                ]
            )
        lanes = slice(LANES + block, 2 * LANES + block)
        whole[rows, :] = pack_planes(cur[0, rows, lanes], cur[1, rows, lanes])
        parts.append(fold_side(whole, side == 0))
    to_left[...], to_right[...] = by_side("col", *parts)


def outer_kernel(
    positions, counts, up, down, left, right, doubled, amplitudes,
    right_f, left_f, right_b, left_b, cur_in, acc_in,
    cur, acc, to_up, to_down, to_left, to_right, order,
):
    extent = 2 * left.shape[0]
    tile, width = extent - BAND, up.shape[1] // 2
    lane = lane_iota(extent)
    up, down = by_side("row", up[...], down[...])
    lefts, rights = map(unfold_side, by_side("col", left[...], right[...]))
    for plane in range(2):
        cur[plane, :extent, :LANES] = jnp.where(lane >= LANES - BORDER, lefts[plane], 0.0)
        cur[plane, :extent, LANES + width :] = jnp.where(lane < BORDER, rights[plane], 0.0)
        inner = slice(LANES, LANES + width)
        cur[plane, :BORDER, inner] = up[:, plane * width : (plane + 1) * width]
        cur[plane, BORDER + tile : extent, inner] = down[:, plane * width : (plane + 1) * width]
        cur[plane, extent:, :] = jnp.zeros_like(cur[plane, extent:, :])
    found = list_slots(order, positions, counts[0, 0], 0, tile - doubled.shape[2], False)
    gradient_slots(
        cur, acc, doubled, amplitudes, positions, order, 0, found, (right_f, left_f, right_b, left_b)
    )
    store_bands(acc, 0, tile, BAND, to_up, to_down, to_left, to_right)


def corner_parts(band, width):
    is_low = lane_iota(band.shape[0]) < BORDER
    halo = unpack_planes(band[:, 2 * width :])
    lefts, rights = [], []
    for plane in range(2):
        low = band[:, plane * width : plane * width + LANES]
        high = band[:, (plane + 1) * width - LANES : (plane + 1) * width]
        lefts.append(jnp.where(is_low, low, halo[plane]))
        rights.append(jnp.where(is_low, halo[plane], high))
    return pack_planes(*lefts), pack_planes(*rights)


def corner_kernel(up, down, after, to_left, to_right):
    width = (up.shape[1] - LANES) // 2
    up, down = by_side("row", up[...], down[...])
    tops, bottoms = corner_parts(up, width), corner_parts(down, width)
    to_left[...], to_right[...] = by_side(
        "col", *(jnp.concatenate([tops[i], bottoms[i]], axis=0) for i in range(2))
    )


def last_corner_kernel(up, down, left, right, after, to_left, to_right, whole):
    count = up.shape[0]
    tile = left.shape[0] - BAND
    width = (up.shape[1] - LANES) // 2
    up, down = by_side("row", up[...], down[...])
    tops, bottoms = corner_parts(up, width), corner_parts(down, width)
    parts = []
    for side, source in enumerate((left, right)):
        whole[...] = source[BORDER : BORDER + tile, :]
        whole[:count, :] += tops[side]
        whole[tile - count :, :] += bottoms[side]
        parts.append(fold_side(whole, side == 1))
    to_left[...], to_right[...] = by_side("col", *parts)


def deep_kernel(
    positions, counts, probe, doubled, amplitudes, right_f, left_f, right_b, left_b, cur_in, acc_in,
    cur, acc, order,
):
    tile, width = cur.shape[1] - SUBLANES - BAND, cur.shape[2] - 2 * LANES
    rate = step_of(probe)
    middle, inner = slice(BORDER, BORDER + tile), slice(LANES, LANES + width)
    for plane in range(2):
        cur[plane, middle, inner] += rate * acc[plane, middle, inner]
    found = list_slots(
        order, positions, counts[0, 0], BORDER, tile - doubled.shape[2] - BORDER, True
    )
    gradient_slots(
        cur, acc, doubled, amplitudes, positions, order, 0, found, (right_f, left_f, right_b, left_b)
    )


def second_kernel(
    row_count, col_count,
    positions, counts, probe, doubled, amplitudes, right_f, left_f, right_b, left_b,
    up, down, left, right, left_corners, right_corners, cur_in, acc_in,
    cur, acc, to_up, to_down, to_left, to_right, order,
):
    tile, width = cur.shape[1] - SUBLANES - BAND, cur.shape[2] - 2 * LANES
    extent = tile + BAND
    rate = step_of(probe)
    row_at, row_last = lax.axis_index("row"), row_count - 1
    col_at, col_last = lax.axis_index("col"), col_count - 1
    top = jnp.where(row_at > 0, 1.0, 0.0)
    bottom = jnp.where(row_at < row_last, 1.0, 0.0)
    before = jnp.where(col_at > 0, 1.0, 0.0)
    after = jnp.where(col_at < col_last, 1.0, 0.0)
    early, _ = list_late_slots(order, positions, counts[0, 0], tile - doubled.shape[2])
    inner = slice(LANES, LANES + width)
    lane = lane_iota(extent)
    is_low, is_high = lane < BORDER, lane >= LANES - BORDER
    lefts, rights = (
        unpack_planes(
            jnp.concatenate(
                [
                    side[:BAND, :] + corners[:BAND, :],
                    side[BAND:tile, :],
                    side[tile:, :] + corners[BAND:, :],
                ],
                axis=0,
            )
        )
        for side, corners in zip(
            by_side("col", left[...], right[...]),
            by_side("col", left_corners[...], right_corners[...]),
        )
    )
    up, down = by_side("row", up[...], down[...])
    row_id = lax.broadcasted_iota(jnp.int32, (extent, LANES), 0)
    row_gain = rate * jnp.where(
        row_id < BORDER, top, jnp.where(row_id >= BORDER + tile, bottom, 1.0)
    )
    for plane in range(2):
        for row, band, on_grid in ((0, up, top), (tile, down, bottom)):
            halo_first = row == 0
            values = band[:, plane * width : (plane + 1) * width]
            own, out = (BORDER, 0) if halo_first else (0, BORDER)
            own_rows = slice(row + own, row + own + BORDER)
            out_rows = slice(row + out, row + out + BORDER)
            cur[plane, own_rows, inner] += rate * values[own : own + BORDER]
            acc[plane, own_rows, inner] += values[own : own + BORDER]
            cur[plane, out_rows, inner] += (rate * on_grid) * (
                acc[plane, out_rows, inner] + values[out : out + BORDER]
            )
            acc[plane, out_rows, inner] = jnp.zeros_like(acc[plane, out_rows, inner])
            halo = unpack_planes(band[:, 2 * width :])[plane]
            for lanes, keep in (
                (slice(0, LANES), is_high[:BAND]),
                (slice(LANES + width, None), is_low[:BAND]),
            ):
                acc[plane, row : row + BAND, lanes] += jnp.where(keep, halo, 0.0)
        for block, band, on_grid, own_first in (
            (0, lefts[plane], before, False),
            (width, rights[plane], after, True),
        ):
            low_block = slice(block, block + LANES)
            high_block = slice(block + LANES, block + 2 * LANES)
            own, out = (low_block, high_block) if own_first else (high_block, low_block)
            keep_own, keep_out = (is_high, is_low) if own_first else (is_low, is_high)
            own_band = jnp.where(keep_own, band, 0.0)
            cur[plane, :extent, own] += row_gain * own_band
            acc[plane, BORDER : BORDER + tile, own] += own_band[BORDER : BORDER + tile]
            cur[plane, :extent, out] += (row_gain * on_grid) * (
                acc[plane, :extent, out] + jnp.where(keep_out, band, 0.0)
            )
            acc[plane, :extent, out] = jnp.zeros_like(acc[plane, :extent, out])
    gradient_slots(
        cur, acc, doubled, amplitudes, positions, order, 0, early, (right_f, left_f, right_b, left_b)
    )
    store_bands(acc, 0, BORDER + tile, BORDER, to_up, to_down, to_left, to_right)


def list_late_slots(order, positions, live, last):
    reaching = list_slots(order, positions, live, 0, last, False)

    def visit(slot, found):
        row, col = positions[0, slot], positions[1, slot]
        inner = (row >= 0) & (row <= last) & (col >= 0) & (col <= last)
        deep = (row >= BORDER) & (row <= last - BORDER) & (col >= BORDER) & (col <= last - BORDER)
        order[found] = slot
        return found + jnp.where(inner & jnp.logical_not(deep), 1, 0)

    found = lax.fori_loop(0, live, visit, reaching)
    return jnp.minimum(found, (reaching + GROUP - 1) // GROUP * GROUP), found


def second_rest_kernel(
    positions, counts, cur, doubled, amplitudes, right_f, left_f, right_b, left_b, acc_in,
    acc, order,
):
    tile = cur.shape[1] - SUBLANES - BAND
    early, found = list_late_slots(order, positions, counts[0, 0], tile - doubled.shape[2])
    gradient_slots(
        cur, acc, doubled, amplitudes, positions, order, early, found,
        (right_f, left_f, right_b, left_b),
    )


def store_bands(acc, top, bottom, count, to_up, to_down, to_left, to_right):
    ups = pack_row_band(acc, top, count), pack_row_band(acc, bottom, count)
    to_up[...], to_down[...] = by_side("row", *ups)
    sides = pack_side_bands(acc, to_left.shape[0])
    if count == BAND:
        sides = by_side("col", *sides)
    to_left[...], to_right[...] = sides


def middle_kernel(objects, probe, acc, held, estimate, correction, estimated, corrected, sems):
    tile, width = objects.shape[1:]
    load = pltpu.make_async_copy(objects, held, sems.at[0])
    load.start()
    rate = step_of(probe)
    rows, lanes = slice(BORDER, tile - BORDER), slice(LANES, width - LANES)
    load.wait()
    for plane in range(2):
        corrected[plane] = rate * acc[plane, 2 * BORDER : tile, 2 * LANES : width]
        estimated[plane] = held[plane, rows, lanes] + corrected[plane]
    stores = [
        pltpu.make_async_copy(
            source,
            target.at[:, pl.ds(BORDER, tile - BAND), pl.ds(LANES, width - 2 * LANES)],
            sems.at[1 + i],
        )
        for i, (source, target) in enumerate(((corrected, correction), (estimated, estimate)))
    ]
    for store in stores:
        store.start()
    for store in stores:
        store.wait()


def last_kernel(
    probe, up, down, left, right, acc, held, estimate_in, correction_in,
    estimate, correction, side_parts, row_parts, sems,
):
    tile, width = held.shape[1:]
    rate = step_of(probe)
    lane = lane_iota(tile)
    rows = slice(BORDER, BORDER + tile)
    lefts, rights = map(unfold_side, by_side("col", left[...], right[...]))
    up, down = by_side("row", up[...], down[...])
    stores = []

    def send(index, source, target):
        store = pltpu.make_async_copy(source, target, sems.at[index])
        store.start()
        stores.append(store)

    for side, (block, bands) in enumerate(((0, lefts), (width - LANES, rights))):
        keep = (lane < BORDER) if side == 0 else (lane >= LANES - BORDER)
        for plane in range(2):
            at = plane * width + block
            total = acc[plane, rows, LANES + block : 2 * LANES + block]
            total += jnp.where(keep, bands[plane], 0.0)
            total = jnp.concatenate(
                [
                    total[:BORDER] + up[:, at : at + LANES],
                    total[BORDER : tile - BORDER],
                    total[tile - BORDER :] + down[:, at : at + LANES],
                ],
                axis=0,
            )
            side_parts[0, side, plane] = rate * total
            side_parts[1, side, plane] = (
                held[plane, :, block : block + LANES] + side_parts[0, side, plane]
            )
        for number, target in enumerate((correction, estimate)):
            send(
                2 * side + number, side_parts.at[number, side],
                target.at[:, :, pl.ds(block, LANES)],
            )
    lanes = slice(LANES, width - LANES)
    for end, (row, band) in enumerate(((0, up), (tile - BORDER, down))):
        for plane in range(2):
            total = acc[plane, BORDER + row : 2 * BORDER + row, 2 * LANES : width]
            total += band[:, plane * width + LANES : (plane + 1) * width - LANES]
            row_parts[0, end, plane] = rate * total
            row_parts[1, end, plane] = (
                held[plane, row : row + BORDER, lanes] + row_parts[0, end, plane]
            )
        for number, target in enumerate((correction, estimate)):
            send(
                4 + 2 * end + number, row_parts.at[number, end],
                target.at[:, pl.ds(row, BORDER), pl.ds(LANES, width - 2 * LANES)],
            )
    for store in stores:
        store.wait()


VMEM = pl.BlockSpec(memory_space=pltpu.VMEM)
SMEM = pl.BlockSpec(memory_space=pltpu.SMEM)
HBM = pl.BlockSpec(memory_space=pltpu.HBM)
PARAMS = pltpu.CompilerParams(vmem_limit_bytes=32 * 1024 * 1024)


def f32(*shape):
    return pltpu.VMEM(shape, jnp.float32)


def in_hbm(array):
    return pltpu.with_memory_space_constraint(array, pltpu.HBM)


def in_vmem(array):
    return pltpu.with_memory_space_constraint(array, pltpu.VMEM)


def swap_pairs(axis, first, second):
    count = lax.axis_size(axis)

    def swap(array, begin):
        ends = [(i, i + 1) for i in range(begin, count - 1, 2)]
        return in_vmem(lax.ppermute(array, axis, ends + [(j, i) for i, j in ends]))

    first = swap(first, 0)
    second = swap(second, 1)
    return first, second


def on_device(object_field, probe_field, amplitudes, positions, counts):
    tile, width = object_field.shape[1:]
    probe = probe_field.shape[1]
    extent = tile + BAND
    padded = f32(2, extent + SUBLANES, width + 2 * LANES)
    doubled_shape = f32(2, 2 * probe, probe)
    tables = tuple(jnp.asarray(table) for table in dft_blocks(probe))
    places = positions[0, 0]
    order = pltpu.SMEM((amplitudes.shape[0] + 1,), jnp.int32)
    sides = (f32(extent, LANES), f32(extent, LANES))

    def row_bands(count):
        band = f32(count, 2 * width + LANES)
        return (band, band)

    def call(kernel, scalars, arrays, outs, scratch=(), aliases=None):
        return pl.pallas_call(
            kernel,
            out_shape=outs,
            in_specs=[SMEM] * len(scalars) + [VMEM] * len(arrays),
            out_specs=jax.tree.map(lambda out: VMEM, outs),
            scratch_shapes=list(scratch),
            input_output_aliases=aliases or {},
            compiler_params=PARAMS,
        )(*scalars, *arrays)

    slots = (in_hbm(places), counts)
    strips = [
        jnp.concatenate([object_field[0, rows], object_field[1, rows]], axis=1)
        for rows in (slice(0, BORDER), slice(tile - BORDER, tile))
    ]
    table_shapes = tuple(pltpu.VMEM(table.shape, table.dtype) for table in tables)
    up, down = swap_pairs("row", *by_side("row", *strips))
    cur, acc, doubled, held, *tables = pl.pallas_call(
        inner_start_kernel,
        out_shape=(padded, padded, doubled_shape, f32(*amplitudes.shape), *table_shapes),
        in_specs=[SMEM, SMEM] + [HBM] * (3 + len(tables)),
        out_specs=(VMEM,) * (4 + len(tables)),
        scratch_shapes=[order, pltpu.SemaphoreType.DMA((7 + len(tables),))],
        compiler_params=PARAMS,
        name="inner_start",
    )(*slots, *map(in_hbm, (object_field, probe_field, amplitudes, *tables)))
    to_left, to_right = call(
        object_pack_kernel, (), (cur, up, down),
        (f32(extent // 2, LANES),) * 2, (f32(extent, LANES),),
    )
    left, right = swap_pairs("col", to_left, to_right)
    acc = call(
        inner_rest_kernel, slots, (cur, doubled, held, *tables, acc),
        padded, (order,), {9: 0},
    )
    cur, acc, to_up, to_down, to_left, to_right = call(
        outer_kernel, slots, (up, down, left, right, doubled, held, *tables, cur, acc),
        (padded, padded, *row_bands(BAND), *sides), (order,), {12: 0, 13: 1},
    )
    up, down = swap_pairs("row", to_up, to_down)
    left, right = swap_pairs("col", to_left, to_right)
    cur, acc = call(
        deep_kernel, slots, (probe_field, doubled, held, *tables, cur, acc),
        (padded, padded), (order,), {9: 0, 10: 1},
    )
    corners = (f32(2 * BAND, LANES),) * 2
    left_corners, right_corners = swap_pairs("col", *call(corner_kernel, (), (up, down, acc), corners))
    cur, acc, to_up, to_down, to_left, to_right = call(
        functools.partial(second_kernel, lax.axis_size("row"), lax.axis_size("col")),
        slots,
        (
            probe_field, doubled, held, *tables,
            up, down, left, right, left_corners, right_corners, cur, acc,
        ),
        (padded, padded, *row_bands(BORDER), *sides), (order,), {15: 0, 16: 1},
    )
    up, down = swap_pairs("row", to_up, to_down)
    acc = call(
        second_rest_kernel, slots, (cur, doubled, held, *tables, acc),
        padded, (order,), {9: 0},
    )
    folded = f32(tile // 2, LANES)
    to_left, to_right = call(
        last_corner_kernel, (), (up, down, to_left, to_right, acc),
        (folded, folded), (f32(tile, LANES),),
    )
    left, right = swap_pairs("col", to_left, to_right)
    result = jax.ShapeDtypeStruct((2, tile, width), jnp.float32)
    middle = f32(2, tile - BAND, width - 2 * LANES)
    tile_held, estimate, correction = pl.pallas_call(
        middle_kernel,
        out_shape=(f32(2, tile, width), result, result),
        in_specs=[HBM, VMEM, VMEM],
        out_specs=(VMEM, HBM, HBM),
        scratch_shapes=[middle, middle, pltpu.SemaphoreType.DMA((3,))],
        compiler_params=PARAMS,
        name="middle",
    )(in_hbm(object_field), probe_field, acc)
    estimate, correction = pl.pallas_call(
        last_kernel,
        out_shape=(result, result),
        in_specs=[VMEM] * 7 + [HBM] * 2,
        out_specs=(HBM, HBM),
        scratch_shapes=[
            f32(2, 2, 2, tile, LANES), f32(2, 2, 2, BORDER, width - 2 * LANES),
            pltpu.SemaphoreType.DMA((8,)),
        ],
        input_output_aliases={7: 0, 8: 1},
        compiler_params=PARAMS,
        name="finish",
    )(probe_field, up, down, left, right, acc, tile_held, estimate, correction)
    return estimate, correction


def solution(mesh):
    placed = (
        P(None, "row", "col"),
        P(),
        P("row", None, "col"),
        P("row", "col", None, None),
        P("row", "col"),
    )
    return jax.shard_map(
        on_device,
        mesh=mesh,
        in_specs=placed,
        out_specs=(P(None, "row", "col"), P(None, "row", "col")),
        check_vma=False,
    )
```

```python
import functools

import jax
import jax.numpy as jnp
import numpy as np
from jax import lax
from jax.experimental import pallas as pl
from jax.experimental.pallas import tpu as pltpu
from jax.sharding import PartitionSpec as P

BORDER = 32
BAND = 2 * BORDER
ITERS = 2
LANES = 128
SUBLANES = 8
LARGE, MIDDLE, SMALL = 8, 4, 2
RIGHT = 4

smoothing = 0.5
step_gain = 0.5


def split_host(table):
    high = table.astype(jnp.bfloat16)
    low = (table - high.astype(np.float64)).astype(jnp.bfloat16)
    return high, low


def dft_blocks(length):
    counter = np.arange(length)
    angles = 2.0 * np.pi * (np.outer(counter, counter) % length) / length
    real, imag = np.cos(angles) / np.sqrt(length), -np.sin(angles) / np.sqrt(length)
    blocks = []
    for sign in (1.0, -1.0):
        right = np.block([[real, sign * imag], [-sign * imag, real]])
        high, low = split_host(right)
        blocks.append(np.concatenate([high, high, low], axis=0))
        left = np.block([[real, -sign * imag], [sign * imag, real]])
        high, low = split_host(left)
        blocks.append(np.concatenate([high, low], axis=0))
    return blocks


def split(value):
    high = value.astype(jnp.bfloat16)
    low = (value - high.astype(jnp.float32)).astype(jnp.bfloat16)
    return high, low


def dot(left, right):
    return jnp.dot(left, right, preferred_element_type=jnp.float32)


def times_right(rows, block):
    high, low = split(rows)
    return dot(jnp.concatenate([high, low, high], axis=1), block)


def right_groups(members, block):
    rows = members[0].shape[0]
    results = []
    count = min(RIGHT, len(members))
    for start in range(0, len(members), count):
        product = times_right(jnp.concatenate(members[start : start + count], axis=0), block[...])
        results += [product[i * rows : (i + 1) * rows] for i in range(count)]
    return results


def times_left(block, columns):
    high, low = split(columns)
    count = block.shape[0] // 2
    both = dot(block, high)
    return both[:count] + (both[count:] + dot(block[:count], low))


def lane_iota(rows):
    return lax.broadcasted_iota(jnp.int32, (rows, LANES), 1)


def edge_lanes(rows):
    lane = lane_iota(rows)
    return (lane < BORDER) | (lane >= LANES - BORDER)


def pack_planes(real, imag):
    return jnp.where(edge_lanes(real.shape[0]), real, pltpu.roll(imag, LANES // 2, 1))


def unpack_planes(packed):
    return packed, pltpu.roll(packed, LANES // 2, 1)


def slot_kinds(row, col, last):
    row_out, col_out = (row < 0) | (row > last), (col < 0) | (col > last)
    row_edge = (row < BORDER) | (row > last - BORDER)
    col_edge = (col < BORDER) | (col > last - BORDER)
    return row_out, col_out, row_edge, col_edge


def is_deep(row_out, col_out, row_edge, col_edge):
    return jnp.logical_not(row_edge | col_edge)


def is_beside(row_out, col_out, row_edge, col_edge):
    return col_out


def is_early(row_out, col_out, row_edge, col_edge):
    return (row_edge | col_edge) & jnp.logical_not(col_out)


def is_reaching(row_out, col_out, row_edge, col_edge):
    return (row_out | col_out) & jnp.logical_not(row_edge & col_edge)


def is_rim(row_out, col_out, row_edge, col_edge):
    return (row_edge ^ col_edge) & jnp.logical_not(row_out | col_out)


def is_reaching_corner(row_out, col_out, row_edge, col_edge):
    return (row_out | col_out) & row_edge & col_edge


def is_rim_corner(row_out, col_out, row_edge, col_edge):
    return row_edge & col_edge & jnp.logical_not(row_out | col_out)


class Slots:
    def __init__(self, positions, live, order, last):
        self.positions, self.live, self.order, self.last = positions, live, order, last

    def append(self, kind, begin, skip=0):
        def visit(slot, carry):
            found, seen = carry
            kinds = slot_kinds(self.positions[0, slot], self.positions[1, slot], self.last)
            of_kind = jnp.where(kind(*kinds), 1, 0)
            self.order[found] = slot
            return found + jnp.where(seen >= skip, of_kind, 0), seen + of_kind

        return lax.fori_loop(0, self.live, visit, (begin, 0))[0]

    def lead(self):
        return jnp.minimum(self.append(is_deep, 0), MIDDLE)

    def side(self):
        lead = self.lead()
        early = self.append(is_early, 0)
        end = self.append(is_deep, early, lead)
        stop = jnp.minimum(end, round_up(early))
        return stop, lead + jnp.maximum(stop - early, 0), end

    def band(self):
        done = self.side()[1]
        deep = self.append(is_deep, 0)
        room = 2 * LARGE - (deep - done + LARGE - 1) // LARGE * LARGE
        return done, deep, jnp.minimum(deep, jnp.maximum(room, 0))

    def corner(self):
        reaching = self.append(is_reaching, 0)
        end = self.append(is_rim, reaching)
        return jnp.minimum(end, round_up(reaching)), end

    def rest(self):
        deep_done = self.band()[2]
        begin, end = self.corner()
        return begin, self.append(is_deep, self.append(is_rim_corner, end), deep_done)


def round_up(count):
    return jnp.maximum((count + LARGE - 1) // LARGE, 1) * LARGE


def gradient_slots(cur, acc, doubled, amplitudes, positions, order, begin, stop, tables, size=LARGE):
    right_f, left_f, right_b, left_b = tables
    probe = doubled.shape[1] // 2
    frame = probe + SUBLANES
    lane = lane_iota(frame)
    sub = lax.broadcasted_iota(jnp.int32, (SUBLANES, LANES), 0)

    def group_body(group, carry):
        places, probes, exits = [], [], []
        for member in range(size):
            slot = begin + group * size + member
            at = order[jnp.minimum(slot, stop - 1)]
            row = positions[0, at] + BORDER
            col = positions[1, at] + LANES
            row_at = pl.multiple_of(row // SUBLANES * SUBLANES, SUBLANES)
            col_at = pl.multiple_of(col // LANES * LANES, LANES)
            row_off, col_off = row - row_at, col - col_at
            from_left = lane >= col_off
            from_top = sub >= row_off
            planes, rolled = [], []
            for plane in range(2):
                wide = jnp.where(
                    from_left,
                    cur[plane, pl.ds(row_at, frame), pl.ds(col_at, LANES)],
                    cur[plane, pl.ds(row_at, frame), pl.ds(col_at + LANES, LANES)],
                )
                first = jnp.where(from_top, wide[:SUBLANES], wide[probe:])
                planes.append(jnp.concatenate([first, wide[SUBLANES:probe]], axis=0))
                shifted = doubled[plane, pl.ds(probe - row_off, probe), :]
                rolled.append(pltpu.roll(shifted, col_off, 1))
            places.append((at, slot, row_at, col_at, from_left, from_top))
            probes.append(rolled)
            exits.append(
                jnp.concatenate(
                    [
                        rolled[0] * planes[0] - rolled[1] * planes[1],
                        rolled[0] * planes[1] + rolled[1] * planes[0],
                    ],
                    axis=1,
                )
            )
        half = right_groups(exits, right_f)
        shrunk = []
        for pair in range(0, size, 2):
            first, second = half[pair], half[pair + 1]
            stacked = jnp.concatenate(
                [
                    jnp.concatenate([first[:, :probe], second[:, :probe]], axis=1),
                    jnp.concatenate([first[:, probe:], second[:, probe:]], axis=1),
                ],
                axis=0,
            )
            wave = times_left(left_f[...], stacked)
            for member in range(2):
                at = places[pair + member][0]
                real = wave[:probe, member * probe : (member + 1) * probe]
                imag = wave[probe:, member * probe : (member + 1) * probe]
                shrink = amplitudes[at] * lax.rsqrt(real * real + imag * imag + smoothing) - 1.0
                shrunk.append(jnp.concatenate([real * shrink, imag * shrink], axis=1))
        half = right_groups(shrunk, right_b)
        for pair in range(0, size, 2):
            first, second = half[pair], half[pair + 1]
            stacked = jnp.concatenate(
                [
                    jnp.concatenate([first[:, :probe], second[:, :probe]], axis=1),
                    jnp.concatenate([first[:, probe:], second[:, probe:]], axis=1),
                ],
                axis=0,
            )
            back = times_left(left_b[...], stacked)
            for member in range(2):
                at, slot, row_at, col_at, from_left, from_top = places[pair + member]
                real = back[:probe, member * probe : (member + 1) * probe]
                imag = back[probe:, member * probe : (member + 1) * probe]
                rolled = probes[pair + member]
                grads = (
                    rolled[0] * real + rolled[1] * imag,
                    rolled[0] * imag - rolled[1] * real,
                )
                is_live = slot < stop
                keep_left = from_left & is_live
                keep_right = jnp.logical_not(from_left) & is_live
                for plane in range(2):
                    grad = grads[plane]
                    frame_grad = jnp.concatenate(
                        [
                            jnp.where(from_top, grad[:SUBLANES], 0.0),
                            grad[SUBLANES:],
                            jnp.where(from_top, 0.0, grad[:SUBLANES]),
                        ],
                        axis=0,
                    )
                    rows = pl.ds(row_at, frame)
                    acc[plane, rows, pl.ds(col_at, LANES)] += jnp.where(keep_left, frame_grad, 0.0)
                    acc[plane, rows, pl.ds(col_at + LANES, LANES)] += jnp.where(
                        keep_right, frame_grad, 0.0
                    )
        return carry

    lax.fori_loop(0, (stop - begin + size - 1) // size, group_body, 0)


def step_of(probe):
    return step_gain / (jnp.max(probe[0] * probe[0] + probe[1] * probe[1]) + 1e-06)


def pack_row_band(acc, row, count):
    rows = slice(row, row + count)
    width = acc.shape[2] - 2 * LANES
    is_low = lane_iota(count) < BORDER
    halo = [
        jnp.where(is_low, acc[plane, rows, LANES + width :], acc[plane, rows, :LANES])
        for plane in range(2)
    ]
    own = [acc[plane, rows, LANES : LANES + width] for plane in range(2)]
    return jnp.concatenate([*own, pack_planes(*halo)], axis=1)


def pack_side_bands(acc, height):
    width = acc.shape[2] - 2 * LANES
    is_low = lane_iota(height) < BORDER
    return [
        pack_planes(
            *[
                jnp.where(
                    is_low,
                    acc[plane, :height, block + LANES : block + 2 * LANES],
                    acc[plane, :height, block : block + LANES],
                )
                for plane in range(2)
            ]
        )
        for block in (0, width)
    ]


def inner_start_kernel(
    positions, counts, objects, probe_in, amplitudes, *refs
):
    table_count = (len(refs) - 6) // 2
    tables_in, refs = refs[:table_count], refs[table_count:]
    cur, acc, doubled, held = refs[:4]
    tables, (order, sems) = refs[4:-2], refs[-2:]
    tile, width = objects.shape[1:]
    probe = probe_in.shape[1]
    sources = [(amplitudes, held)] + list(zip(tables_in, tables))
    for plane in range(2):
        sources.append(
            (
                objects.at[plane],
                cur.at[plane, pl.ds(BORDER, tile), pl.ds(LANES, width)],
            )
        )
        for row in (0, probe):
            sources.append((probe_in.at[plane], doubled.at[plane, pl.ds(row, probe), :]))
    loads = [
        pltpu.make_async_copy(source, target, sems.at[i])
        for i, (source, target) in enumerate(sources)
    ]
    for load in loads:
        load.start()
    acc[...] = jnp.zeros_like(acc)
    lead = Slots(positions, counts[0, 0], order, tile - probe).lead()
    for load in loads:
        load.wait()
    gradient_slots(cur, acc, doubled, held, positions, order, 0, lead, tables, MIDDLE)


def side_kernel(
    positions, counts, up, down, doubled, amplitudes, right_f, left_f, right_b, left_b, cur_in, acc_in,
    cur, acc, order,
):
    tile, width = cur.shape[1] - SUBLANES - BAND, cur.shape[2] - 2 * LANES
    up, down = by_side("row", up[...], down[...])
    inner = slice(LANES, LANES + width)
    for plane in range(2):
        lanes = slice(plane * width, (plane + 1) * width)
        cur[plane, :BORDER, inner] = up[:, lanes]
        cur[plane, BORDER + tile : BAND + tile, inner] = down[:, lanes]
        cur[plane, BAND + tile :, :] = jnp.zeros_like(cur[plane, BAND + tile :, :])
    slots = Slots(positions, counts[0, 0], order, tile - doubled.shape[2])
    gradient_slots(
        cur, acc, doubled, amplitudes, positions, order, 0, slots.side()[0],
        (right_f, left_f, right_b, left_b),
    )


def fold_side(whole, is_low):
    half = whole.shape[0] // 2
    low = lane_iota(half) % (LANES // 2) < BORDER
    keep = low if is_low else jnp.logical_not(low)
    return jnp.where(keep, whole[:half, :], pltpu.roll(whole[half:, :], BORDER, 1))


def unfold_side(packed):
    return unpack_planes(
        jnp.concatenate([packed, pltpu.roll(packed, LANES - BORDER, 1)], axis=0)
    )


def by_side(axis, first, second):
    even = lax.axis_index(axis) % 2 == 0
    return jnp.where(even, second, first), jnp.where(even, first, second)


def object_pack_kernel(cur, up, down, to_left, to_right, whole):
    count = up.shape[0]
    width = up.shape[1] // 2
    extent = whole.shape[0]
    rows = slice(count, extent - count)
    up, down = by_side("row", up[...], down[...])
    parts = []
    for side in range(2):
        block = side * (width - LANES)
        for row, band in ((0, up), (extent - count, down)):
            whole[row : row + count, :] = pack_planes(
                *[
                    band[:, plane * width + block : plane * width + block + LANES]
                    for plane in range(2)
                ]
            )
        lanes = slice(LANES + block, 2 * LANES + block)
        whole[rows, :] = pack_planes(cur[0, rows, lanes], cur[1, rows, lanes])
        parts.append(fold_side(whole, side == 0))
    to_left[...], to_right[...] = by_side("col", *parts)


def outer_kernel(
    positions, counts, left, right, doubled, amplitudes,
    right_f, left_f, right_b, left_b, cur_in, acc_in,
    cur, acc, to_up, to_down, to_left, to_right, order,
):
    extent = 2 * left.shape[0]
    tile, width = extent - BAND, cur.shape[2] - 2 * LANES
    lane = lane_iota(extent)
    lefts, rights = map(unfold_side, by_side("col", left[...], right[...]))
    for plane in range(2):
        cur[plane, :extent, :LANES] = jnp.where(lane >= LANES - BORDER, lefts[plane], 0.0)
        cur[plane, :extent, LANES + width :] = jnp.where(lane < BORDER, rights[plane], 0.0)
    found = Slots(positions, counts[0, 0], order, tile - doubled.shape[2]).append(is_beside, 0)
    gradient_slots(
        cur, acc, doubled, amplitudes, positions, order, 0, found,
        (right_f, left_f, right_b, left_b), MIDDLE,
    )
    store_bands(acc, 0, tile, BAND, to_up, to_down, to_left, to_right)


def corner_parts(band, width):
    is_low = lane_iota(band.shape[0]) < BORDER
    halo = unpack_planes(band[:, 2 * width :])
    lefts, rights = [], []
    for plane in range(2):
        low = band[:, plane * width : plane * width + LANES]
        high = band[:, (plane + 1) * width - LANES : (plane + 1) * width]
        lefts.append(jnp.where(is_low, low, halo[plane]))
        rights.append(jnp.where(is_low, halo[plane], high))
    return pack_planes(*lefts), pack_planes(*rights)


def corner_kernel(up, down, after, to_left, to_right):
    width = (up.shape[1] - LANES) // 2
    up, down = by_side("row", up[...], down[...])
    tops, bottoms = corner_parts(up, width), corner_parts(down, width)
    to_left[...], to_right[...] = by_side(
        "col", *(jnp.concatenate([tops[i], bottoms[i]], axis=0) for i in range(2))
    )


def last_corner_kernel(up, down, left, right, after, to_left, to_right, whole):
    count = up.shape[0]
    tile = left.shape[0] - BAND
    width = (up.shape[1] - LANES) // 2
    up, down = by_side("row", up[...], down[...])
    tops, bottoms = corner_parts(up, width), corner_parts(down, width)
    parts = []
    for side, source in enumerate((left, right)):
        whole[...] = source[BORDER : BORDER + tile, :]
        whole[:count, :] += tops[side]
        whole[tile - count :, :] += bottoms[side]
        parts.append(fold_side(whole, side == 1))
    to_left[...], to_right[...] = by_side("col", *parts)


def deep_kernel(
    positions, counts, probe, doubled, amplitudes, right_f, left_f, right_b, left_b, cur_in, acc_in,
    cur, acc, order,
):
    tile, width = cur.shape[1] - SUBLANES - BAND, cur.shape[2] - 2 * LANES
    rate = step_of(probe)
    middle, inner = slice(BORDER, BORDER + tile), slice(LANES, LANES + width)
    slots = Slots(positions, counts[0, 0], order, tile - doubled.shape[2])
    done, deep, room = slots.band()

    def turn(iteration, carry):
        @pl.when(iteration == 1)
        def update():
            for plane in range(2):
                cur[plane, middle, inner] += rate * acc[plane, middle, inner]

        gradient_slots(
            cur, acc, doubled, amplitudes, positions, order,
            jnp.where(iteration == 0, done, 0), jnp.where(iteration == 0, deep, room),
            (right_f, left_f, right_b, left_b),
        )
        return carry

    lax.fori_loop(0, ITERS, turn, 0)


def grid_gains(row_count, col_count, tile, rate):
    row_at, col_at = lax.axis_index("row"), lax.axis_index("col")
    top = jnp.where(row_at > 0, 1.0, 0.0)
    bottom = jnp.where(row_at < row_count - 1, 1.0, 0.0)
    before = jnp.where(col_at > 0, 1.0, 0.0)
    after = jnp.where(col_at < col_count - 1, 1.0, 0.0)
    row_id = lax.broadcasted_iota(jnp.int32, (tile + BAND, LANES), 0)
    row_gain = rate * jnp.where(
        row_id < BORDER, top, jnp.where(row_id >= BORDER + tile, bottom, 1.0)
    )
    return row_gain, top, bottom, before, after


def second_kernel(
    row_count, col_count,
    positions, counts, probe, doubled, amplitudes, right_f, left_f, right_b, left_b,
    up, down, left, right, cur_in, acc_in,
    cur, acc, order,
):
    tile, width = cur.shape[1] - SUBLANES - BAND, cur.shape[2] - 2 * LANES
    extent = tile + BAND
    rate = step_of(probe)
    row_gain, top, bottom, before, after = grid_gains(row_count, col_count, tile, rate)
    slots = Slots(positions, counts[0, 0], order, tile - doubled.shape[2])
    inner = slice(LANES, LANES + width)
    lane = lane_iota(extent)
    is_low, is_high = lane < BORDER, lane >= LANES - BORDER
    lefts, rights = map(unpack_planes, by_side("col", left[...], right[...]))
    up, down = by_side("row", up[...], down[...])
    for plane in range(2):
        for row, band, on_grid in ((0, up, top), (tile, down, bottom)):
            halo_first = row == 0
            values = band[:, plane * width : (plane + 1) * width]
            own, out = (BORDER, 0) if halo_first else (0, BORDER)
            own_rows = slice(row + own, row + own + BORDER)
            out_rows = slice(row + out, row + out + BORDER)
            cur[plane, own_rows, inner] += rate * values[own : own + BORDER]
            acc[plane, own_rows, inner] += values[own : own + BORDER]
            cur[plane, out_rows, inner] += (rate * on_grid) * (
                acc[plane, out_rows, inner] + values[out : out + BORDER]
            )
            acc[plane, out_rows, inner] = jnp.zeros_like(acc[plane, out_rows, inner])
            halo = unpack_planes(band[:, 2 * width :])[plane]
            for lanes, keep in (
                (slice(0, LANES), is_high[:BAND]),
                (slice(LANES + width, None), is_low[:BAND]),
            ):
                acc[plane, row : row + BAND, lanes] += jnp.where(keep, halo, 0.0)
        for block, band, on_grid, own_first in (
            (0, lefts[plane], before, False),
            (width, rights[plane], after, True),
        ):
            low_block = slice(block, block + LANES)
            high_block = slice(block + LANES, block + 2 * LANES)
            own, out = (low_block, high_block) if own_first else (high_block, low_block)
            keep_own, keep_out = (is_high, is_low) if own_first else (is_low, is_high)
            own_band = jnp.where(keep_own, band, 0.0)
            cur[plane, :extent, own] += row_gain * own_band
            acc[plane, BORDER : BORDER + tile, own] += own_band[BORDER : BORDER + tile]
            cur[plane, :extent, out] += (row_gain * on_grid) * (
                acc[plane, :extent, out] + jnp.where(keep_out, band, 0.0)
            )
            acc[plane, :extent, out] = jnp.zeros_like(acc[plane, :extent, out])
    gradient_slots(
        cur, acc, doubled, amplitudes, positions, order, 0, slots.corner()[0],
        (right_f, left_f, right_b, left_b),
    )


def corner_slots_kernel(
    row_count, col_count,
    positions, counts, probe, doubled, amplitudes, right_f, left_f, right_b, left_b,
    left, right, cur_in, acc_in,
    cur, acc, to_up, to_down, to_left, to_right, order,
):
    tile, width = cur.shape[1] - SUBLANES - BAND, cur.shape[2] - 2 * LANES
    row_gain, _, _, before, after = grid_gains(row_count, col_count, tile, step_of(probe))
    lane = lane_iota(BAND)
    is_low, is_high = lane < BORDER, lane >= LANES - BORDER
    left, right = by_side("col", left[...], right[...])
    for block, corners, on_grid, own_first in (
        (0, left, before, False), (width, right, after, True),
    ):
        low_block = slice(block, block + LANES)
        high_block = slice(block + LANES, block + 2 * LANES)
        own, out = (low_block, high_block) if own_first else (high_block, low_block)
        keep_own, keep_out = (is_high, is_low) if own_first else (is_low, is_high)
        both = unpack_planes(corners)
        for plane in range(2):
            for row, own_at in ((0, BORDER), (tile, 0)):
                rows = slice(row, row + BAND)
                part = both[plane][:BAND] if row == 0 else both[plane][BAND:]
                own_part = jnp.where(keep_own, part, 0.0)
                gain = row_gain[rows]
                cur[plane, rows, own] += gain * own_part
                cur[plane, rows, out] += (gain * on_grid) * jnp.where(keep_out, part, 0.0)
                acc[plane, row + own_at : row + own_at + BORDER, own] += own_part[
                    own_at : own_at + BORDER
                ]
    found = Slots(positions, counts[0, 0], order, tile - doubled.shape[2]).append(
        is_reaching_corner, 0
    )
    gradient_slots(
        cur, acc, doubled, amplitudes, positions, order, 0, found,
        (right_f, left_f, right_b, left_b), SMALL,
    )
    store_bands(acc, 0, BORDER + tile, BORDER, to_up, to_down, to_left, to_right)


def second_rest_kernel(
    positions, counts, cur, doubled, amplitudes, right_f, left_f, right_b, left_b, acc_in,
    acc, order,
):
    tile = cur.shape[1] - SUBLANES - BAND
    slots = Slots(positions, counts[0, 0], order, tile - doubled.shape[2])
    begin, end = slots.rest()
    gradient_slots(
        cur, acc, doubled, amplitudes, positions, order, begin, end,
        (right_f, left_f, right_b, left_b),
    )


def store_bands(acc, top, bottom, count, to_up, to_down, to_left, to_right):
    ups = pack_row_band(acc, top, count), pack_row_band(acc, bottom, count)
    to_up[...], to_down[...] = by_side("row", *ups)
    sides = pack_side_bands(acc, to_left.shape[0])
    if count == BAND:
        sides = by_side("col", *sides)
    to_left[...], to_right[...] = sides


def middle_kernel(objects, probe, acc, held, estimate, correction, estimated, corrected, sems):
    tile, width = objects.shape[1:]
    load = pltpu.make_async_copy(objects, held, sems.at[0])
    load.start()
    rate = step_of(probe)
    rows, lanes = slice(BORDER, tile - BORDER), slice(LANES, width - LANES)
    load.wait()
    for plane in range(2):
        corrected[plane] = rate * acc[plane, 2 * BORDER : tile, 2 * LANES : width]
        estimated[plane] = held[plane, rows, lanes] + corrected[plane]
    stores = [
        pltpu.make_async_copy(
            source,
            target.at[:, pl.ds(BORDER, tile - BAND), pl.ds(LANES, width - 2 * LANES)],
            sems.at[1 + i],
        )
        for i, (source, target) in enumerate(((corrected, correction), (estimated, estimate)))
    ]
    for store in stores:
        store.start()
    for store in stores:
        store.wait()


def last_kernel(
    probe, up, down, left, right, acc, held, estimate_in, correction_in,
    estimate, correction, side_parts, row_parts, sems,
):
    tile, width = held.shape[1:]
    rate = step_of(probe)
    lane = lane_iota(tile)
    rows = slice(BORDER, BORDER + tile)
    lefts, rights = map(unfold_side, by_side("col", left[...], right[...]))
    up, down = by_side("row", up[...], down[...])
    stores = []

    def send(index, source, target):
        store = pltpu.make_async_copy(source, target, sems.at[index])
        store.start()
        stores.append(store)

    for side, (block, bands) in enumerate(((0, lefts), (width - LANES, rights))):
        keep = (lane < BORDER) if side == 0 else (lane >= LANES - BORDER)
        for plane in range(2):
            at = plane * width + block
            total = acc[plane, rows, LANES + block : 2 * LANES + block]
            total += jnp.where(keep, bands[plane], 0.0)
            total = jnp.concatenate(
                [
                    total[:BORDER] + up[:, at : at + LANES],
                    total[BORDER : tile - BORDER],
                    total[tile - BORDER :] + down[:, at : at + LANES],
                ],
                axis=0,
            )
            side_parts[0, side, plane] = rate * total
            side_parts[1, side, plane] = (
                held[plane, :, block : block + LANES] + side_parts[0, side, plane]
            )
        for number, target in enumerate((correction, estimate)):
            send(
                2 * side + number, side_parts.at[number, side],
                target.at[:, :, pl.ds(block, LANES)],
            )
    lanes = slice(LANES, width - LANES)
    for end, (row, band) in enumerate(((0, up), (tile - BORDER, down))):
        for plane in range(2):
            total = acc[plane, BORDER + row : 2 * BORDER + row, 2 * LANES : width]
            total += band[:, plane * width + LANES : (plane + 1) * width - LANES]
            row_parts[0, end, plane] = rate * total
            row_parts[1, end, plane] = (
                held[plane, row : row + BORDER, lanes] + row_parts[0, end, plane]
            )
        for number, target in enumerate((correction, estimate)):
            send(
                4 + 2 * end + number, row_parts.at[number, end],
                target.at[:, pl.ds(row, BORDER), pl.ds(LANES, width - 2 * LANES)],
            )
    for store in stores:
        store.wait()


VMEM = pl.BlockSpec(memory_space=pltpu.VMEM)
SMEM = pl.BlockSpec(memory_space=pltpu.SMEM)
HBM = pl.BlockSpec(memory_space=pltpu.HBM)
PARAMS = pltpu.CompilerParams(vmem_limit_bytes=32 * 1024 * 1024)


def f32(*shape):
    return pltpu.VMEM(shape, jnp.float32)


def in_hbm(array):
    return pltpu.with_memory_space_constraint(array, pltpu.HBM)


def in_vmem(array):
    return pltpu.with_memory_space_constraint(array, pltpu.VMEM)


def swap_pairs(axis, first, second):
    count = lax.axis_size(axis)

    def swap(array, begin):
        ends = [(i, i + 1) for i in range(begin, count - 1, 2)]
        return in_vmem(lax.ppermute(array, axis, ends + [(j, i) for i, j in ends]))

    first = swap(first, 0)
    second = swap(second, 1)
    return first, second


def on_device(object_field, probe_field, amplitudes, positions, counts):
    tile, width = object_field.shape[1:]
    probe = probe_field.shape[1]
    extent = tile + BAND
    padded = f32(2, extent + SUBLANES, width + 2 * LANES)
    doubled_shape = f32(2, 2 * probe, probe)
    tables = tuple(jnp.asarray(table) for table in dft_blocks(probe))
    places = positions[0, 0]
    order = pltpu.SMEM((amplitudes.shape[0] + 1,), jnp.int32)
    sides = (f32(extent, LANES), f32(extent, LANES))

    def row_bands(count):
        band = f32(count, 2 * width + LANES)
        return (band, band)

    def call(kernel, scalars, arrays, outs, scratch=(), aliases=None):
        return pl.pallas_call(
            kernel,
            out_shape=outs,
            in_specs=[SMEM] * len(scalars) + [VMEM] * len(arrays),
            out_specs=jax.tree.map(lambda out: VMEM, outs),
            scratch_shapes=list(scratch),
            input_output_aliases=aliases or {},
            compiler_params=PARAMS,
        )(*scalars, *arrays)

    slots = (in_hbm(places), counts)
    strips = [
        jnp.concatenate([object_field[0, rows], object_field[1, rows]], axis=1)
        for rows in (slice(0, BORDER), slice(tile - BORDER, tile))
    ]
    table_shapes = tuple(pltpu.VMEM(table.shape, table.dtype) for table in tables)
    up, down = swap_pairs("row", *by_side("row", *strips))
    cur, acc, doubled, held, *tables = pl.pallas_call(
        inner_start_kernel,
        out_shape=(padded, padded, doubled_shape, f32(*amplitudes.shape), *table_shapes),
        in_specs=[SMEM, SMEM] + [HBM] * (3 + len(tables)),
        out_specs=(VMEM,) * (4 + len(tables)),
        scratch_shapes=[order, pltpu.SemaphoreType.DMA((7 + len(tables),))],
        compiler_params=PARAMS,
        name="inner_start",
    )(*slots, *map(in_hbm, (object_field, probe_field, amplitudes, *tables)))
    to_left, to_right = call(
        object_pack_kernel, (), (cur, up, down),
        (f32(extent // 2, LANES),) * 2, (f32(extent, LANES),),
    )
    left, right = swap_pairs("col", to_left, to_right)
    cur, acc = call(
        side_kernel, slots, (up, down, doubled, held, *tables, cur, acc),
        (padded, padded), (order,), {10: 0, 11: 1},
    )
    cur, acc, to_up, to_down, to_left, to_right = call(
        outer_kernel, slots, (left, right, doubled, held, *tables, cur, acc),
        (padded, padded, *row_bands(BAND), *sides), (order,), {10: 0, 11: 1},
    )
    up, down = swap_pairs("row", to_up, to_down)
    left, right = swap_pairs("col", to_left, to_right)
    cur, acc = call(
        deep_kernel, slots, (probe_field, doubled, held, *tables, cur, acc),
        (padded, padded), (order,), {9: 0, 10: 1},
    )
    corners = (f32(2 * BAND, LANES),) * 2
    left_corners, right_corners = swap_pairs("col", *call(corner_kernel, (), (up, down, acc), corners))
    grid = (lax.axis_size("row"), lax.axis_size("col"))
    cur, acc = call(
        functools.partial(second_kernel, *grid), slots,
        (probe_field, doubled, held, *tables, up, down, left, right, cur, acc),
        (padded, padded), (order,), {13: 0, 14: 1},
    )
    cur, acc, to_up, to_down, to_left, to_right = call(
        functools.partial(corner_slots_kernel, *grid), slots,
        (probe_field, doubled, held, *tables, left_corners, right_corners, cur, acc),
        (padded, padded, *row_bands(BORDER), *sides), (order,), {11: 0, 12: 1},
    )
    up, down = swap_pairs("row", to_up, to_down)
    acc = call(
        second_rest_kernel, slots, (cur, doubled, held, *tables, acc),
        padded, (order,), {9: 0},
    )
    folded = f32(tile // 2, LANES)
    to_left, to_right = call(
        last_corner_kernel, (), (up, down, to_left, to_right, acc),
        (folded, folded), (f32(tile, LANES),),
    )
    left, right = swap_pairs("col", to_left, to_right)
    result = jax.ShapeDtypeStruct((2, tile, width), jnp.float32)
    middle = f32(2, tile - BAND, width - 2 * LANES)
    tile_held, estimate, correction = pl.pallas_call(
        middle_kernel,
        out_shape=(f32(2, tile, width), result, result),
        in_specs=[HBM, VMEM, VMEM],
        out_specs=(VMEM, HBM, HBM),
        scratch_shapes=[middle, middle, pltpu.SemaphoreType.DMA((3,))],
        compiler_params=PARAMS,
        name="middle",
    )(in_hbm(object_field), probe_field, acc)
    estimate, correction = pl.pallas_call(
        last_kernel,
        out_shape=(result, result),
        in_specs=[VMEM] * 7 + [HBM] * 2,
        out_specs=(HBM, HBM),
        scratch_shapes=[
            f32(2, 2, 2, tile, LANES), f32(2, 2, 2, BORDER, width - 2 * LANES),
            pltpu.SemaphoreType.DMA((8,)),
        ],
        input_output_aliases={7: 0, 8: 1},
        compiler_params=PARAMS,
        name="finish",
    )(probe_field, up, down, left, right, acc, tile_held, estimate, correction)
    return estimate, correction


def solution(mesh):
    placed = (
        P(None, "row", "col"),
        P(),
        P("row", None, "col"),
        P("row", "col", None, None),
        P("row", "col"),
    )
    return jax.shard_map(
        on_device,
        mesh=mesh,
        in_specs=placed,
        out_specs=(P(None, "row", "col"), P(None, "row", "col")),
        check_vma=False,
    )
```

```python
import functools

import jax
import jax.numpy as jnp
import numpy as np
from jax import lax
from jax.experimental import pallas as pl
from jax.experimental.pallas import tpu as pltpu
from jax.sharding import PartitionSpec as P

BORDER = 32
BAND = 2 * BORDER
ITERS = 2
LANES = 128
SUBLANES = 8
LARGE, MIDDLE, SMALL = 8, 4, 2
RIGHT = 4

smoothing = 0.5
step_gain = 0.5


def split_host(table):
    high = table.astype(jnp.bfloat16)
    low = (table - high.astype(np.float64)).astype(jnp.bfloat16)
    return high, low


def dft_blocks(length):
    counter = np.arange(length)
    angles = 2.0 * np.pi * (np.outer(counter, counter) % length) / length
    real, imag = np.cos(angles) / np.sqrt(length), -np.sin(angles) / np.sqrt(length)
    blocks = []
    for sign in (1.0, -1.0):
        block = np.block([[real, sign * imag], [-sign * imag, real]])
        blocks.append(np.concatenate(split_host(block), axis=0))
    return blocks


def split(value):
    high = value.astype(jnp.bfloat16)
    low = (value - high.astype(jnp.float32)).astype(jnp.bfloat16)
    return high, low


def dot(left, right):
    return jnp.dot(left, right, preferred_element_type=jnp.float32)


def times_right(rows, block):
    high, low = split(rows)
    count = block.shape[0] // 2
    stacked = jnp.concatenate([block[:count], block], axis=0)
    return dot(jnp.concatenate([high, low, high], axis=1), stacked)


def right_groups(members, block):
    rows = members[0].shape[0]
    results = []
    count = min(RIGHT, len(members))
    for start in range(0, len(members), count):
        product = times_right(jnp.concatenate(members[start : start + count], axis=0), block[...])
        results += [product[i * rows : (i + 1) * rows] for i in range(count)]
    return results


def times_left(block, columns):
    high, low = split(columns)
    count = block.shape[0] // 2
    both = dot(block, high)
    return both[:count] + (both[count:] + dot(block[:count], low))


def lane_iota(rows):
    return lax.broadcasted_iota(jnp.int32, (rows, LANES), 1)


def edge_lanes(rows):
    lane = lane_iota(rows)
    return (lane < BORDER) | (lane >= LANES - BORDER)


def pack_planes(real, imag):
    return jnp.where(edge_lanes(real.shape[0]), real, pltpu.roll(imag, LANES // 2, 1))


def unpack_planes(packed):
    return packed, pltpu.roll(packed, LANES // 2, 1)


def slot_kinds(row, col, last):
    row_out, col_out = (row < 0) | (row > last), (col < 0) | (col > last)
    row_edge = (row < BORDER) | (row > last - BORDER)
    col_edge = (col < BORDER) | (col > last - BORDER)
    return row_out, col_out, row_edge, col_edge


def is_deep(row_out, col_out, row_edge, col_edge):
    return jnp.logical_not(row_edge | col_edge)


def is_beside(row_out, col_out, row_edge, col_edge):
    return col_out


def is_early(row_out, col_out, row_edge, col_edge):
    return (row_edge | col_edge) & jnp.logical_not(col_out)


def is_reaching(row_out, col_out, row_edge, col_edge):
    return (row_out | col_out) & jnp.logical_not(row_edge & col_edge)


def is_rim(row_out, col_out, row_edge, col_edge):
    return (row_edge ^ col_edge) & jnp.logical_not(row_out | col_out)


def is_reaching_corner(row_out, col_out, row_edge, col_edge):
    return (row_out | col_out) & row_edge & col_edge


def is_rim_corner(row_out, col_out, row_edge, col_edge):
    return row_edge & col_edge & jnp.logical_not(row_out | col_out)


class Plan:
    DEEP, SIDE, BESIDE, SECOND, CORNER, ROW, COL, NUMBER = range(8)
    LEAD, SIDE_STOP, BAND_BEGIN, BAND_END, SECOND_DEEP, BESIDE_END, SECOND_STOP, REST_END, CORNER_END = range(9)

    @staticmethod
    def shape(slot_total):
        return 8, max(slot_total + 1, 9)

    @staticmethod
    def fill(plan, positions, live, last):
        def append(row, kind, begin, skip=0):
            def visit(slot, carry):
                found, seen = carry
                kinds = slot_kinds(positions[0, slot], positions[1, slot], last)
                of_kind = jnp.where(kind(*kinds), 1, 0)
                plan[row, found] = slot
                return found + jnp.where(seen >= skip, of_kind, 0), seen + of_kind

            return lax.fori_loop(0, live, visit, (begin, 0))[0]

        def place(slot, carry):
            plan[Plan.ROW, slot] = positions[0, slot]
            plan[Plan.COL, slot] = positions[1, slot]
            return carry

        lax.fori_loop(0, live, place, 0)
        deep = append(Plan.DEEP, is_deep, 0)
        lead = jnp.minimum(deep, MIDDLE)
        early = append(Plan.SIDE, is_early, 0)
        side_end = append(Plan.SIDE, is_deep, early, lead)
        side_stop = jnp.minimum(side_end, round_up(early))
        done = lead + side_stop - early
        room = 2 * LARGE - (deep - done + LARGE - 1) // LARGE * LARGE
        second_deep = jnp.minimum(deep, jnp.maximum(room, 0))
        reaching = append(Plan.SECOND, is_reaching, 0)
        rim = append(Plan.SECOND, is_rim, reaching)
        rim_corner = append(Plan.SECOND, is_rim_corner, rim)
        numbers = (
            lead, side_stop, done, deep, second_deep,
            append(Plan.BESIDE, is_beside, 0),
            jnp.minimum(rim, round_up(reaching)),
            append(Plan.SECOND, is_deep, rim_corner, second_deep),
            append(Plan.CORNER, is_reaching_corner, 0),
        )
        for index, number in enumerate(numbers):
            plan[Plan.NUMBER, index] = number


def round_up(count):
    return jnp.maximum((count + LARGE - 1) // LARGE, 1) * LARGE


def gradient_slots(cur, acc, doubled, amplitudes, plan, listed, begin, stop, tables, size=LARGE, before_use=None):
    right_f, right_b = tables
    left_f, left_b = right_b, right_f
    probe = doubled.shape[1] // 2
    frame = probe + SUBLANES
    lane = lane_iota(frame)
    sub = lax.broadcasted_iota(jnp.int32, (SUBLANES, LANES), 0)

    def group_body(group, carry):
        places, probes, exits = [], [], []
        for member in range(size):
            slot = begin + group * size + member
            at = plan[listed, jnp.minimum(slot, stop - 1)]
            row = plan[Plan.ROW, at] + BORDER
            col = plan[Plan.COL, at] + LANES
            row_at = pl.multiple_of(row // SUBLANES * SUBLANES, SUBLANES)
            col_at = pl.multiple_of(col // LANES * LANES, LANES)
            row_off, col_off = row - row_at, col - col_at
            from_left = lane >= col_off
            from_top = sub >= row_off
            planes, rolled = [], []
            for plane in range(2):
                wide = jnp.where(
                    from_left,
                    cur[plane, pl.ds(row_at, frame), pl.ds(col_at, LANES)],
                    cur[plane, pl.ds(row_at, frame), pl.ds(col_at + LANES, LANES)],
                )
                first = jnp.where(from_top, wide[:SUBLANES], wide[probe:])
                planes.append(jnp.concatenate([first, wide[SUBLANES:probe]], axis=0))
                shifted = doubled[plane, pl.ds(probe - row_off, probe), :]
                rolled.append(pltpu.roll(shifted, col_off, 1))
            places.append((at, slot, row_at, col_at, from_left, from_top))
            probes.append(rolled)
            exits.append(
                jnp.concatenate(
                    [
                        rolled[0] * planes[0] - rolled[1] * planes[1],
                        rolled[0] * planes[1] + rolled[1] * planes[0],
                    ],
                    axis=1,
                )
            )
        half = right_groups(exits, right_f)
        shrunk = []
        for pair in range(0, size, 2):
            first, second = half[pair], half[pair + 1]
            stacked = jnp.concatenate(
                [
                    jnp.concatenate([first[:, :probe], second[:, :probe]], axis=1),
                    jnp.concatenate([first[:, probe:], second[:, probe:]], axis=1),
                ],
                axis=0,
            )
            wave = times_left(left_f[...], stacked)
            if before_use is not None and pair == 0:
                before_use()
            for member in range(2):
                at = places[pair + member][0]
                real = wave[:probe, member * probe : (member + 1) * probe]
                imag = wave[probe:, member * probe : (member + 1) * probe]
                shrink = amplitudes[at] * lax.rsqrt(real * real + imag * imag + smoothing) - 1.0
                shrunk.append(jnp.concatenate([real * shrink, imag * shrink], axis=1))
        half = right_groups(shrunk, right_b)
        for pair in range(0, size, 2):
            first, second = half[pair], half[pair + 1]
            stacked = jnp.concatenate(
                [
                    jnp.concatenate([first[:, :probe], second[:, :probe]], axis=1),
                    jnp.concatenate([first[:, probe:], second[:, probe:]], axis=1),
                ],
                axis=0,
            )
            back = times_left(left_b[...], stacked)
            for member in range(2):
                at, slot, row_at, col_at, from_left, from_top = places[pair + member]
                real = back[:probe, member * probe : (member + 1) * probe]
                imag = back[probe:, member * probe : (member + 1) * probe]
                rolled = probes[pair + member]
                grads = (
                    rolled[0] * real + rolled[1] * imag,
                    rolled[0] * imag - rolled[1] * real,
                )
                is_live = slot < stop
                keep_left = from_left & is_live
                keep_right = jnp.logical_not(from_left) & is_live
                for plane in range(2):
                    grad = grads[plane]
                    frame_grad = jnp.concatenate(
                        [
                            jnp.where(from_top, grad[:SUBLANES], 0.0),
                            grad[SUBLANES:],
                            jnp.where(from_top, 0.0, grad[:SUBLANES]),
                        ],
                        axis=0,
                    )
                    rows = pl.ds(row_at, frame)
                    acc[plane, rows, pl.ds(col_at, LANES)] += jnp.where(keep_left, frame_grad, 0.0)
                    acc[plane, rows, pl.ds(col_at + LANES, LANES)] += jnp.where(
                        keep_right, frame_grad, 0.0
                    )
        return carry

    lax.fori_loop(0, (stop - begin + size - 1) // size, group_body, 0)


def step_of(probe):
    return step_gain / (jnp.max(probe[0] * probe[0] + probe[1] * probe[1]) + 1e-06)


def pack_row_band(acc, row, count):
    rows = slice(row, row + count)
    width = acc.shape[2] - 2 * LANES
    is_low = lane_iota(count) < BORDER
    halo = [
        jnp.where(is_low, acc[plane, rows, LANES + width :], acc[plane, rows, :LANES])
        for plane in range(2)
    ]
    own = [acc[plane, rows, LANES : LANES + width] for plane in range(2)]
    return jnp.concatenate([*own, pack_planes(*halo)], axis=1)


def pack_side_bands(acc, height):
    width = acc.shape[2] - 2 * LANES
    is_low = lane_iota(height) < BORDER
    return [
        pack_planes(
            *[
                jnp.where(
                    is_low,
                    acc[plane, :height, block + LANES : block + 2 * LANES],
                    acc[plane, :height, block : block + LANES],
                )
                for plane in range(2)
            ]
        )
        for block in (0, width)
    ]


def inner_start_kernel(
    positions, counts, objects, probe_in, amplitudes, *refs
):
    table_count = (len(refs) - 6) // 2
    tables_in, refs = refs[:table_count], refs[table_count:]
    cur, acc, doubled, held, plan = refs[:5]
    tables, sems = refs[5:-1], refs[-1]
    tile, width = objects.shape[1:]
    probe = probe_in.shape[1]
    sources = list(zip(tables_in, tables))
    for plane in range(2):
        sources.append(
            (
                objects.at[plane],
                cur.at[plane, pl.ds(BORDER, tile), pl.ds(LANES, width)],
            )
        )
        for row in (0, probe):
            sources.append((probe_in.at[plane], doubled.at[plane, pl.ds(row, probe), :]))
    sources.append((amplitudes, held))
    loads = [
        pltpu.make_async_copy(source, target, sems.at[i])
        for i, (source, target) in enumerate(sources)
    ]
    for load in loads:
        load.start()
    acc[...] = jnp.zeros_like(acc)
    Plan.fill(plan, positions, counts[0, 0], tile - probe)
    lead = plan[Plan.NUMBER, Plan.LEAD]
    for load in loads[:-1]:
        load.wait()
    gradient_slots(
        cur, acc, doubled, held, plan, Plan.DEEP, 0, lead, tables, MIDDLE, loads[-1].wait
    )

    @pl.when(lead == 0)
    def unused():
        loads[-1].wait()


def side_kernel(
    plan, up, down, doubled, amplitudes, forth, back, cur_in, acc_in,
    cur, acc,
):
    tile, width = cur.shape[1] - SUBLANES - BAND, cur.shape[2] - 2 * LANES
    up, down = by_side("row", up[...], down[...])
    inner = slice(LANES, LANES + width)
    for plane in range(2):
        lanes = slice(plane * width, (plane + 1) * width)
        cur[plane, :BORDER, inner] = up[:, lanes]
        cur[plane, BORDER + tile : BAND + tile, inner] = down[:, lanes]
        cur[plane, BAND + tile :, :] = jnp.zeros_like(cur[plane, BAND + tile :, :])
    gradient_slots(
        cur, acc, doubled, amplitudes, plan, Plan.SIDE, 0, plan[Plan.NUMBER, Plan.SIDE_STOP],
        (forth, back),
    )


def fold_side(whole, is_low):
    half = whole.shape[0] // 2
    low = lane_iota(half) % (LANES // 2) < BORDER
    keep = low if is_low else jnp.logical_not(low)
    return jnp.where(keep, whole[:half, :], pltpu.roll(whole[half:, :], BORDER, 1))


def unfold_side(packed):
    return unpack_planes(
        jnp.concatenate([packed, pltpu.roll(packed, LANES - BORDER, 1)], axis=0)
    )


def by_side(axis, first, second):
    even = lax.axis_index(axis) % 2 == 0
    return jnp.where(even, second, first), jnp.where(even, first, second)


def object_pack_kernel(cur, up, down, to_left, to_right, whole):
    count = up.shape[0]
    width = up.shape[1] // 2
    extent = whole.shape[0]
    rows = slice(count, extent - count)
    up, down = by_side("row", up[...], down[...])
    parts = []
    for side in range(2):
        block = side * (width - LANES)
        for row, band in ((0, up), (extent - count, down)):
            whole[row : row + count, :] = pack_planes(
                *[
                    band[:, plane * width + block : plane * width + block + LANES]
                    for plane in range(2)
                ]
            )
        lanes = slice(LANES + block, 2 * LANES + block)
        whole[rows, :] = pack_planes(cur[0, rows, lanes], cur[1, rows, lanes])
        parts.append(fold_side(whole, side == 0))
    to_left[...], to_right[...] = by_side("col", *parts)


def outer_kernel(
    plan, left, right, doubled, amplitudes,
    forth, back, cur_in, acc_in,
    cur, acc, to_up, to_down, to_left, to_right,
):
    extent = 2 * left.shape[0]
    tile, width = extent - BAND, cur.shape[2] - 2 * LANES
    lane = lane_iota(extent)
    lefts, rights = map(unfold_side, by_side("col", left[...], right[...]))
    for plane in range(2):
        cur[plane, :extent, :LANES] = jnp.where(lane >= LANES - BORDER, lefts[plane], 0.0)
        cur[plane, :extent, LANES + width :] = jnp.where(lane < BORDER, rights[plane], 0.0)
    gradient_slots(
        cur, acc, doubled, amplitudes, plan, Plan.BESIDE, 0, plan[Plan.NUMBER, Plan.BESIDE_END],
        (forth, back), MIDDLE,
    )
    store_bands(acc, 0, tile, BAND, to_up, to_down, to_left, to_right)


def corner_parts(band, width):
    is_low = lane_iota(band.shape[0]) < BORDER
    halo = unpack_planes(band[:, 2 * width :])
    lefts, rights = [], []
    for plane in range(2):
        low = band[:, plane * width : plane * width + LANES]
        high = band[:, (plane + 1) * width - LANES : (plane + 1) * width]
        lefts.append(jnp.where(is_low, low, halo[plane]))
        rights.append(jnp.where(is_low, halo[plane], high))
    return pack_planes(*lefts), pack_planes(*rights)


def corner_kernel(up, down, after, to_left, to_right):
    count = up.shape[0]
    width = (up.shape[1] - LANES) // 2
    up, down = by_side("row", up[...], down[...])
    tops, bottoms = corner_parts(up, width), corner_parts(down, width)
    to_left[...], to_right[...] = by_side(
        "col", *(jnp.concatenate([tops[i], bottoms[i]], axis=0) for i in range(2))
    )


def last_corner_kernel(up, down, left, right, after, to_left, to_right, whole):
    count = up.shape[0]
    tile = left.shape[0] - BAND
    width = (up.shape[1] - LANES) // 2
    up, down = by_side("row", up[...], down[...])
    tops, bottoms = corner_parts(up, width), corner_parts(down, width)
    parts = []
    for side, source in enumerate((left, right)):
        whole[...] = source[BORDER : BORDER + tile, :]
        whole[:count, :] += tops[side]
        whole[tile - count :, :] += bottoms[side]
        parts.append(fold_side(whole, side == 1))
    to_left[...], to_right[...] = by_side("col", *parts)


def deep_kernel(
    plan, objects, probe, doubled, amplitudes, forth, back, cur_in, acc_in,
    cur, acc, tile_held, sem,
):
    load = pltpu.make_async_copy(objects, tile_held, sem)
    load.start()
    tile, width = cur.shape[1] - SUBLANES - BAND, cur.shape[2] - 2 * LANES
    rate = step_of(probe)
    middle, inner = slice(BORDER, BORDER + tile), slice(LANES, LANES + width)
    begins = (plan[Plan.NUMBER, Plan.BAND_BEGIN], 0)
    ends = (plan[Plan.NUMBER, Plan.BAND_END], plan[Plan.NUMBER, Plan.SECOND_DEEP])

    def turn(iteration, carry):
        @pl.when(iteration == 1)
        def update():
            for plane in range(2):
                cur[plane, middle, inner] += rate * acc[plane, middle, inner]

        gradient_slots(
            cur, acc, doubled, amplitudes, plan, Plan.DEEP,
            jnp.where(iteration == 0, *begins), jnp.where(iteration == 0, *ends),
            (forth, back),
        )
        return carry

    lax.fori_loop(0, ITERS, turn, 0)
    load.wait()


def grid_gains(row_count, col_count, tile, rate):
    row_at, col_at = lax.axis_index("row"), lax.axis_index("col")
    top = jnp.where(row_at > 0, 1.0, 0.0)
    bottom = jnp.where(row_at < row_count - 1, 1.0, 0.0)
    before = jnp.where(col_at > 0, 1.0, 0.0)
    after = jnp.where(col_at < col_count - 1, 1.0, 0.0)
    row_id = lax.broadcasted_iota(jnp.int32, (tile + BAND, LANES), 0)
    row_gain = rate * jnp.where(
        row_id < BORDER, top, jnp.where(row_id >= BORDER + tile, bottom, 1.0)
    )
    return row_gain, top, bottom, before, after


def second_kernel(
    row_count, col_count,
    plan, probe, doubled, amplitudes, forth, back,
    up, down, left, right, cur_in, acc_in,
    cur, acc,
):
    tile, width = cur.shape[1] - SUBLANES - BAND, cur.shape[2] - 2 * LANES
    extent = tile + BAND
    rate = step_of(probe)
    row_gain, top, bottom, before, after = grid_gains(row_count, col_count, tile, rate)
    inner = slice(LANES, LANES + width)
    lane = lane_iota(extent)
    is_low, is_high = lane < BORDER, lane >= LANES - BORDER
    lefts, rights = map(unpack_planes, by_side("col", left[...], right[...]))
    up, down = by_side("row", up[...], down[...])
    for plane in range(2):
        for row, band, on_grid in ((0, up, top), (tile, down, bottom)):
            halo_first = row == 0
            values = band[:, plane * width : (plane + 1) * width]
            own, out = (BORDER, 0) if halo_first else (0, BORDER)
            own_rows = slice(row + own, row + own + BORDER)
            out_rows = slice(row + out, row + out + BORDER)
            cur[plane, own_rows, inner] += rate * values[own : own + BORDER]
            acc[plane, own_rows, inner] += values[own : own + BORDER]
            cur[plane, out_rows, inner] += (rate * on_grid) * (
                acc[plane, out_rows, inner] + values[out : out + BORDER]
            )
            acc[plane, out_rows, inner] = jnp.zeros_like(acc[plane, out_rows, inner])
            halo = unpack_planes(band[:, 2 * width :])[plane]
            for lanes, keep in (
                (slice(0, LANES), is_high[:BAND]),
                (slice(LANES + width, None), is_low[:BAND]),
            ):
                acc[plane, row : row + BAND, lanes] += jnp.where(keep, halo, 0.0)
        for block, band, on_grid, own_first in (
            (0, lefts[plane], before, False),
            (width, rights[plane], after, True),
        ):
            low_block = slice(block, block + LANES)
            high_block = slice(block + LANES, block + 2 * LANES)
            own, out = (low_block, high_block) if own_first else (high_block, low_block)
            keep_own, keep_out = (is_high, is_low) if own_first else (is_low, is_high)
            own_band = jnp.where(keep_own, band, 0.0)
            cur[plane, :extent, own] += row_gain * own_band
            acc[plane, BORDER : BORDER + tile, own] += own_band[BORDER : BORDER + tile]
            cur[plane, :extent, out] += (row_gain * on_grid) * (
                acc[plane, :extent, out] + jnp.where(keep_out, band, 0.0)
            )
            acc[plane, :extent, out] = jnp.zeros_like(acc[plane, :extent, out])
    gradient_slots(
        cur, acc, doubled, amplitudes, plan, Plan.SECOND, 0, plan[Plan.NUMBER, Plan.SECOND_STOP],
        (forth, back),
    )


def corner_slots_kernel(
    row_count, col_count,
    plan, probe, doubled, amplitudes, forth, back,
    left, right, cur_in, acc_in,
    cur, acc, to_up, to_down, to_left, to_right,
):
    tile, width = cur.shape[1] - SUBLANES - BAND, cur.shape[2] - 2 * LANES
    row_gain, _, _, before, after = grid_gains(row_count, col_count, tile, step_of(probe))
    lane = lane_iota(BAND)
    is_low, is_high = lane < BORDER, lane >= LANES - BORDER
    left, right = by_side("col", left[...], right[...])
    for block, corners, on_grid, own_first in (
        (0, left, before, False), (width, right, after, True),
    ):
        low_block = slice(block, block + LANES)
        high_block = slice(block + LANES, block + 2 * LANES)
        own, out = (low_block, high_block) if own_first else (high_block, low_block)
        keep_own, keep_out = (is_high, is_low) if own_first else (is_low, is_high)
        both = unpack_planes(corners)
        for plane in range(2):
            for row, own_at in ((0, BORDER), (tile, 0)):
                rows = slice(row, row + BAND)
                part = both[plane][:BAND] if row == 0 else both[plane][BAND:]
                own_part = jnp.where(keep_own, part, 0.0)
                gain = row_gain[rows]
                cur[plane, rows, own] += gain * own_part
                cur[plane, rows, out] += (gain * on_grid) * jnp.where(keep_out, part, 0.0)
                acc[plane, row + own_at : row + own_at + BORDER, own] += own_part[
                    own_at : own_at + BORDER
                ]
    gradient_slots(
        cur, acc, doubled, amplitudes, plan, Plan.CORNER, 0, plan[Plan.NUMBER, Plan.CORNER_END],
        (forth, back), SMALL,
    )
    store_bands(acc, 0, BORDER + tile, BORDER, to_up, to_down, to_left, to_right)


def second_rest_kernel(
    plan, cur, doubled, amplitudes, forth, back, acc_in,
    acc,
):
    gradient_slots(
        cur, acc, doubled, amplitudes, plan, Plan.SECOND,
        plan[Plan.NUMBER, Plan.SECOND_STOP], plan[Plan.NUMBER, Plan.REST_END],
        (forth, back),
    )


def store_bands(acc, top, bottom, count, to_up, to_down, to_left, to_right):
    ups = pack_row_band(acc, top, count), pack_row_band(acc, bottom, count)
    to_up[...], to_down[...] = by_side("row", *ups)
    sides = pack_side_bands(acc, to_left.shape[0])
    if count == BAND:
        sides = by_side("col", *sides)
    to_left[...], to_right[...] = sides


def middle_kernel(probe, acc, held, estimate, correction, estimated, corrected, sems):
    tile, width = held.shape[1:]
    rate = step_of(probe)
    rows, lanes = slice(BORDER, tile - BORDER), slice(LANES, width - LANES)
    for plane in range(2):
        corrected[plane] = rate * acc[plane, 2 * BORDER : tile, 2 * LANES : width]
        estimated[plane] = held[plane, rows, lanes] + corrected[plane]
    stores = [
        pltpu.make_async_copy(
            source,
            target.at[:, pl.ds(BORDER, tile - BAND), pl.ds(LANES, width - 2 * LANES)],
            sems.at[i],
        )
        for i, (source, target) in enumerate(((corrected, correction), (estimated, estimate)))
    ]
    for store in stores:
        store.start()
    for store in stores:
        store.wait()


def last_kernel(
    probe, up, down, left, right, acc, held, estimate_in, correction_in,
    estimate, correction, side_parts, row_parts, sems,
):
    tile, width = held.shape[1:]
    rate = step_of(probe)
    lane = lane_iota(tile)
    rows = slice(BORDER, BORDER + tile)
    lefts, rights = map(unfold_side, by_side("col", left[...], right[...]))
    up, down = by_side("row", up[...], down[...])
    stores = []

    def send(index, source, target):
        store = pltpu.make_async_copy(source, target, sems.at[index])
        store.start()
        stores.append(store)

    for side, (block, bands) in enumerate(((0, lefts), (width - LANES, rights))):
        keep = (lane < BORDER) if side == 0 else (lane >= LANES - BORDER)
        for plane in range(2):
            at = plane * width + block
            total = acc[plane, rows, LANES + block : 2 * LANES + block]
            total += jnp.where(keep, bands[plane], 0.0)
            total = jnp.concatenate(
                [
                    total[:BORDER] + up[:, at : at + LANES],
                    total[BORDER : tile - BORDER],
                    total[tile - BORDER :] + down[:, at : at + LANES],
                ],
                axis=0,
            )
            side_parts[0, side, plane] = rate * total
            side_parts[1, side, plane] = (
                held[plane, :, block : block + LANES] + side_parts[0, side, plane]
            )
        for number, target in enumerate((correction, estimate)):
            send(
                2 * side + number, side_parts.at[number, side],
                target.at[:, :, pl.ds(block, LANES)],
            )
    lanes = slice(LANES, width - LANES)
    for end, (row, band) in enumerate(((0, up), (tile - BORDER, down))):
        for plane in range(2):
            total = acc[plane, BORDER + row : 2 * BORDER + row, 2 * LANES : width]
            total += band[:, plane * width + LANES : (plane + 1) * width - LANES]
            row_parts[0, end, plane] = rate * total
            row_parts[1, end, plane] = (
                held[plane, row : row + BORDER, lanes] + row_parts[0, end, plane]
            )
        for number, target in enumerate((correction, estimate)):
            send(
                4 + 2 * end + number, row_parts.at[number, end],
                target.at[:, pl.ds(row, BORDER), pl.ds(LANES, width - 2 * LANES)],
            )
    for store in stores:
        store.wait()


VMEM = pl.BlockSpec(memory_space=pltpu.VMEM)
SMEM = pl.BlockSpec(memory_space=pltpu.SMEM)
HBM = pl.BlockSpec(memory_space=pltpu.HBM)
PARAMS = pltpu.CompilerParams(vmem_limit_bytes=32 * 1024 * 1024)


def f32(*shape):
    return pltpu.VMEM(shape, jnp.float32)


def in_hbm(array):
    return pltpu.with_memory_space_constraint(array, pltpu.HBM)


def in_smem(array):
    return pltpu.with_memory_space_constraint(array, pltpu.SMEM)


def in_vmem(array):
    return pltpu.with_memory_space_constraint(array, pltpu.VMEM)


def swap_pairs(axis, first, second):
    count = lax.axis_size(axis)

    def swap(array, begin):
        ends = [(i, i + 1) for i in range(begin, count - 1, 2)]
        return in_vmem(lax.ppermute(array, axis, ends + [(j, i) for i, j in ends]))

    first = swap(first, 0)
    second = swap(second, 1)
    return first, second


def on_device(object_field, probe_field, amplitudes, positions, counts):
    tile, width = object_field.shape[1:]
    probe = probe_field.shape[1]
    extent = tile + BAND
    padded = f32(2, extent + SUBLANES, width + 2 * LANES)
    doubled_shape = f32(2, 2 * probe, probe)
    tables = tuple(jnp.asarray(table) for table in dft_blocks(probe))
    places = positions[0, 0]
    plan_shape = pltpu.SMEM(Plan.shape(amplitudes.shape[0]), jnp.int32)
    sides = (f32(extent, LANES), f32(extent, LANES))

    def row_bands(count):
        band = f32(count, 2 * width + LANES)
        return (band, band)

    def call(kernel, scalars, arrays, outs, scratch=(), aliases=None):
        return pl.pallas_call(
            kernel,
            out_shape=outs,
            in_specs=[SMEM] * len(scalars) + [VMEM] * len(arrays),
            out_specs=jax.tree.map(lambda out: VMEM, outs),
            scratch_shapes=list(scratch),
            input_output_aliases=aliases or {},
            compiler_params=PARAMS,
        )(*scalars, *arrays)

    slots = (in_hbm(places), counts)
    strips = [
        jnp.concatenate([object_field[0, rows], object_field[1, rows]], axis=1)
        for rows in (slice(0, BORDER), slice(tile - BORDER, tile))
    ]
    table_shapes = tuple(pltpu.VMEM(table.shape, table.dtype) for table in tables)
    up, down = swap_pairs("row", *by_side("row", *strips))
    cur, acc, doubled, held, plan, *tables = pl.pallas_call(
        inner_start_kernel,
        out_shape=(
            padded, padded, doubled_shape, f32(*amplitudes.shape), plan_shape, *table_shapes,
        ),
        in_specs=[SMEM, SMEM] + [HBM] * (3 + len(tables)),
        out_specs=(VMEM,) * 4 + (SMEM,) + (VMEM,) * len(tables),
        scratch_shapes=[pltpu.SemaphoreType.DMA((7 + len(tables),))],
        compiler_params=PARAMS,
        name="inner_start",
    )(*slots, *map(in_hbm, (object_field, probe_field, amplitudes, *tables)))
    slots = (in_smem(plan),)
    to_left, to_right = call(
        object_pack_kernel, (), (cur, up, down),
        (f32(extent // 2, LANES),) * 2, (f32(extent, LANES),),
    )
    left, right = swap_pairs("col", to_left, to_right)
    cur, acc = call(
        side_kernel, slots, (up, down, doubled, held, *tables, cur, acc),
        (padded, padded), (), {7: 0, 8: 1},
    )
    cur, acc, to_up, to_down, to_left, to_right = call(
        outer_kernel, slots, (left, right, doubled, held, *tables, cur, acc),
        (padded, padded, *row_bands(BAND), *sides), (), {7: 0, 8: 1},
    )
    up, down = swap_pairs("row", to_up, to_down)
    left, right = swap_pairs("col", to_left, to_right)
    cur, acc, tile_held = pl.pallas_call(
        deep_kernel,
        out_shape=(padded, padded, f32(2, tile, width)),
        in_specs=[SMEM, HBM] + [VMEM] * 7,
        out_specs=(VMEM,) * 3,
        scratch_shapes=[pltpu.SemaphoreType.DMA(())],
        input_output_aliases={7: 0, 8: 1},
        compiler_params=PARAMS,
        name="deep",
    )(*slots, in_hbm(object_field), probe_field, doubled, held, *tables, cur, acc)
    corners = (f32(2 * BAND, LANES),) * 2
    left_corners, right_corners = swap_pairs("col", *call(corner_kernel, (), (up, down, acc), corners))
    grid = (lax.axis_size("row"), lax.axis_size("col"))
    cur, acc = call(
        functools.partial(second_kernel, *grid), slots,
        (probe_field, doubled, held, *tables, up, down, left, right, cur, acc),
        (padded, padded), (), {10: 0, 11: 1},
    )
    cur, acc, to_up, to_down, to_left, to_right = call(
        functools.partial(corner_slots_kernel, *grid), slots,
        (probe_field, doubled, held, *tables, left_corners, right_corners, cur, acc),
        (padded, padded, *row_bands(BORDER), *sides), (), {8: 0, 9: 1},
    )
    up, down = swap_pairs("row", to_up, to_down)
    acc = call(
        second_rest_kernel, slots, (cur, doubled, held, *tables, acc),
        padded, (), {6: 0},
    )
    folded = f32(tile // 2, LANES)
    to_left, to_right = call(
        last_corner_kernel, (), (up, down, to_left, to_right, acc),
        (folded, folded), (f32(tile, LANES),),
    )
    left, right = swap_pairs("col", to_left, to_right)
    result = jax.ShapeDtypeStruct((2, tile, width), jnp.float32)
    middle = f32(2, tile - BAND, width - 2 * LANES)
    estimate, correction = pl.pallas_call(
        middle_kernel,
        out_shape=(result, result),
        in_specs=[VMEM] * 3,
        out_specs=(HBM, HBM),
        scratch_shapes=[middle, middle, pltpu.SemaphoreType.DMA((2,))],
        compiler_params=PARAMS,
        name="middle",
    )(probe_field, acc, tile_held)
    estimate, correction = pl.pallas_call(
        last_kernel,
        out_shape=(result, result),
        in_specs=[VMEM] * 7 + [HBM] * 2,
        out_specs=(HBM, HBM),
        scratch_shapes=[
            f32(2, 2, 2, tile, LANES), f32(2, 2, 2, BORDER, width - 2 * LANES),
            pltpu.SemaphoreType.DMA((8,)),
        ],
        input_output_aliases={7: 0, 8: 1},
        compiler_params=PARAMS,
        name="finish",
    )(probe_field, up, down, left, right, acc, tile_held, estimate, correction)
    return estimate, correction


def solution(mesh):
    placed = (
        P(None, "row", "col"),
        P(),
        P("row", None, "col"),
        P("row", "col", None, None),
        P("row", "col"),
    )
    return jax.shard_map(
        on_device,
        mesh=mesh,
        in_specs=placed,
        out_specs=(P(None, "row", "col"), P(None, "row", "col")),
        check_vma=False,
    )
```

```python
import functools

import jax
import jax.numpy as jnp
import numpy as np
from jax import lax
from jax.experimental import pallas as pl
from jax.experimental.pallas import tpu as pltpu
from jax.sharding import PartitionSpec as P

BORDER = 32
BAND = 2 * BORDER
ITERS = 2
LANES = 128
SUBLANES = 8
LARGE, MIDDLE, SMALL = 8, 4, 2
RIGHT = 4

smoothing = 0.5
step_gain = 0.5


def split_host(table):
    high = table.astype(jnp.bfloat16)
    low = (table - high.astype(np.float64)).astype(jnp.bfloat16)
    return high, low


def dft_blocks(length):
    counter = np.arange(length)
    angles = 2.0 * np.pi * (np.outer(counter, counter) % length) / length
    real, imag = np.cos(angles) / np.sqrt(length), -np.sin(angles) / np.sqrt(length)
    blocks = []
    for sign in (1.0, -1.0):
        block = np.block([[real, sign * imag], [-sign * imag, real]])
        blocks.append(np.concatenate(split_host(block), axis=0))
    return blocks


def split(value):
    high = value.astype(jnp.bfloat16)
    low = (value - high.astype(jnp.float32)).astype(jnp.bfloat16)
    return high, low


def dot(left, right):
    return jnp.dot(left, right, preferred_element_type=jnp.float32)


def times_right(rows, block):
    high, low = split(rows)
    count = block.shape[0] // 2
    stacked = jnp.concatenate([block[:count], block], axis=0)
    return dot(jnp.concatenate([high, low, high], axis=1), stacked)


def right_groups(members, block):
    rows = members[0].shape[0]
    results = []
    count = min(RIGHT, len(members))
    for start in range(0, len(members), count):
        product = times_right(jnp.concatenate(members[start : start + count], axis=0), block[...])
        results += [product[i * rows : (i + 1) * rows] for i in range(count)]
    return results


def times_left(block, columns):
    high, low = split(columns)
    count = block.shape[0] // 2
    both = dot(block, high)
    return both[:count] + (both[count:] + dot(block[:count], low))


def lane_iota(rows):
    return lax.broadcasted_iota(jnp.int32, (rows, LANES), 1)


def edge_lanes(rows):
    lane = lane_iota(rows)
    return (lane < BORDER) | (lane >= LANES - BORDER)


def pack_planes(real, imag):
    return jnp.where(edge_lanes(real.shape[0]), real, pltpu.roll(imag, LANES // 2, 1))


def unpack_planes(packed):
    return packed, pltpu.roll(packed, LANES // 2, 1)


def slot_kinds(row, col, last):
    row_out, col_out = (row < 0) | (row > last), (col < 0) | (col > last)
    row_edge = (row < BORDER) | (row > last - BORDER)
    col_edge = (col < BORDER) | (col > last - BORDER)
    return row_out, col_out, row_edge, col_edge


def is_deep(row_out, col_out, row_edge, col_edge):
    return jnp.logical_not(row_edge | col_edge)


def is_beside(row_out, col_out, row_edge, col_edge):
    return col_out


def is_early(row_out, col_out, row_edge, col_edge):
    return (row_edge | col_edge) & jnp.logical_not(col_out)


def is_reaching(row_out, col_out, row_edge, col_edge):
    return (row_out | col_out) & jnp.logical_not(row_edge & col_edge)


def is_rim(row_out, col_out, row_edge, col_edge):
    return (row_edge ^ col_edge) & jnp.logical_not(row_out | col_out)


def is_reaching_corner(row_out, col_out, row_edge, col_edge):
    return (row_out | col_out) & row_edge & col_edge


def is_rim_corner(row_out, col_out, row_edge, col_edge):
    return row_edge & col_edge & jnp.logical_not(row_out | col_out)


class Plan:
    DEEP, SIDE, BESIDE, SECOND, CORNER, RIM, RIM_CORNER, ROW, COL, NUMBER = range(10)
    SIDE_STOP, BAND_BEGIN, BAND_END, SECOND_DEEP, BESIDE_END, SECOND_STOP, REST_END, CORNER_END = range(8)
    BAND_GROUPS = 3

    @staticmethod
    def shape(slot_total):
        return 10, max(slot_total + 1, 8)

    @staticmethod
    def fill(plan, positions, live, last):
        kinds = (
            (Plan.DEEP, is_deep), (Plan.SIDE, is_early), (Plan.BESIDE, is_beside),
            (Plan.SECOND, is_reaching), (Plan.RIM, is_rim), (Plan.RIM_CORNER, is_rim_corner),
            (Plan.CORNER, is_reaching_corner),
        )

        def visit(slot, found):
            row, col = positions[0, slot], positions[1, slot]
            plan[Plan.ROW, slot] = row
            plan[Plan.COL, slot] = col
            where = slot_kinds(row, col, last)
            counted = []
            for (listed, kind), number in zip(kinds, found):
                plan[listed, number] = slot
                counted.append(number + jnp.where(kind(*where), 1, 0))
            return tuple(counted)

        deep, early, beside, reaching, rim, rim_corner, corner = lax.fori_loop(
            0, live, visit, (0,) * len(kinds)
        )

        def extend(listed, begin, source, first, count):
            def move(index, carry):
                plan[listed, begin + index - first] = plan[source, index]
                return carry

            lax.fori_loop(first, count, move, 0)
            return begin + count - first

        side_stop = jnp.minimum(extend(Plan.SIDE, early, Plan.DEEP, 0, deep), round_up(early))
        done = side_stop - early
        room = (Plan.BAND_GROUPS - (deep - done + LARGE - 1) // LARGE) * LARGE
        second_deep = jnp.minimum(deep, jnp.maximum(room, 0))
        second_end = extend(Plan.SECOND, reaching, Plan.RIM, 0, rim)
        end = extend(Plan.SECOND, second_end, Plan.RIM_CORNER, 0, rim_corner)
        numbers = (
            side_stop, done, deep, second_deep, beside,
            jnp.minimum(second_end, round_up(reaching)),
            extend(Plan.SECOND, end, Plan.DEEP, second_deep, deep),
            corner,
        )
        for index, number in enumerate(numbers):
            plan[Plan.NUMBER, index] = number


def round_up(count):
    return jnp.maximum((count + LARGE - 1) // LARGE, 1) * LARGE


def gradient_slots(cur, acc, doubled, amplitudes, plan, listed, begin, stop, tables, size=LARGE):
    right_f, right_b = tables
    left_f, left_b = right_b, right_f
    probe = doubled.shape[1] // 2
    frame = probe + SUBLANES
    lane = lane_iota(frame)
    sub = lax.broadcasted_iota(jnp.int32, (SUBLANES, LANES), 0)

    def group_body(group, carry):
        places, probes, exits = [], [], []
        for member in range(size):
            slot = begin + group * size + member
            at = plan[listed, jnp.minimum(slot, stop - 1)]
            row = plan[Plan.ROW, at] + BORDER
            col = plan[Plan.COL, at] + LANES
            row_at = pl.multiple_of(row // SUBLANES * SUBLANES, SUBLANES)
            col_at = pl.multiple_of(col // LANES * LANES, LANES)
            row_off, col_off = row - row_at, col - col_at
            from_left = lane >= col_off
            from_top = sub >= row_off
            planes, rolled = [], []
            for plane in range(2):
                wide = jnp.where(
                    from_left,
                    cur[plane, pl.ds(row_at, frame), pl.ds(col_at, LANES)],
                    cur[plane, pl.ds(row_at, frame), pl.ds(col_at + LANES, LANES)],
                )
                first = jnp.where(from_top, wide[:SUBLANES], wide[probe:])
                planes.append(jnp.concatenate([first, wide[SUBLANES:probe]], axis=0))
                shifted = doubled[plane, pl.ds(probe - row_off, probe), :]
                rolled.append(pltpu.roll(shifted, col_off, 1))
            places.append((at, slot, row_at, col_at, from_left, from_top))
            probes.append(rolled)
            exits.append(
                jnp.concatenate(
                    [
                        rolled[0] * planes[0] - rolled[1] * planes[1],
                        rolled[0] * planes[1] + rolled[1] * planes[0],
                    ],
                    axis=1,
                )
            )
        half = right_groups(exits, right_f)
        shrunk = []
        for pair in range(0, size, 2):
            first, second = half[pair], half[pair + 1]
            stacked = jnp.concatenate(
                [
                    jnp.concatenate([first[:, :probe], second[:, :probe]], axis=1),
                    jnp.concatenate([first[:, probe:], second[:, probe:]], axis=1),
                ],
                axis=0,
            )
            wave = times_left(left_f[...], stacked)
            for member in range(2):
                at = places[pair + member][0]
                real = wave[:probe, member * probe : (member + 1) * probe]
                imag = wave[probe:, member * probe : (member + 1) * probe]
                shrink = amplitudes[at] * lax.rsqrt(real * real + imag * imag + smoothing) - 1.0
                shrunk.append(jnp.concatenate([real * shrink, imag * shrink], axis=1))
        half = right_groups(shrunk, right_b)
        for pair in range(0, size, 2):
            first, second = half[pair], half[pair + 1]
            stacked = jnp.concatenate(
                [
                    jnp.concatenate([first[:, :probe], second[:, :probe]], axis=1),
                    jnp.concatenate([first[:, probe:], second[:, probe:]], axis=1),
                ],
                axis=0,
            )
            back = times_left(left_b[...], stacked)
            for member in range(2):
                at, slot, row_at, col_at, from_left, from_top = places[pair + member]
                real = back[:probe, member * probe : (member + 1) * probe]
                imag = back[probe:, member * probe : (member + 1) * probe]
                rolled = probes[pair + member]
                grads = (
                    rolled[0] * real + rolled[1] * imag,
                    rolled[0] * imag - rolled[1] * real,
                )
                is_live = slot < stop
                keep_left = from_left & is_live
                keep_right = jnp.logical_not(from_left) & is_live
                for plane in range(2):
                    grad = grads[plane]
                    frame_grad = jnp.concatenate(
                        [
                            jnp.where(from_top, grad[:SUBLANES], 0.0),
                            grad[SUBLANES:],
                            jnp.where(from_top, 0.0, grad[:SUBLANES]),
                        ],
                        axis=0,
                    )
                    rows = pl.ds(row_at, frame)
                    acc[plane, rows, pl.ds(col_at, LANES)] += jnp.where(keep_left, frame_grad, 0.0)
                    acc[plane, rows, pl.ds(col_at + LANES, LANES)] += jnp.where(
                        keep_right, frame_grad, 0.0
                    )
        return carry

    lax.fori_loop(0, (stop - begin + size - 1) // size, group_body, 0)


def step_of(probe):
    return step_gain / (jnp.max(probe[0] * probe[0] + probe[1] * probe[1]) + 1e-06)


def pack_row_band(acc, row, count):
    rows = slice(row, row + count)
    width = acc.shape[2] - 2 * LANES
    is_low = lane_iota(count) < BORDER
    halo = [
        jnp.where(is_low, acc[plane, rows, LANES + width :], acc[plane, rows, :LANES])
        for plane in range(2)
    ]
    own = [acc[plane, rows, LANES : LANES + width] for plane in range(2)]
    return jnp.concatenate([*own, pack_planes(*halo)], axis=1)


def pack_side_bands(acc, height):
    width = acc.shape[2] - 2 * LANES
    is_low = lane_iota(height) < BORDER
    return [
        pack_planes(
            *[
                jnp.where(
                    is_low,
                    acc[plane, :height, block + LANES : block + 2 * LANES],
                    acc[plane, :height, block : block + LANES],
                )
                for plane in range(2)
            ]
        )
        for block in (0, width)
    ]


def start_kernel(
    positions, counts, objects, probe_in, amplitudes, *refs
):
    table_count = (len(refs) - 6) // 2
    tables_in, refs = refs[:table_count], refs[table_count:]
    cur, acc, doubled, held, plan = refs[:5]
    tables, sems = refs[5:-1], refs[-1]
    tile, width = objects.shape[1:]
    probe = probe_in.shape[1]
    sources = list(zip(tables_in, tables))
    for plane in range(2):
        sources.append(
            (
                objects.at[plane],
                cur.at[plane, pl.ds(BORDER, tile), pl.ds(LANES, width)],
            )
        )
        for row in (0, probe):
            sources.append((probe_in.at[plane], doubled.at[plane, pl.ds(row, probe), :]))
    sources.append((amplitudes, held))
    loads = [
        pltpu.make_async_copy(source, target, sems.at[i])
        for i, (source, target) in enumerate(sources)
    ]
    for load in loads:
        load.start()
    acc[...] = jnp.zeros_like(acc)
    Plan.fill(plan, positions, counts[0, 0], tile - probe)
    for load in loads:
        load.wait()


def side_kernel(
    plan, up, down, doubled, amplitudes, forth, back, cur_in, acc_in,
    cur, acc,
):
    tile, width = cur.shape[1] - SUBLANES - BAND, cur.shape[2] - 2 * LANES
    up, down = by_side("row", up[...], down[...])
    inner = slice(LANES, LANES + width)
    for plane in range(2):
        lanes = slice(plane * width, (plane + 1) * width)
        cur[plane, :BORDER, inner] = up[:, lanes]
        cur[plane, BORDER + tile : BAND + tile, inner] = down[:, lanes]
        cur[plane, BAND + tile :, :] = jnp.zeros_like(cur[plane, BAND + tile :, :])
    gradient_slots(
        cur, acc, doubled, amplitudes, plan, Plan.SIDE, 0, plan[Plan.NUMBER, Plan.SIDE_STOP],
        (forth, back),
    )


def fold_side(whole, is_low):
    half = whole.shape[0] // 2
    low = lane_iota(half) % (LANES // 2) < BORDER
    keep = low if is_low else jnp.logical_not(low)
    return jnp.where(keep, whole[:half, :], pltpu.roll(whole[half:, :], BORDER, 1))


def unfold_side(packed):
    return unpack_planes(
        jnp.concatenate([packed, pltpu.roll(packed, LANES - BORDER, 1)], axis=0)
    )


def by_side(axis, first, second):
    even = lax.axis_index(axis) % 2 == 0
    return jnp.where(even, second, first), jnp.where(even, first, second)


def object_pack_kernel(cur, up, down, to_left, to_right, whole):
    count = up.shape[0]
    width = up.shape[1] // 2
    extent = whole.shape[0]
    rows = slice(count, extent - count)
    up, down = by_side("row", up[...], down[...])
    parts = []
    for side in range(2):
        block = side * (width - LANES)
        for row, band in ((0, up), (extent - count, down)):
            whole[row : row + count, :] = pack_planes(
                *[
                    band[:, plane * width + block : plane * width + block + LANES]
                    for plane in range(2)
                ]
            )
        lanes = slice(LANES + block, 2 * LANES + block)
        whole[rows, :] = pack_planes(cur[0, rows, lanes], cur[1, rows, lanes])
        parts.append(fold_side(whole, side == 0))
    to_left[...], to_right[...] = by_side("col", *parts)


def outer_kernel(
    plan, left, right, doubled, amplitudes,
    forth, back, cur_in, acc_in,
    cur, acc, to_up, to_down, to_left, to_right,
):
    extent = 2 * left.shape[0]
    tile, width = extent - BAND, cur.shape[2] - 2 * LANES
    lane = lane_iota(extent)
    lefts, rights = map(unfold_side, by_side("col", left[...], right[...]))
    for plane in range(2):
        cur[plane, :extent, :LANES] = jnp.where(lane >= LANES - BORDER, lefts[plane], 0.0)
        cur[plane, :extent, LANES + width :] = jnp.where(lane < BORDER, rights[plane], 0.0)
    gradient_slots(
        cur, acc, doubled, amplitudes, plan, Plan.BESIDE, 0, plan[Plan.NUMBER, Plan.BESIDE_END],
        (forth, back), MIDDLE,
    )
    store_bands(acc, 0, tile, BAND, to_up, to_down, to_left, to_right)


def corner_parts(band, width):
    is_low = lane_iota(band.shape[0]) < BORDER
    halo = unpack_planes(band[:, 2 * width :])
    lefts, rights = [], []
    for plane in range(2):
        low = band[:, plane * width : plane * width + LANES]
        high = band[:, (plane + 1) * width - LANES : (plane + 1) * width]
        lefts.append(jnp.where(is_low, low, halo[plane]))
        rights.append(jnp.where(is_low, halo[plane], high))
    return pack_planes(*lefts), pack_planes(*rights)


def corner_kernel(up, down, after, to_left, to_right):
    count = up.shape[0]
    width = (up.shape[1] - LANES) // 2
    up, down = by_side("row", up[...], down[...])
    tops, bottoms = corner_parts(up, width), corner_parts(down, width)
    to_left[...], to_right[...] = by_side(
        "col", *(jnp.concatenate([tops[i], bottoms[i]], axis=0) for i in range(2))
    )


def last_corner_kernel(up, down, left, right, after, to_left, to_right, whole):
    count = up.shape[0]
    tile = left.shape[0] - BAND
    width = (up.shape[1] - LANES) // 2
    up, down = by_side("row", up[...], down[...])
    tops, bottoms = corner_parts(up, width), corner_parts(down, width)
    parts = []
    for side, source in enumerate((left, right)):
        whole[...] = source[BORDER : BORDER + tile, :]
        whole[:count, :] += tops[side]
        whole[tile - count :, :] += bottoms[side]
        parts.append(fold_side(whole, side == 1))
    to_left[...], to_right[...] = by_side("col", *parts)


def deep_kernel(
    plan, objects, probe, doubled, amplitudes, forth, back, cur_in, acc_in,
    cur, acc, tile_held, sem,
):
    load = pltpu.make_async_copy(objects, tile_held, sem)
    load.start()
    tile, width = cur.shape[1] - SUBLANES - BAND, cur.shape[2] - 2 * LANES
    rate = step_of(probe)
    middle, inner = slice(BORDER, BORDER + tile), slice(LANES, LANES + width)
    begins = (plan[Plan.NUMBER, Plan.BAND_BEGIN], 0)
    ends = (plan[Plan.NUMBER, Plan.BAND_END], plan[Plan.NUMBER, Plan.SECOND_DEEP])

    def turn(iteration, carry):
        @pl.when(iteration == 1)
        def update():
            for plane in range(2):
                cur[plane, middle, inner] += rate * acc[plane, middle, inner]

        gradient_slots(
            cur, acc, doubled, amplitudes, plan, Plan.DEEP,
            jnp.where(iteration == 0, *begins), jnp.where(iteration == 0, *ends),
            (forth, back),
        )
        return carry

    lax.fori_loop(0, ITERS, turn, 0)
    load.wait()


def grid_gains(row_count, col_count, tile, rate):
    row_at, col_at = lax.axis_index("row"), lax.axis_index("col")
    top = jnp.where(row_at > 0, 1.0, 0.0)
    bottom = jnp.where(row_at < row_count - 1, 1.0, 0.0)
    before = jnp.where(col_at > 0, 1.0, 0.0)
    after = jnp.where(col_at < col_count - 1, 1.0, 0.0)
    row_id = lax.broadcasted_iota(jnp.int32, (tile + BAND, LANES), 0)
    row_gain = rate * jnp.where(
        row_id < BORDER, top, jnp.where(row_id >= BORDER + tile, bottom, 1.0)
    )
    return row_gain, top, bottom, before, after


def second_kernel(
    row_count, col_count,
    plan, probe, doubled, amplitudes, forth, back,
    up, down, left, right, cur_in, acc_in,
    cur, acc,
):
    tile, width = cur.shape[1] - SUBLANES - BAND, cur.shape[2] - 2 * LANES
    extent = tile + BAND
    rate = step_of(probe)
    row_gain, top, bottom, before, after = grid_gains(row_count, col_count, tile, rate)
    inner = slice(LANES, LANES + width)
    lane = lane_iota(extent)
    is_low, is_high = lane < BORDER, lane >= LANES - BORDER
    lefts, rights = map(unpack_planes, by_side("col", left[...], right[...]))
    up, down = by_side("row", up[...], down[...])
    for plane in range(2):
        for row, band, on_grid in ((0, up, top), (tile, down, bottom)):
            halo_first = row == 0
            values = band[:, plane * width : (plane + 1) * width]
            own, out = (BORDER, 0) if halo_first else (0, BORDER)
            own_rows = slice(row + own, row + own + BORDER)
            out_rows = slice(row + out, row + out + BORDER)
            cur[plane, own_rows, inner] += rate * values[own : own + BORDER]
            acc[plane, own_rows, inner] += values[own : own + BORDER]
            cur[plane, out_rows, inner] += (rate * on_grid) * (
                acc[plane, out_rows, inner] + values[out : out + BORDER]
            )
            acc[plane, out_rows, inner] = jnp.zeros_like(acc[plane, out_rows, inner])
            halo = unpack_planes(band[:, 2 * width :])[plane]
            for lanes, keep in (
                (slice(0, LANES), is_high[:BAND]),
                (slice(LANES + width, None), is_low[:BAND]),
            ):
                acc[plane, row : row + BAND, lanes] += jnp.where(keep, halo, 0.0)
        for block, band, on_grid, own_first in (
            (0, lefts[plane], before, False),
            (width, rights[plane], after, True),
        ):
            low_block = slice(block, block + LANES)
            high_block = slice(block + LANES, block + 2 * LANES)
            own, out = (low_block, high_block) if own_first else (high_block, low_block)
            keep_own, keep_out = (is_high, is_low) if own_first else (is_low, is_high)
            own_band = jnp.where(keep_own, band, 0.0)
            cur[plane, :extent, own] += row_gain * own_band
            acc[plane, BORDER : BORDER + tile, own] += own_band[BORDER : BORDER + tile]
            cur[plane, :extent, out] += (row_gain * on_grid) * (
                acc[plane, :extent, out] + jnp.where(keep_out, band, 0.0)
            )
            acc[plane, :extent, out] = jnp.zeros_like(acc[plane, :extent, out])
    gradient_slots(
        cur, acc, doubled, amplitudes, plan, Plan.SECOND, 0, plan[Plan.NUMBER, Plan.SECOND_STOP],
        (forth, back),
    )


def corner_slots_kernel(
    row_count, col_count,
    plan, probe, doubled, amplitudes, forth, back,
    left, right, cur_in, acc_in,
    cur, acc, to_up, to_down, to_left, to_right,
):
    tile, width = cur.shape[1] - SUBLANES - BAND, cur.shape[2] - 2 * LANES
    row_gain, _, _, before, after = grid_gains(row_count, col_count, tile, step_of(probe))
    lane = lane_iota(BAND)
    is_low, is_high = lane < BORDER, lane >= LANES - BORDER
    left, right = by_side("col", left[...], right[...])
    for block, corners, on_grid, own_first in (
        (0, left, before, False), (width, right, after, True),
    ):
        low_block = slice(block, block + LANES)
        high_block = slice(block + LANES, block + 2 * LANES)
        own, out = (low_block, high_block) if own_first else (high_block, low_block)
        keep_own, keep_out = (is_high, is_low) if own_first else (is_low, is_high)
        both = unpack_planes(corners)
        for plane in range(2):
            for row, own_at in ((0, BORDER), (tile, 0)):
                rows = slice(row, row + BAND)
                part = both[plane][:BAND] if row == 0 else both[plane][BAND:]
                own_part = jnp.where(keep_own, part, 0.0)
                gain = row_gain[rows]
                cur[plane, rows, own] += gain * own_part
                cur[plane, rows, out] += (gain * on_grid) * jnp.where(keep_out, part, 0.0)
                acc[plane, row + own_at : row + own_at + BORDER, own] += own_part[
                    own_at : own_at + BORDER
                ]
    gradient_slots(
        cur, acc, doubled, amplitudes, plan, Plan.CORNER, 0, plan[Plan.NUMBER, Plan.CORNER_END],
        (forth, back), SMALL,
    )
    store_bands(acc, 0, BORDER + tile, BORDER, to_up, to_down, to_left, to_right)


def second_rest_kernel(
    plan, cur, doubled, amplitudes, forth, back, acc_in,
    acc,
):
    gradient_slots(
        cur, acc, doubled, amplitudes, plan, Plan.SECOND,
        plan[Plan.NUMBER, Plan.SECOND_STOP], plan[Plan.NUMBER, Plan.REST_END],
        (forth, back),
    )


def store_bands(acc, top, bottom, count, to_up, to_down, to_left, to_right):
    ups = pack_row_band(acc, top, count), pack_row_band(acc, bottom, count)
    to_up[...], to_down[...] = by_side("row", *ups)
    sides = pack_side_bands(acc, to_left.shape[0])
    if count == BAND:
        sides = by_side("col", *sides)
    to_left[...], to_right[...] = sides


def middle_kernel(
    probe, up, down, acc, held, estimate, correction, estimated, corrected, sems,
):
    tile, width = held.shape[1:]
    rate = step_of(probe)
    lanes = slice(LANES, width - LANES)
    up, down = by_side("row", up[...], down[...])
    for plane in range(2):
        total = acc[plane, BORDER : BORDER + tile, 2 * LANES : width]
        at = slice(plane * width + LANES, (plane + 1) * width - LANES)
        corrected[plane] = rate * jnp.concatenate(
            [
                total[:BORDER] + up[:, at],
                total[BORDER : tile - BORDER],
                total[tile - BORDER :] + down[:, at],
            ],
            axis=0,
        )
        estimated[plane] = held[plane, :, lanes] + corrected[plane]
    stores = [
        pltpu.make_async_copy(
            source, target.at[:, :, pl.ds(LANES, width - 2 * LANES)], sems.at[i]
        )
        for i, (source, target) in enumerate(((corrected, correction), (estimated, estimate)))
    ]
    for store in stores:
        store.start()
    for store in stores:
        store.wait()


def last_kernel(
    probe, up, down, left, right, acc, held, estimate_in, correction_in,
    estimate, correction, parts, sems,
):
    tile, width = held.shape[1:]
    rate = step_of(probe)
    lane = lane_iota(tile)
    rows = slice(BORDER, BORDER + tile)
    lefts, rights = map(unfold_side, by_side("col", left[...], right[...]))
    up, down = by_side("row", up[...], down[...])
    stores = []
    for side, (block, bands) in enumerate(((0, lefts), (width - LANES, rights))):
        keep = (lane < BORDER) if side == 0 else (lane >= LANES - BORDER)
        for plane in range(2):
            at = plane * width + block
            total = acc[plane, rows, LANES + block : 2 * LANES + block]
            total += jnp.where(keep, bands[plane], 0.0)
            total = jnp.concatenate(
                [
                    total[:BORDER] + up[:, at : at + LANES],
                    total[BORDER : tile - BORDER],
                    total[tile - BORDER :] + down[:, at : at + LANES],
                ],
                axis=0,
            )
            parts[0, side, plane] = rate * total
            parts[1, side, plane] = held[plane, :, block : block + LANES] + parts[0, side, plane]
            for number, target in enumerate((correction, estimate)):
                store = pltpu.make_async_copy(
                    parts.at[number, side, plane],
                    target.at[plane, :, pl.ds(block, LANES)],
                    sems.at[side, plane, number],
                )
                store.start()
                stores.append(store)
    for store in stores:
        store.wait()


VMEM = pl.BlockSpec(memory_space=pltpu.VMEM)
SMEM = pl.BlockSpec(memory_space=pltpu.SMEM)
HBM = pl.BlockSpec(memory_space=pltpu.HBM)
PARAMS = pltpu.CompilerParams(vmem_limit_bytes=32 * 1024 * 1024)


def f32(*shape):
    return pltpu.VMEM(shape, jnp.float32)


def in_hbm(array):
    return pltpu.with_memory_space_constraint(array, pltpu.HBM)


def in_smem(array):
    return pltpu.with_memory_space_constraint(array, pltpu.SMEM)


def in_vmem(array):
    return pltpu.with_memory_space_constraint(array, pltpu.VMEM)


def swap_pairs(axis, first, second):
    count = lax.axis_size(axis)

    def swap(array, begin):
        ends = [(i, i + 1) for i in range(begin, count - 1, 2)]
        return in_vmem(lax.ppermute(array, axis, ends + [(j, i) for i, j in ends]))

    first = swap(first, 0)
    second = swap(second, 1)
    return first, second


def on_device(object_field, probe_field, amplitudes, positions, counts):
    tile, width = object_field.shape[1:]
    probe = probe_field.shape[1]
    extent = tile + BAND
    padded = f32(2, extent + SUBLANES, width + 2 * LANES)
    doubled_shape = f32(2, 2 * probe, probe)
    tables = tuple(jnp.asarray(table) for table in dft_blocks(probe))
    places = positions[0, 0]
    plan_shape = pltpu.SMEM(Plan.shape(amplitudes.shape[0]), jnp.int32)
    sides = (f32(extent, LANES), f32(extent, LANES))

    def row_bands(count):
        band = f32(count, 2 * width + LANES)
        return (band, band)

    def call(kernel, scalars, arrays, outs, scratch=(), aliases=None):
        return pl.pallas_call(
            kernel,
            out_shape=outs,
            in_specs=[SMEM] * len(scalars) + [VMEM] * len(arrays),
            out_specs=jax.tree.map(lambda out: VMEM, outs),
            scratch_shapes=list(scratch),
            input_output_aliases=aliases or {},
            compiler_params=PARAMS,
        )(*scalars, *arrays)

    slots = (in_hbm(places), counts)
    strips = [
        jnp.concatenate([object_field[0, rows], object_field[1, rows]], axis=1)
        for rows in (slice(0, BORDER), slice(tile - BORDER, tile))
    ]
    table_shapes = tuple(pltpu.VMEM(table.shape, table.dtype) for table in tables)
    up, down = swap_pairs("row", *by_side("row", *strips))
    cur, acc, doubled, held, plan, *tables = pl.pallas_call(
        start_kernel,
        out_shape=(
            padded, padded, doubled_shape, f32(*amplitudes.shape), plan_shape, *table_shapes,
        ),
        in_specs=[SMEM, SMEM] + [HBM] * (3 + len(tables)),
        out_specs=(VMEM,) * 4 + (SMEM,) + (VMEM,) * len(tables),
        scratch_shapes=[pltpu.SemaphoreType.DMA((7 + len(tables),))],
        compiler_params=PARAMS,
        name="start",
    )(*slots, *map(in_hbm, (object_field, probe_field, amplitudes, *tables)))
    slots = (in_smem(plan),)
    to_left, to_right = call(
        object_pack_kernel, (), (cur, up, down),
        (f32(extent // 2, LANES),) * 2, (f32(extent, LANES),),
    )
    left, right = swap_pairs("col", to_left, to_right)
    cur, acc = call(
        side_kernel, slots, (up, down, doubled, held, *tables, cur, acc),
        (padded, padded), (), {7: 0, 8: 1},
    )
    cur, acc, to_up, to_down, to_left, to_right = call(
        outer_kernel, slots, (left, right, doubled, held, *tables, cur, acc),
        (padded, padded, *row_bands(BAND), *sides), (), {7: 0, 8: 1},
    )
    up, down = swap_pairs("row", to_up, to_down)
    left, right = swap_pairs("col", to_left, to_right)
    cur, acc, tile_held = pl.pallas_call(
        deep_kernel,
        out_shape=(padded, padded, f32(2, tile, width)),
        in_specs=[SMEM, HBM] + [VMEM] * 7,
        out_specs=(VMEM,) * 3,
        scratch_shapes=[pltpu.SemaphoreType.DMA(())],
        input_output_aliases={7: 0, 8: 1},
        compiler_params=PARAMS,
        name="deep",
    )(*slots, in_hbm(object_field), probe_field, doubled, held, *tables, cur, acc)
    corners = (f32(2 * BAND, LANES),) * 2
    left_corners, right_corners = swap_pairs("col", *call(corner_kernel, (), (up, down, acc), corners))
    grid = (lax.axis_size("row"), lax.axis_size("col"))
    cur, acc = call(
        functools.partial(second_kernel, *grid), slots,
        (probe_field, doubled, held, *tables, up, down, left, right, cur, acc),
        (padded, padded), (), {10: 0, 11: 1},
    )
    cur, acc, to_up, to_down, to_left, to_right = call(
        functools.partial(corner_slots_kernel, *grid), slots,
        (probe_field, doubled, held, *tables, left_corners, right_corners, cur, acc),
        (padded, padded, *row_bands(BORDER), *sides), (), {8: 0, 9: 1},
    )
    up, down = swap_pairs("row", to_up, to_down)
    acc = call(
        second_rest_kernel, slots, (cur, doubled, held, *tables, acc),
        padded, (), {6: 0},
    )
    folded = f32(tile // 2, LANES)
    to_left, to_right = call(
        last_corner_kernel, (), (up, down, to_left, to_right, acc),
        (folded, folded), (f32(tile, LANES),),
    )
    left, right = swap_pairs("col", to_left, to_right)
    result = jax.ShapeDtypeStruct((2, tile, width), jnp.float32)
    middle = f32(2, tile, width - 2 * LANES)
    estimate, correction = pl.pallas_call(
        middle_kernel,
        out_shape=(result, result),
        in_specs=[VMEM] * 5,
        out_specs=(HBM, HBM),
        scratch_shapes=[middle, middle, pltpu.SemaphoreType.DMA((2,))],
        compiler_params=PARAMS,
        name="middle",
    )(probe_field, up, down, acc, tile_held)
    estimate, correction = pl.pallas_call(
        last_kernel,
        out_shape=(result, result),
        in_specs=[VMEM] * 7 + [HBM] * 2,
        out_specs=(HBM, HBM),
        scratch_shapes=[
            f32(2, 2, 2, tile, LANES), pltpu.SemaphoreType.DMA((2, 2, 2)),
        ],
        input_output_aliases={7: 0, 8: 1},
        compiler_params=PARAMS,
        name="finish",
    )(probe_field, up, down, left, right, acc, tile_held, estimate, correction)
    return estimate, correction


def solution(mesh):
    placed = (
        P(None, "row", "col"),
        P(),
        P("row", None, "col"),
        P("row", "col", None, None),
        P("row", "col"),
    )
    return jax.shard_map(
        on_device,
        mesh=mesh,
        in_specs=placed,
        out_specs=(P(None, "row", "col"), P(None, "row", "col")),
        check_vma=False,
    )
```

```python
import functools

import jax
import jax.numpy as jnp
import numpy as np
from jax import lax
from jax.experimental import pallas as pl
from jax.experimental.pallas import tpu as pltpu
from jax.sharding import PartitionSpec as P

BORDER = 32
BAND = 2 * BORDER
ITERS = 2
LANES = 128
SUBLANES = 8
LARGE, MIDDLE, SMALL = 8, 4, 2
RIGHT = 4

smoothing = 0.5
step_gain = 0.5


def split_host(table):
    high = table.astype(jnp.bfloat16)
    low = (table - high.astype(np.float64)).astype(jnp.bfloat16)
    return high, low


def dft_blocks(length):
    counter = np.arange(length)
    angles = 2.0 * np.pi * (np.outer(counter, counter) % length) / length
    real, imag = np.cos(angles) / np.sqrt(length), -np.sin(angles) / np.sqrt(length)
    blocks = []
    for sign in (1.0, -1.0):
        block = np.block([[real, sign * imag], [-sign * imag, real]])
        blocks.append(np.concatenate(split_host(block), axis=0))
    return blocks


def split(value):
    high = value.astype(jnp.bfloat16)
    low = (value - high.astype(jnp.float32)).astype(jnp.bfloat16)
    return high, low


def dot(left, right):
    return jnp.dot(left, right, preferred_element_type=jnp.float32)


def times_right(rows, block):
    high, low = split(rows)
    count = block.shape[0] // 2
    stacked = jnp.concatenate([block[:count], block], axis=0)
    return dot(jnp.concatenate([high, low, high], axis=1), stacked)


def right_groups(members, block):
    rows = members[0].shape[0]
    results = []
    count = min(RIGHT, len(members))
    for start in range(0, len(members), count):
        product = times_right(jnp.concatenate(members[start : start + count], axis=0), block[...])
        results += [product[i * rows : (i + 1) * rows] for i in range(count)]
    return results


def times_left(block, columns):
    high, low = split(columns)
    count = block.shape[0] // 2
    both = dot(block, high)
    return both[:count] + (both[count:] + dot(block[:count], low))


def lane_iota(rows):
    return lax.broadcasted_iota(jnp.int32, (rows, LANES), 1)


def edge_lanes(rows):
    lane = lane_iota(rows)
    return (lane < BORDER) | (lane >= LANES - BORDER)


def pack_planes(real, imag):
    return jnp.where(edge_lanes(real.shape[0]), real, pltpu.roll(imag, LANES // 2, 1))


def unpack_planes(packed):
    return packed, pltpu.roll(packed, LANES // 2, 1)


def slot_kinds(row, col, last):
    row_out, col_out = (row < 0) | (row > last), (col < 0) | (col > last)
    row_edge = (row < BORDER) | (row > last - BORDER)
    col_edge = (col < BORDER) | (col > last - BORDER)
    return row_out, col_out, row_edge, col_edge


def is_deep(row_out, col_out, row_edge, col_edge):
    return jnp.logical_not(row_edge | col_edge)


def is_beside(row_out, col_out, row_edge, col_edge):
    return col_out & jnp.logical_not(row_edge)


def is_beside_edge(row_out, col_out, row_edge, col_edge):
    return col_out & row_edge


def is_early(row_out, col_out, row_edge, col_edge):
    return (row_edge | col_edge) & jnp.logical_not(col_out)


def is_reaching(row_out, col_out, row_edge, col_edge):
    return (row_out | col_out) & jnp.logical_not(row_edge & col_edge)


def is_rim(row_out, col_out, row_edge, col_edge):
    return (row_edge ^ col_edge) & jnp.logical_not(row_out | col_out)


def is_reaching_corner(row_out, col_out, row_edge, col_edge):
    return (row_out | col_out) & row_edge & col_edge


def is_rim_corner(row_out, col_out, row_edge, col_edge):
    return row_edge & col_edge & jnp.logical_not(row_out | col_out)


class Plan:
    DEEP, SIDE, BESIDE, SECOND, CORNER, RIM, RIM_CORNER, BESIDE_EDGE, ROW, COL, NUMBER = range(11)
    SIDE_STOP, BAND_BEGIN, BAND_END, SECOND_DEEP, BESIDE_END, SECOND_STOP, REST_END, CORNER_END, BESIDE_EDGE_END = range(9)
    BAND_GROUPS = 2

    @staticmethod
    def shape(slot_total):
        return 11, max(slot_total + 1, 9)

    @staticmethod
    def fill(plan, positions, live, last):
        kinds = (
            (Plan.DEEP, is_deep), (Plan.SIDE, is_early), (Plan.BESIDE, is_beside),
            (Plan.SECOND, is_reaching), (Plan.RIM, is_rim), (Plan.RIM_CORNER, is_rim_corner),
            (Plan.CORNER, is_reaching_corner), (Plan.BESIDE_EDGE, is_beside_edge),
        )

        def visit(slot, found):
            row, col = positions[0, slot], positions[1, slot]
            plan[Plan.ROW, slot] = row
            plan[Plan.COL, slot] = col
            where = slot_kinds(row, col, last)
            counted = []
            for (listed, kind), number in zip(kinds, found):
                plan[listed, number] = slot
                counted.append(number + jnp.where(kind(*where), 1, 0))
            return tuple(counted)

        deep, early, beside, reaching, rim, rim_corner, corner, beside_edge = lax.fori_loop(
            0, live, visit, (0,) * len(kinds)
        )

        def extend(listed, begin, source, first, count):
            def move(index, carry):
                plan[listed, begin + index - first] = plan[source, index]
                return carry

            lax.fori_loop(first, count, move, 0)
            return begin + count - first

        side_stop = jnp.minimum(extend(Plan.SIDE, early, Plan.DEEP, 0, deep), round_up(early))
        done = side_stop - early
        room = (Plan.BAND_GROUPS - (deep - done + LARGE - 1) // LARGE) * LARGE
        second_deep = jnp.minimum(deep, jnp.maximum(room, 0))
        second_end = extend(Plan.SECOND, reaching, Plan.RIM, 0, rim)
        end = extend(Plan.SECOND, second_end, Plan.RIM_CORNER, 0, rim_corner)
        numbers = (
            side_stop, done, deep, second_deep, beside,
            jnp.minimum(second_end, round_up(reaching)),
            extend(Plan.SECOND, end, Plan.DEEP, second_deep, deep),
            corner, beside_edge,
        )
        for index, number in enumerate(numbers):
            plan[Plan.NUMBER, index] = number


def round_up(count):
    return jnp.maximum((count + LARGE - 1) // LARGE, 1) * LARGE


def gradient_slots(cur, acc, doubled, amplitudes, plan, listed, begin, stop, tables, size=LARGE):
    right_f, right_b = tables
    left_f, left_b = right_b, right_f
    probe = doubled.shape[1] // 2
    frame = probe + SUBLANES
    lane = lane_iota(frame)
    sub = lax.broadcasted_iota(jnp.int32, (SUBLANES, LANES), 0)

    def group_body(group, carry):
        places, probes, exits = [], [], []
        for member in range(size):
            slot = begin + group * size + member
            at = plan[listed, jnp.minimum(slot, stop - 1)]
            row = plan[Plan.ROW, at] + BORDER
            col = plan[Plan.COL, at] + LANES
            row_at = pl.multiple_of(row // SUBLANES * SUBLANES, SUBLANES)
            col_at = pl.multiple_of(col // LANES * LANES, LANES)
            row_off, col_off = row - row_at, col - col_at
            from_left = lane >= col_off
            from_top = sub >= row_off
            planes, rolled = [], []
            for plane in range(2):
                wide = jnp.where(
                    from_left,
                    cur[plane, pl.ds(row_at, frame), pl.ds(col_at, LANES)],
                    cur[plane, pl.ds(row_at, frame), pl.ds(col_at + LANES, LANES)],
                )
                first = jnp.where(from_top, wide[:SUBLANES], wide[probe:])
                planes.append(jnp.concatenate([first, wide[SUBLANES:probe]], axis=0))
                shifted = doubled[plane, pl.ds(probe - row_off, probe), :]
                rolled.append(pltpu.roll(shifted, col_off, 1))
            places.append((at, slot, row_at, col_at, from_left, from_top))
            probes.append(rolled)
            exits.append(
                jnp.concatenate(
                    [
                        rolled[0] * planes[0] - rolled[1] * planes[1],
                        rolled[0] * planes[1] + rolled[1] * planes[0],
                    ],
                    axis=1,
                )
            )
        half = right_groups(exits, right_f)
        shrunk = []
        for pair in range(0, size, 2):
            first, second = half[pair], half[pair + 1]
            stacked = jnp.concatenate(
                [
                    jnp.concatenate([first[:, :probe], second[:, :probe]], axis=1),
                    jnp.concatenate([first[:, probe:], second[:, probe:]], axis=1),
                ],
                axis=0,
            )
            wave = times_left(left_f[...], stacked)
            for member in range(2):
                at = places[pair + member][0]
                real = wave[:probe, member * probe : (member + 1) * probe]
                imag = wave[probe:, member * probe : (member + 1) * probe]
                shrink = amplitudes[at] * lax.rsqrt(real * real + imag * imag + smoothing) - 1.0
                shrunk.append(jnp.concatenate([real * shrink, imag * shrink], axis=1))
        half = right_groups(shrunk, right_b)
        for pair in range(0, size, 2):
            first, second = half[pair], half[pair + 1]
            stacked = jnp.concatenate(
                [
                    jnp.concatenate([first[:, :probe], second[:, :probe]], axis=1),
                    jnp.concatenate([first[:, probe:], second[:, probe:]], axis=1),
                ],
                axis=0,
            )
            back = times_left(left_b[...], stacked)
            for member in range(2):
                at, slot, row_at, col_at, from_left, from_top = places[pair + member]
                real = back[:probe, member * probe : (member + 1) * probe]
                imag = back[probe:, member * probe : (member + 1) * probe]
                rolled = probes[pair + member]
                grads = (
                    rolled[0] * real + rolled[1] * imag,
                    rolled[0] * imag - rolled[1] * real,
                )
                is_live = slot < stop
                keep_left = from_left & is_live
                keep_right = jnp.logical_not(from_left) & is_live
                for plane in range(2):
                    grad = grads[plane]
                    frame_grad = jnp.concatenate(
                        [
                            jnp.where(from_top, grad[:SUBLANES], 0.0),
                            grad[SUBLANES:],
                            jnp.where(from_top, 0.0, grad[:SUBLANES]),
                        ],
                        axis=0,
                    )
                    rows = pl.ds(row_at, frame)
                    acc[plane, rows, pl.ds(col_at, LANES)] += jnp.where(keep_left, frame_grad, 0.0)
                    acc[plane, rows, pl.ds(col_at + LANES, LANES)] += jnp.where(
                        keep_right, frame_grad, 0.0
                    )
        return carry

    lax.fori_loop(0, (stop - begin + size - 1) // size, group_body, 0)


def few_slots(cur, acc, doubled, amplitudes, plan, listed, stop, tables):
    whole = jnp.minimum((stop + 1) // MIDDLE * MIDDLE, stop)
    gradient_slots(cur, acc, doubled, amplitudes, plan, listed, 0, whole, tables, MIDDLE)
    gradient_slots(cur, acc, doubled, amplitudes, plan, listed, whole, stop, tables, SMALL)


def step_of(probe):
    return step_gain / (jnp.max(probe[0] * probe[0] + probe[1] * probe[1]) + 1e-06)


def pack_row_band(acc, row, count):
    rows = slice(row, row + count)
    width = acc.shape[2] - 2 * LANES
    is_low = lane_iota(count) < BORDER
    halo = [
        jnp.where(is_low, acc[plane, rows, LANES + width :], acc[plane, rows, :LANES])
        for plane in range(2)
    ]
    own = [acc[plane, rows, LANES : LANES + width] for plane in range(2)]
    return jnp.concatenate([*own, pack_planes(*halo)], axis=1)


def pack_side_bands(acc, height):
    width = acc.shape[2] - 2 * LANES
    is_low = lane_iota(height) < BORDER
    return [
        pack_planes(
            *[
                jnp.where(
                    is_low,
                    acc[plane, :height, block + LANES : block + 2 * LANES],
                    acc[plane, :height, block : block + LANES],
                )
                for plane in range(2)
            ]
        )
        for block in (0, width)
    ]


def start_kernel(
    positions, counts, objects, probe_in, amplitudes, *refs
):
    table_count = (len(refs) - 6) // 2
    tables_in, refs = refs[:table_count], refs[table_count:]
    cur, acc, doubled, held, plan = refs[:5]
    tables, sems = refs[5:-1], refs[-1]
    tile, width = objects.shape[1:]
    probe = probe_in.shape[1]
    sources = list(zip(tables_in, tables))
    for plane in range(2):
        sources.append(
            (
                objects.at[plane],
                cur.at[plane, pl.ds(BORDER, tile), pl.ds(LANES, width)],
            )
        )
        for row in (0, probe):
            sources.append((probe_in.at[plane], doubled.at[plane, pl.ds(row, probe), :]))
    sources.append((amplitudes, held))
    loads = [
        pltpu.make_async_copy(source, target, sems.at[i])
        for i, (source, target) in enumerate(sources)
    ]
    for load in loads:
        load.start()
    acc[...] = jnp.zeros_like(acc)
    Plan.fill(plan, positions, counts[0, 0], tile - probe)
    for load in loads:
        load.wait()


def side_kernel(
    plan, up, down, doubled, amplitudes, forth, back, cur_in, acc_in,
    cur, acc,
):
    tile, width = cur.shape[1] - SUBLANES - BAND, cur.shape[2] - 2 * LANES
    up, down = by_side("row", up[...], down[...])
    inner = slice(LANES, LANES + width)
    for plane in range(2):
        lanes = slice(plane * width, (plane + 1) * width)
        cur[plane, :BORDER, inner] = up[:, lanes]
        cur[plane, BORDER + tile : BAND + tile, inner] = down[:, lanes]
        cur[plane, BAND + tile :, :] = jnp.zeros_like(cur[plane, BAND + tile :, :])
    gradient_slots(
        cur, acc, doubled, amplitudes, plan, Plan.SIDE, 0, plan[Plan.NUMBER, Plan.SIDE_STOP],
        (forth, back),
    )


def fold_side(whole, is_low):
    half = whole.shape[0] // 2
    low = lane_iota(half) % (LANES // 2) < BORDER
    keep = low if is_low else jnp.logical_not(low)
    return jnp.where(keep, whole[:half, :], pltpu.roll(whole[half:, :], BORDER, 1))


def unfold_side(packed):
    return unpack_planes(
        jnp.concatenate([packed, pltpu.roll(packed, LANES - BORDER, 1)], axis=0)
    )


def by_side(axis, first, second):
    even = lax.axis_index(axis) % 2 == 0
    return jnp.where(even, second, first), jnp.where(even, first, second)


def object_pack_kernel(cur, up, down, to_left, to_right, whole):
    count = up.shape[0]
    width = up.shape[1] // 2
    extent = whole.shape[0]
    rows = slice(count, extent - count)
    up, down = by_side("row", up[...], down[...])
    parts = []
    for side in range(2):
        block = side * (width - LANES)
        for row, band in ((0, up), (extent - count, down)):
            whole[row : row + count, :] = pack_planes(
                *[
                    band[:, plane * width + block : plane * width + block + LANES]
                    for plane in range(2)
                ]
            )
        lanes = slice(LANES + block, 2 * LANES + block)
        whole[rows, :] = pack_planes(cur[0, rows, lanes], cur[1, rows, lanes])
        parts.append(fold_side(whole, side == 0))
    to_left[...], to_right[...] = by_side("col", *parts)


def outer_kernel(
    plan, left, right, doubled, amplitudes, forth, back, cur_in, acc_in,
    cur, acc, to_up, to_down,
):
    extent = 2 * left.shape[0]
    tile, width = extent - BAND, cur.shape[2] - 2 * LANES
    lane = lane_iota(extent)
    lefts, rights = map(unfold_side, by_side("col", left[...], right[...]))
    for plane in range(2):
        cur[plane, :extent, :LANES] = jnp.where(lane >= LANES - BORDER, lefts[plane], 0.0)
        cur[plane, :extent, LANES + width :] = jnp.where(lane < BORDER, rights[plane], 0.0)
    few_slots(
        cur, acc, doubled, amplitudes, plan, Plan.BESIDE_EDGE,
        plan[Plan.NUMBER, Plan.BESIDE_EDGE_END], (forth, back),
    )
    store_rows(acc, 0, tile, BAND, to_up, to_down)


def outer_rest_kernel(
    plan, cur, doubled, amplitudes, forth, back, acc_in,
    acc, to_left, to_right,
):
    few_slots(
        cur, acc, doubled, amplitudes, plan, Plan.BESIDE,
        plan[Plan.NUMBER, Plan.BESIDE_END], (forth, back),
    )
    sides = pack_side_bands(acc, to_left.shape[0])
    to_left[...], to_right[...] = by_side("col", *sides)


def corner_parts(band, width):
    is_low = lane_iota(band.shape[0]) < BORDER
    halo = unpack_planes(band[:, 2 * width :])
    lefts, rights = [], []
    for plane in range(2):
        low = band[:, plane * width : plane * width + LANES]
        high = band[:, (plane + 1) * width - LANES : (plane + 1) * width]
        lefts.append(jnp.where(is_low, low, halo[plane]))
        rights.append(jnp.where(is_low, halo[plane], high))
    return pack_planes(*lefts), pack_planes(*rights)


def corner_kernel(up, down, after, to_left, to_right):
    count = up.shape[0]
    width = (up.shape[1] - LANES) // 2
    up, down = by_side("row", up[...], down[...])
    tops, bottoms = corner_parts(up, width), corner_parts(down, width)
    to_left[...], to_right[...] = by_side(
        "col", *(jnp.concatenate([tops[i], bottoms[i]], axis=0) for i in range(2))
    )


def last_corner_kernel(up, down, left, right, after, to_left, to_right, whole):
    count = up.shape[0]
    tile = left.shape[0] - BAND
    width = (up.shape[1] - LANES) // 2
    up, down = by_side("row", up[...], down[...])
    tops, bottoms = corner_parts(up, width), corner_parts(down, width)
    parts = []
    for side, source in enumerate((left, right)):
        whole[...] = source[BORDER : BORDER + tile, :]
        whole[:count, :] += tops[side]
        whole[tile - count :, :] += bottoms[side]
        parts.append(fold_side(whole, side == 1))
    to_left[...], to_right[...] = by_side("col", *parts)


def deep_kernel(
    plan, objects, probe, doubled, amplitudes, forth, back, cur_in, acc_in,
    cur, acc, tile_held, sem,
):
    load = pltpu.make_async_copy(objects, tile_held, sem)
    load.start()
    tile, width = cur.shape[1] - SUBLANES - BAND, cur.shape[2] - 2 * LANES
    rate = step_of(probe)
    middle, inner = slice(BORDER, BORDER + tile), slice(LANES, LANES + width)
    begins = (plan[Plan.NUMBER, Plan.BAND_BEGIN], 0)
    ends = (plan[Plan.NUMBER, Plan.BAND_END], plan[Plan.NUMBER, Plan.SECOND_DEEP])

    def turn(iteration, carry):
        @pl.when(iteration == 1)
        def update():
            for plane in range(2):
                cur[plane, middle, inner] += rate * acc[plane, middle, inner]

        gradient_slots(
            cur, acc, doubled, amplitudes, plan, Plan.DEEP,
            jnp.where(iteration == 0, *begins), jnp.where(iteration == 0, *ends),
            (forth, back),
        )
        return carry

    lax.fori_loop(0, ITERS, turn, 0)
    load.wait()


def grid_gains(row_count, col_count, tile, rate):
    row_at, col_at = lax.axis_index("row"), lax.axis_index("col")
    top = jnp.where(row_at > 0, 1.0, 0.0)
    bottom = jnp.where(row_at < row_count - 1, 1.0, 0.0)
    before = jnp.where(col_at > 0, 1.0, 0.0)
    after = jnp.where(col_at < col_count - 1, 1.0, 0.0)
    row_id = lax.broadcasted_iota(jnp.int32, (tile + BAND, LANES), 0)
    row_gain = rate * jnp.where(
        row_id < BORDER, top, jnp.where(row_id >= BORDER + tile, bottom, 1.0)
    )
    return row_gain, top, bottom, before, after


def second_kernel(
    row_count, col_count,
    plan, probe, doubled, amplitudes, forth, back,
    up, down, left, right, cur_in, acc_in,
    cur, acc,
):
    tile, width = cur.shape[1] - SUBLANES - BAND, cur.shape[2] - 2 * LANES
    extent = tile + BAND
    rate = step_of(probe)
    row_gain, top, bottom, before, after = grid_gains(row_count, col_count, tile, rate)
    inner = slice(LANES, LANES + width)
    lane = lane_iota(extent)
    is_low, is_high = lane < BORDER, lane >= LANES - BORDER
    lefts, rights = map(unpack_planes, by_side("col", left[...], right[...]))
    up, down = by_side("row", up[...], down[...])
    for plane in range(2):
        for row, band, on_grid in ((0, up, top), (tile, down, bottom)):
            halo_first = row == 0
            values = band[:, plane * width : (plane + 1) * width]
            own, out = (BORDER, 0) if halo_first else (0, BORDER)
            own_rows = slice(row + own, row + own + BORDER)
            out_rows = slice(row + out, row + out + BORDER)
            cur[plane, own_rows, inner] += rate * values[own : own + BORDER]
            acc[plane, own_rows, inner] += values[own : own + BORDER]
            cur[plane, out_rows, inner] += (rate * on_grid) * (
                acc[plane, out_rows, inner] + values[out : out + BORDER]
            )
            acc[plane, out_rows, inner] = jnp.zeros_like(acc[plane, out_rows, inner])
            halo = unpack_planes(band[:, 2 * width :])[plane]
            for lanes, keep in (
                (slice(0, LANES), is_high[:BAND]),
                (slice(LANES + width, None), is_low[:BAND]),
            ):
                acc[plane, row : row + BAND, lanes] += jnp.where(keep, halo, 0.0)
        for block, band, on_grid, own_first in (
            (0, lefts[plane], before, False),
            (width, rights[plane], after, True),
        ):
            low_block = slice(block, block + LANES)
            high_block = slice(block + LANES, block + 2 * LANES)
            own, out = (low_block, high_block) if own_first else (high_block, low_block)
            keep_own, keep_out = (is_high, is_low) if own_first else (is_low, is_high)
            own_band = jnp.where(keep_own, band, 0.0)
            cur[plane, :extent, own] += row_gain * own_band
            acc[plane, BORDER : BORDER + tile, own] += own_band[BORDER : BORDER + tile]
            cur[plane, :extent, out] += (row_gain * on_grid) * (
                acc[plane, :extent, out] + jnp.where(keep_out, band, 0.0)
            )
            acc[plane, :extent, out] = jnp.zeros_like(acc[plane, :extent, out])
    gradient_slots(
        cur, acc, doubled, amplitudes, plan, Plan.SECOND, 0, plan[Plan.NUMBER, Plan.SECOND_STOP],
        (forth, back),
    )


def corner_slots_kernel(
    row_count, col_count,
    plan, probe, doubled, amplitudes, forth, back,
    left, right, cur_in, acc_in,
    cur, acc, to_up, to_down, to_left, to_right,
):
    tile, width = cur.shape[1] - SUBLANES - BAND, cur.shape[2] - 2 * LANES
    row_gain, _, _, before, after = grid_gains(row_count, col_count, tile, step_of(probe))
    lane = lane_iota(BAND)
    is_low, is_high = lane < BORDER, lane >= LANES - BORDER
    left, right = by_side("col", left[...], right[...])
    for block, corners, on_grid, own_first in (
        (0, left, before, False), (width, right, after, True),
    ):
        low_block = slice(block, block + LANES)
        high_block = slice(block + LANES, block + 2 * LANES)
        own, out = (low_block, high_block) if own_first else (high_block, low_block)
        keep_own, keep_out = (is_high, is_low) if own_first else (is_low, is_high)
        both = unpack_planes(corners)
        for plane in range(2):
            for row, own_at in ((0, BORDER), (tile, 0)):
                rows = slice(row, row + BAND)
                part = both[plane][:BAND] if row == 0 else both[plane][BAND:]
                own_part = jnp.where(keep_own, part, 0.0)
                gain = row_gain[rows]
                cur[plane, rows, own] += gain * own_part
                cur[plane, rows, out] += (gain * on_grid) * jnp.where(keep_out, part, 0.0)
                acc[plane, row + own_at : row + own_at + BORDER, own] += own_part[
                    own_at : own_at + BORDER
                ]
    few_slots(
        cur, acc, doubled, amplitudes, plan, Plan.CORNER,
        plan[Plan.NUMBER, Plan.CORNER_END], (forth, back),
    )
    store_rows(acc, 0, BORDER + tile, BORDER, to_up, to_down)
    to_left[...], to_right[...] = pack_side_bands(acc, to_left.shape[0])


def second_rest_kernel(
    plan, cur, doubled, amplitudes, forth, back, acc_in,
    acc,
):
    gradient_slots(
        cur, acc, doubled, amplitudes, plan, Plan.SECOND,
        plan[Plan.NUMBER, Plan.SECOND_STOP], plan[Plan.NUMBER, Plan.REST_END],
        (forth, back),
    )


def store_rows(acc, top, bottom, count, to_up, to_down):
    ups = pack_row_band(acc, top, count), pack_row_band(acc, bottom, count)
    to_up[...], to_down[...] = by_side("row", *ups)


def middle_kernel(
    probe, up, down, acc, held, estimate, correction, estimated, corrected, sems,
):
    tile, width = held.shape[1:]
    rate = step_of(probe)
    lanes = slice(LANES, width - LANES)
    up, down = by_side("row", up[...], down[...])
    for plane in range(2):
        total = acc[plane, BORDER : BORDER + tile, 2 * LANES : width]
        at = slice(plane * width + LANES, (plane + 1) * width - LANES)
        corrected[plane] = rate * jnp.concatenate(
            [
                total[:BORDER] + up[:, at],
                total[BORDER : tile - BORDER],
                total[tile - BORDER :] + down[:, at],
            ],
            axis=0,
        )
        estimated[plane] = held[plane, :, lanes] + corrected[plane]
    stores = [
        pltpu.make_async_copy(
            source, target.at[:, :, pl.ds(LANES, width - 2 * LANES)], sems.at[i]
        )
        for i, (source, target) in enumerate(((corrected, correction), (estimated, estimate)))
    ]
    for store in stores:
        store.start()
    for store in stores:
        store.wait()


def last_kernel(
    probe, up, down, left, right, acc, held, estimate_in, correction_in,
    estimate, correction, parts, sems,
):
    tile, width = held.shape[1:]
    rate = step_of(probe)
    lane = lane_iota(tile)
    rows = slice(BORDER, BORDER + tile)
    lefts, rights = map(unfold_side, by_side("col", left[...], right[...]))
    up, down = by_side("row", up[...], down[...])
    stores = []
    for side, (block, bands) in enumerate(((0, lefts), (width - LANES, rights))):
        keep = (lane < BORDER) if side == 0 else (lane >= LANES - BORDER)
        for plane in range(2):
            at = plane * width + block
            total = acc[plane, rows, LANES + block : 2 * LANES + block]
            total += jnp.where(keep, bands[plane], 0.0)
            total = jnp.concatenate(
                [
                    total[:BORDER] + up[:, at : at + LANES],
                    total[BORDER : tile - BORDER],
                    total[tile - BORDER :] + down[:, at : at + LANES],
                ],
                axis=0,
            )
            parts[0, side, plane] = rate * total
            parts[1, side, plane] = held[plane, :, block : block + LANES] + parts[0, side, plane]
            for number, target in enumerate((correction, estimate)):
                store = pltpu.make_async_copy(
                    parts.at[number, side, plane],
                    target.at[plane, :, pl.ds(block, LANES)],
                    sems.at[side, plane, number],
                )
                store.start()
                stores.append(store)
    for store in stores:
        store.wait()


VMEM = pl.BlockSpec(memory_space=pltpu.VMEM)
SMEM = pl.BlockSpec(memory_space=pltpu.SMEM)
HBM = pl.BlockSpec(memory_space=pltpu.HBM)
PARAMS = pltpu.CompilerParams(vmem_limit_bytes=32 * 1024 * 1024)


def f32(*shape):
    return pltpu.VMEM(shape, jnp.float32)


def in_hbm(array):
    return pltpu.with_memory_space_constraint(array, pltpu.HBM)


def in_smem(array):
    return pltpu.with_memory_space_constraint(array, pltpu.SMEM)


def in_vmem(array):
    return pltpu.with_memory_space_constraint(array, pltpu.VMEM)


def swap_pairs(axis, first, second):
    count = lax.axis_size(axis)

    def swap(array, begin):
        ends = [(i, i + 1) for i in range(begin, count - 1, 2)]
        return in_vmem(lax.ppermute(array, axis, ends + [(j, i) for i, j in ends]))

    first = swap(first, 0)
    second = swap(second, 1)
    return first, second


def on_device(object_field, probe_field, amplitudes, positions, counts):
    tile, width = object_field.shape[1:]
    probe = probe_field.shape[1]
    extent = tile + BAND
    padded = f32(2, extent + SUBLANES, width + 2 * LANES)
    doubled_shape = f32(2, 2 * probe, probe)
    tables = tuple(jnp.asarray(table) for table in dft_blocks(probe))
    places = positions[0, 0]
    plan_shape = pltpu.SMEM(Plan.shape(amplitudes.shape[0]), jnp.int32)
    sides = (f32(extent, LANES), f32(extent, LANES))

    def row_bands(count):
        band = f32(count, 2 * width + LANES)
        return (band, band)

    def call(kernel, scalars, arrays, outs, scratch=(), aliases=None):
        return pl.pallas_call(
            kernel,
            out_shape=outs,
            in_specs=[SMEM] * len(scalars) + [VMEM] * len(arrays),
            out_specs=jax.tree.map(lambda out: VMEM, outs),
            scratch_shapes=list(scratch),
            input_output_aliases=aliases or {},
            compiler_params=PARAMS,
        )(*scalars, *arrays)

    slots = (in_hbm(places), counts)
    strips = [
        jnp.concatenate([object_field[0, rows], object_field[1, rows]], axis=1)
        for rows in (slice(0, BORDER), slice(tile - BORDER, tile))
    ]
    table_shapes = tuple(pltpu.VMEM(table.shape, table.dtype) for table in tables)
    up, down = swap_pairs("row", *by_side("row", *strips))
    cur, acc, doubled, held, plan, *tables = pl.pallas_call(
        start_kernel,
        out_shape=(
            padded, padded, doubled_shape, f32(*amplitudes.shape), plan_shape, *table_shapes,
        ),
        in_specs=[SMEM, SMEM] + [HBM] * (3 + len(tables)),
        out_specs=(VMEM,) * 4 + (SMEM,) + (VMEM,) * len(tables),
        scratch_shapes=[pltpu.SemaphoreType.DMA((7 + len(tables),))],
        compiler_params=PARAMS,
        name="start",
    )(*slots, *map(in_hbm, (object_field, probe_field, amplitudes, *tables)))
    slots = (in_smem(plan),)
    to_left, to_right = call(
        object_pack_kernel, (), (cur, up, down),
        (f32(extent // 2, LANES),) * 2, (f32(extent, LANES),),
    )
    left, right = swap_pairs("col", to_left, to_right)
    cur, acc = call(
        side_kernel, slots, (up, down, doubled, held, *tables, cur, acc),
        (padded, padded), (), {7: 0, 8: 1},
    )
    cur, acc, to_up, to_down = call(
        outer_kernel, slots, (left, right, doubled, held, *tables, cur, acc),
        (padded, padded, *row_bands(BAND)), (), {7: 0, 8: 1},
    )
    up, down = swap_pairs("row", to_up, to_down)
    acc, to_left, to_right = call(
        outer_rest_kernel, slots, (cur, doubled, held, *tables, acc),
        (padded, *sides), (), {6: 0},
    )
    left, right = swap_pairs("col", to_left, to_right)
    cur, acc, tile_held = pl.pallas_call(
        deep_kernel,
        out_shape=(padded, padded, f32(2, tile, width)),
        in_specs=[SMEM, HBM] + [VMEM] * 7,
        out_specs=(VMEM,) * 3,
        scratch_shapes=[pltpu.SemaphoreType.DMA(())],
        input_output_aliases={7: 0, 8: 1},
        compiler_params=PARAMS,
        name="deep",
    )(*slots, in_hbm(object_field), probe_field, doubled, held, *tables, cur, acc)
    corners = (f32(2 * BAND, LANES),) * 2
    left_corners, right_corners = swap_pairs("col", *call(corner_kernel, (), (up, down, acc), corners))
    grid = (lax.axis_size("row"), lax.axis_size("col"))
    cur, acc = call(
        functools.partial(second_kernel, *grid), slots,
        (probe_field, doubled, held, *tables, up, down, left, right, cur, acc),
        (padded, padded), (), {10: 0, 11: 1},
    )
    cur, acc, to_up, to_down, to_left, to_right = call(
        functools.partial(corner_slots_kernel, *grid), slots,
        (probe_field, doubled, held, *tables, left_corners, right_corners, cur, acc),
        (padded, padded, *row_bands(BORDER), *sides), (), {8: 0, 9: 1},
    )
    up, down = swap_pairs("row", to_up, to_down)
    acc = call(
        second_rest_kernel, slots, (cur, doubled, held, *tables, acc),
        padded, (), {6: 0},
    )
    folded = f32(tile // 2, LANES)
    to_left, to_right = call(
        last_corner_kernel, (), (up, down, to_left, to_right, acc),
        (folded, folded), (f32(tile, LANES),),
    )
    left, right = swap_pairs("col", to_left, to_right)
    result = jax.ShapeDtypeStruct((2, tile, width), jnp.float32)
    middle = f32(2, tile, width - 2 * LANES)
    estimate, correction = pl.pallas_call(
        middle_kernel,
        out_shape=(result, result),
        in_specs=[VMEM] * 5,
        out_specs=(HBM, HBM),
        scratch_shapes=[middle, middle, pltpu.SemaphoreType.DMA((2,))],
        compiler_params=PARAMS,
        name="middle",
    )(probe_field, up, down, acc, tile_held)
    estimate, correction = pl.pallas_call(
        last_kernel,
        out_shape=(result, result),
        in_specs=[VMEM] * 7 + [HBM] * 2,
        out_specs=(HBM, HBM),
        scratch_shapes=[
            f32(2, 2, 2, tile, LANES), pltpu.SemaphoreType.DMA((2, 2, 2)),
        ],
        input_output_aliases={7: 0, 8: 1},
        compiler_params=PARAMS,
        name="finish",
    )(probe_field, up, down, left, right, acc, tile_held, estimate, correction)
    return estimate, correction


def solution(mesh):
    placed = (
        P(None, "row", "col"),
        P(),
        P("row", None, "col"),
        P("row", "col", None, None),
        P("row", "col"),
    )
    return jax.shard_map(
        on_device,
        mesh=mesh,
        in_specs=placed,
        out_specs=(P(None, "row", "col"), P(None, "row", "col")),
        check_vma=False,
    )
```

```python
import functools

import jax
import jax.numpy as jnp
import numpy as np
from jax import lax
from jax.experimental import pallas as pl
from jax.experimental.pallas import tpu as pltpu
from jax.sharding import PartitionSpec as P

BORDER = 32
BAND = 2 * BORDER
ITERS = 2
LANES = 128
SUBLANES = 8
LARGE, MIDDLE, SMALL = 8, 4, 2
RIGHT = 4

smoothing = 0.5
step_gain = 0.5


def split_host(table):
    high = table.astype(jnp.bfloat16)
    low = (table - high.astype(np.float64)).astype(jnp.bfloat16)
    return high, low


def dft_blocks(length):
    counter = np.arange(length)
    angles = 2.0 * np.pi * (np.outer(counter, counter) % length) / length
    real, imag = np.cos(angles) / np.sqrt(length), -np.sin(angles) / np.sqrt(length)
    blocks = []
    for sign in (1.0, -1.0):
        block = np.block([[real, sign * imag], [-sign * imag, real]])
        blocks.append(np.concatenate(split_host(block), axis=0))
    return blocks


def split(value):
    high = value.astype(jnp.bfloat16)
    low = (value - high.astype(jnp.float32)).astype(jnp.bfloat16)
    return high, low


def dot(left, right):
    return jnp.dot(left, right, preferred_element_type=jnp.float32)


def times_right(rows, block):
    high, low = split(rows)
    count = block.shape[0] // 2
    stacked = jnp.concatenate([block[:count], block], axis=0)
    return dot(jnp.concatenate([high, low, high], axis=1), stacked)


def right_groups(members, block):
    rows = members[0].shape[0]
    results = []
    count = min(RIGHT, len(members) // 2)
    for start in range(0, len(members), count):
        product = times_right(jnp.concatenate(members[start : start + count], axis=0), block[...])
        results += [product[i * rows : (i + 1) * rows] for i in range(count)]
    return results


def times_left(block, columns):
    high, low = split(columns)
    count = block.shape[0] // 2
    both = dot(block, high)
    return both[:count] + (both[count:] + dot(block[:count], low))


def lane_iota(rows):
    return lax.broadcasted_iota(jnp.int32, (rows, LANES), 1)


def edge_lanes(rows):
    lane = lane_iota(rows)
    return (lane < BORDER) | (lane >= LANES - BORDER)


def pack_planes(real, imag):
    return jnp.where(edge_lanes(real.shape[0]), real, pltpu.roll(imag, LANES // 2, 1))


def unpack_planes(packed):
    return packed, pltpu.roll(packed, LANES // 2, 1)


def slot_kinds(row, col, last):
    row_out, col_out = (row < 0) | (row > last), (col < 0) | (col > last)
    row_edge = (row < BORDER) | (row > last - BORDER)
    col_edge = (col < BORDER) | (col > last - BORDER)
    return row_out, col_out, row_edge, col_edge


def is_deep(row_out, col_out, row_edge, col_edge):
    return jnp.logical_not(row_edge | col_edge)


def is_beside(row_out, col_out, row_edge, col_edge):
    return col_out & jnp.logical_not(row_edge)


def is_beside_edge(row_out, col_out, row_edge, col_edge):
    return col_out & row_edge


def is_early(row_out, col_out, row_edge, col_edge):
    return (row_edge | col_edge) & jnp.logical_not(col_out)


def is_reaching(row_out, col_out, row_edge, col_edge):
    return (row_out | col_out) & jnp.logical_not(row_edge & col_edge)


def is_rim(row_out, col_out, row_edge, col_edge):
    return (row_edge ^ col_edge) & jnp.logical_not(row_out | col_out)


def is_reaching_corner(row_out, col_out, row_edge, col_edge):
    return (row_out | col_out) & row_edge & col_edge


def is_rim_corner(row_out, col_out, row_edge, col_edge):
    return row_edge & col_edge & jnp.logical_not(row_out | col_out)


class Plan:
    DEEP, SIDE, BESIDE, SECOND, CORNER, RIM, RIM_CORNER, BESIDE_EDGE, ROW, COL, NUMBER = range(11)
    SIDE_STOP, BAND_BEGIN, BAND_END, SECOND_DEEP, BESIDE_END, SECOND_STOP, REST_END, CORNER_END, BESIDE_EDGE_END = range(9)
    BAND_GROUPS, REST_GROUPS = 2, 2

    @staticmethod
    def shape(slot_total):
        return 11, max(slot_total + 1, 9)

    @staticmethod
    def fill(plan, positions, live, last):
        kinds = (
            (Plan.DEEP, is_deep), (Plan.SIDE, is_early), (Plan.BESIDE, is_beside),
            (Plan.SECOND, is_reaching), (Plan.RIM, is_rim), (Plan.RIM_CORNER, is_rim_corner),
            (Plan.CORNER, is_reaching_corner), (Plan.BESIDE_EDGE, is_beside_edge),
        )

        def visit(slot, found):
            row, col = positions[0, slot], positions[1, slot]
            plan[Plan.ROW, slot] = row
            plan[Plan.COL, slot] = col
            where = slot_kinds(row, col, last)
            counted = []
            for (listed, kind), number in zip(kinds, found):
                plan[listed, number] = slot
                counted.append(number + jnp.where(kind(*where), 1, 0))
            return tuple(counted)

        deep, early, beside, reaching, rim, rim_corner, corner, beside_edge = lax.fori_loop(
            0, live, visit, (0,) * len(kinds)
        )

        def extend(listed, begin, source, first, count):
            def move(index, carry):
                plan[listed, begin + index - first] = plan[source, index]
                return carry

            lax.fori_loop(first, count, move, 0)
            return begin + count - first

        side_stop = jnp.minimum(extend(Plan.SIDE, early, Plan.DEEP, 0, deep), round_up(early))
        done = side_stop - early
        second_end = extend(Plan.SECOND, reaching, Plan.RIM, 0, rim)
        second_stop = jnp.minimum(second_end, round_up(reaching))

        def deep_taken(groups):
            room = (groups - (deep - done + LARGE - 1) // LARGE) * LARGE
            return jnp.minimum(deep, jnp.maximum(room, 0))

        left = second_end - second_stop + rim_corner + deep - deep_taken(Plan.BAND_GROUPS)
        crowded = left > Plan.REST_GROUPS * LARGE
        second_deep = deep_taken(Plan.BAND_GROUPS + jnp.where(crowded, 1, 0))
        end = extend(Plan.SECOND, second_end, Plan.RIM_CORNER, 0, rim_corner)
        numbers = (
            side_stop, done, deep, second_deep, beside,
            second_stop,
            extend(Plan.SECOND, end, Plan.DEEP, second_deep, deep),
            corner, beside_edge,
        )
        for index, number in enumerate(numbers):
            plan[Plan.NUMBER, index] = number


def round_up(count):
    return jnp.maximum((count + LARGE - 1) // LARGE, 1) * LARGE


def gradient_slots(cur, acc, doubled, amplitudes, plan, listed, begin, stop, tables, size=LARGE):
    right_f, right_b = tables
    left_f, left_b = right_b, right_f
    probe = doubled.shape[1] // 2
    frame = probe + SUBLANES
    lane = lane_iota(frame)
    sub = lax.broadcasted_iota(jnp.int32, (SUBLANES, LANES), 0)

    def group_body(group, carry):
        places, probes, exits = [], [], []
        for member in range(size):
            slot = begin + group * size + member
            at = plan[listed, jnp.minimum(slot, stop - 1)]
            row = plan[Plan.ROW, at] + BORDER
            col = plan[Plan.COL, at] + LANES
            row_at = pl.multiple_of(row // SUBLANES * SUBLANES, SUBLANES)
            col_at = pl.multiple_of(col // LANES * LANES, LANES)
            row_off, col_off = row - row_at, col - col_at
            from_left = lane >= col_off
            from_top = sub >= row_off
            planes, rolled = [], []
            for plane in range(2):
                wide = jnp.where(
                    from_left,
                    cur[plane, pl.ds(row_at, frame), pl.ds(col_at, LANES)],
                    cur[plane, pl.ds(row_at, frame), pl.ds(col_at + LANES, LANES)],
                )
                first = jnp.where(from_top, wide[:SUBLANES], wide[probe:])
                planes.append(jnp.concatenate([first, wide[SUBLANES:probe]], axis=0))
                shifted = doubled[plane, pl.ds(probe - row_off, probe), :]
                rolled.append(pltpu.roll(shifted, col_off, 1))
            places.append((at, slot, row_at, col_at, from_left, from_top))
            probes.append(rolled)
            exits.append(
                jnp.concatenate(
                    [
                        rolled[0] * planes[0] - rolled[1] * planes[1],
                        rolled[0] * planes[1] + rolled[1] * planes[0],
                    ],
                    axis=1,
                )
            )
        half = right_groups(exits, right_f)
        shrunk = []
        for pair in range(0, size, 2):
            first, second = half[pair], half[pair + 1]
            stacked = jnp.concatenate(
                [
                    jnp.concatenate([first[:, :probe], second[:, :probe]], axis=1),
                    jnp.concatenate([first[:, probe:], second[:, probe:]], axis=1),
                ],
                axis=0,
            )
            wave = times_left(left_f[...], stacked)
            for member in range(2):
                at = places[pair + member][0]
                real = wave[:probe, member * probe : (member + 1) * probe]
                imag = wave[probe:, member * probe : (member + 1) * probe]
                shrink = amplitudes[at] * lax.rsqrt(real * real + imag * imag + smoothing) - 1.0
                shrunk.append(jnp.concatenate([real * shrink, imag * shrink], axis=1))
        half = right_groups(shrunk, right_b)
        for pair in range(0, size, 2):
            first, second = half[pair], half[pair + 1]
            stacked = jnp.concatenate(
                [
                    jnp.concatenate([first[:, :probe], second[:, :probe]], axis=1),
                    jnp.concatenate([first[:, probe:], second[:, probe:]], axis=1),
                ],
                axis=0,
            )
            back = times_left(left_b[...], stacked)
            for member in range(2):
                at, slot, row_at, col_at, from_left, from_top = places[pair + member]
                real = back[:probe, member * probe : (member + 1) * probe]
                imag = back[probe:, member * probe : (member + 1) * probe]
                rolled = probes[pair + member]
                grads = (
                    rolled[0] * real + rolled[1] * imag,
                    rolled[0] * imag - rolled[1] * real,
                )
                is_live = slot < stop
                keep_left = from_left & is_live
                keep_right = jnp.logical_not(from_left) & is_live
                for plane in range(2):
                    grad = grads[plane]
                    frame_grad = jnp.concatenate(
                        [
                            jnp.where(from_top, grad[:SUBLANES], 0.0),
                            grad[SUBLANES:],
                            jnp.where(from_top, 0.0, grad[:SUBLANES]),
                        ],
                        axis=0,
                    )
                    rows = pl.ds(row_at, frame)
                    acc[plane, rows, pl.ds(col_at, LANES)] += jnp.where(keep_left, frame_grad, 0.0)
                    acc[plane, rows, pl.ds(col_at + LANES, LANES)] += jnp.where(
                        keep_right, frame_grad, 0.0
                    )
        return carry

    lax.fori_loop(0, (stop - begin + size - 1) // size, group_body, 0)


def few_slots(cur, acc, doubled, amplitudes, plan, listed, stop, tables):
    whole = jnp.minimum((stop + 1) // MIDDLE * MIDDLE, stop)
    gradient_slots(cur, acc, doubled, amplitudes, plan, listed, 0, whole, tables, MIDDLE)
    gradient_slots(cur, acc, doubled, amplitudes, plan, listed, whole, stop, tables, SMALL)


def step_of(probe):
    return step_gain / (jnp.max(probe[0] * probe[0] + probe[1] * probe[1]) + 1e-06)


def pack_row_band(acc, row, count):
    rows = slice(row, row + count)
    width = acc.shape[2] - 2 * LANES
    is_low = lane_iota(count) < BORDER
    halo = [
        jnp.where(is_low, acc[plane, rows, LANES + width :], acc[plane, rows, :LANES])
        for plane in range(2)
    ]
    own = [acc[plane, rows, LANES : LANES + width] for plane in range(2)]
    return jnp.concatenate([*own, pack_planes(*halo)], axis=1)


def pack_side_bands(acc, height):
    width = acc.shape[2] - 2 * LANES
    is_low = lane_iota(height) < BORDER
    return [
        pack_planes(
            *[
                jnp.where(
                    is_low,
                    acc[plane, :height, block + LANES : block + 2 * LANES],
                    acc[plane, :height, block : block + LANES],
                )
                for plane in range(2)
            ]
        )
        for block in (0, width)
    ]


def start_kernel(
    positions, counts, objects, probe_in, amplitudes, *refs
):
    table_count = (len(refs) - 6) // 2
    tables_in, refs = refs[:table_count], refs[table_count:]
    cur, acc, doubled, held, plan = refs[:5]
    tables, sems = refs[5:-1], refs[-1]
    tile, width = objects.shape[1:]
    probe = probe_in.shape[1]
    sources = list(zip(tables_in, tables))
    for plane in range(2):
        sources.append(
            (
                objects.at[plane],
                cur.at[plane, pl.ds(BORDER, tile), pl.ds(LANES, width)],
            )
        )
        for row in (0, probe):
            sources.append((probe_in.at[plane], doubled.at[plane, pl.ds(row, probe), :]))
    sources.append((amplitudes, held))
    loads = [
        pltpu.make_async_copy(source, target, sems.at[i])
        for i, (source, target) in enumerate(sources)
    ]
    for load in loads:
        load.start()
    acc[...] = jnp.zeros_like(acc)
    Plan.fill(plan, positions, counts[0, 0], tile - probe)
    for load in loads:
        load.wait()


def side_kernel(
    plan, up, down, doubled, amplitudes, forth, back, cur_in, acc_in,
    cur, acc,
):
    tile, width = cur.shape[1] - SUBLANES - BAND, cur.shape[2] - 2 * LANES
    up, down = by_side("row", up[...], down[...])
    inner = slice(LANES, LANES + width)
    for plane in range(2):
        lanes = slice(plane * width, (plane + 1) * width)
        cur[plane, :BORDER, inner] = up[:, lanes]
        cur[plane, BORDER + tile : BAND + tile, inner] = down[:, lanes]
        cur[plane, BAND + tile :, :] = jnp.zeros_like(cur[plane, BAND + tile :, :])
    gradient_slots(
        cur, acc, doubled, amplitudes, plan, Plan.SIDE, 0, plan[Plan.NUMBER, Plan.SIDE_STOP],
        (forth, back),
    )


def fold_side(whole, is_low):
    half = whole.shape[0] // 2
    low = lane_iota(half) % (LANES // 2) < BORDER
    keep = low if is_low else jnp.logical_not(low)
    return jnp.where(keep, whole[:half, :], pltpu.roll(whole[half:, :], BORDER, 1))


def unfold_side(packed):
    return unpack_planes(
        jnp.concatenate([packed, pltpu.roll(packed, LANES - BORDER, 1)], axis=0)
    )


def by_side(axis, first, second):
    even = lax.axis_index(axis) % 2 == 0
    return jnp.where(even, second, first), jnp.where(even, first, second)


def object_pack_kernel(cur, up, down, to_left, to_right, whole):
    count = up.shape[0]
    width = up.shape[1] // 2
    extent = whole.shape[0]
    rows = slice(count, extent - count)
    up, down = by_side("row", up[...], down[...])
    parts = []
    for side in range(2):
        block = side * (width - LANES)
        for row, band in ((0, up), (extent - count, down)):
            whole[row : row + count, :] = pack_planes(
                *[
                    band[:, plane * width + block : plane * width + block + LANES]
                    for plane in range(2)
                ]
            )
        lanes = slice(LANES + block, 2 * LANES + block)
        whole[rows, :] = pack_planes(cur[0, rows, lanes], cur[1, rows, lanes])
        parts.append(fold_side(whole, side == 0))
    to_left[...], to_right[...] = by_side("col", *parts)


def outer_kernel(
    plan, left, right, doubled, amplitudes, forth, back, cur_in, acc_in,
    cur, acc, to_up, to_down,
):
    extent = 2 * left.shape[0]
    tile, width = extent - BAND, cur.shape[2] - 2 * LANES
    lane = lane_iota(extent)
    lefts, rights = map(unfold_side, by_side("col", left[...], right[...]))
    for plane in range(2):
        cur[plane, :extent, :LANES] = jnp.where(lane >= LANES - BORDER, lefts[plane], 0.0)
        cur[plane, :extent, LANES + width :] = jnp.where(lane < BORDER, rights[plane], 0.0)
    few_slots(
        cur, acc, doubled, amplitudes, plan, Plan.BESIDE_EDGE,
        plan[Plan.NUMBER, Plan.BESIDE_EDGE_END], (forth, back),
    )
    store_rows(acc, 0, tile, BAND, to_up, to_down)


def outer_rest_kernel(
    plan, cur, doubled, amplitudes, forth, back, acc_in,
    acc, to_left, to_right,
):
    few_slots(
        cur, acc, doubled, amplitudes, plan, Plan.BESIDE,
        plan[Plan.NUMBER, Plan.BESIDE_END], (forth, back),
    )
    sides = pack_side_bands(acc, to_left.shape[0])
    to_left[...], to_right[...] = by_side("col", *sides)


def corner_parts(band, width):
    is_low = lane_iota(band.shape[0]) < BORDER
    halo = unpack_planes(band[:, 2 * width :])
    lefts, rights = [], []
    for plane in range(2):
        low = band[:, plane * width : plane * width + LANES]
        high = band[:, (plane + 1) * width - LANES : (plane + 1) * width]
        lefts.append(jnp.where(is_low, low, halo[plane]))
        rights.append(jnp.where(is_low, halo[plane], high))
    return pack_planes(*lefts), pack_planes(*rights)


def corner_kernel(up, down, after, to_left, to_right):
    count = up.shape[0]
    width = (up.shape[1] - LANES) // 2
    up, down = by_side("row", up[...], down[...])
    tops, bottoms = corner_parts(up, width), corner_parts(down, width)
    to_left[...], to_right[...] = by_side(
        "col", *(jnp.concatenate([tops[i], bottoms[i]], axis=0) for i in range(2))
    )


def last_corner_kernel(up, down, left, right, after, to_left, to_right, whole):
    count = up.shape[0]
    tile = left.shape[0] - BAND
    width = (up.shape[1] - LANES) // 2
    up, down = by_side("row", up[...], down[...])
    tops, bottoms = corner_parts(up, width), corner_parts(down, width)
    parts = []
    for side, source in enumerate((left, right)):
        whole[...] = source[BORDER : BORDER + tile, :]
        whole[:count, :] += tops[side]
        whole[tile - count :, :] += bottoms[side]
        parts.append(fold_side(whole, side == 1))
    to_left[...], to_right[...] = by_side("col", *parts)


def deep_kernel(
    plan, objects, probe, doubled, amplitudes, forth, back, cur_in, acc_in,
    cur, acc, tile_held, sem,
):
    load = pltpu.make_async_copy(objects, tile_held, sem)
    load.start()
    tile, width = cur.shape[1] - SUBLANES - BAND, cur.shape[2] - 2 * LANES
    rate = step_of(probe)
    middle, inner = slice(BORDER, BORDER + tile), slice(LANES, LANES + width)
    begins = (plan[Plan.NUMBER, Plan.BAND_BEGIN], 0)
    ends = (plan[Plan.NUMBER, Plan.BAND_END], plan[Plan.NUMBER, Plan.SECOND_DEEP])

    def turn(iteration, carry):
        @pl.when(iteration == 1)
        def update():
            for plane in range(2):
                cur[plane, middle, inner] += rate * acc[plane, middle, inner]

        gradient_slots(
            cur, acc, doubled, amplitudes, plan, Plan.DEEP,
            jnp.where(iteration == 0, *begins), jnp.where(iteration == 0, *ends),
            (forth, back),
        )
        return carry

    lax.fori_loop(0, ITERS, turn, 0)
    load.wait()


def grid_gains(row_count, col_count, tile, rate):
    row_at, col_at = lax.axis_index("row"), lax.axis_index("col")
    top = jnp.where(row_at > 0, 1.0, 0.0)
    bottom = jnp.where(row_at < row_count - 1, 1.0, 0.0)
    before = jnp.where(col_at > 0, 1.0, 0.0)
    after = jnp.where(col_at < col_count - 1, 1.0, 0.0)
    row_id = lax.broadcasted_iota(jnp.int32, (tile + BAND, LANES), 0)
    row_gain = rate * jnp.where(
        row_id < BORDER, top, jnp.where(row_id >= BORDER + tile, bottom, 1.0)
    )
    return row_gain, top, bottom, before, after


def second_kernel(
    row_count, col_count,
    plan, probe, doubled, amplitudes, forth, back,
    up, down, left, right, cur_in, acc_in,
    cur, acc,
):
    tile, width = cur.shape[1] - SUBLANES - BAND, cur.shape[2] - 2 * LANES
    extent = tile + BAND
    rate = step_of(probe)
    row_gain, top, bottom, before, after = grid_gains(row_count, col_count, tile, rate)
    inner = slice(LANES, LANES + width)
    lane = lane_iota(extent)
    is_low, is_high = lane < BORDER, lane >= LANES - BORDER
    lefts, rights = map(unpack_planes, by_side("col", left[...], right[...]))
    up, down = by_side("row", up[...], down[...])
    for plane in range(2):
        for row, band, on_grid in ((0, up, top), (tile, down, bottom)):
            halo_first = row == 0
            values = band[:, plane * width : (plane + 1) * width]
            own, out = (BORDER, 0) if halo_first else (0, BORDER)
            own_rows = slice(row + own, row + own + BORDER)
            out_rows = slice(row + out, row + out + BORDER)
            cur[plane, own_rows, inner] += rate * values[own : own + BORDER]
            acc[plane, own_rows, inner] += values[own : own + BORDER]
            cur[plane, out_rows, inner] += (rate * on_grid) * (
                acc[plane, out_rows, inner] + values[out : out + BORDER]
            )
            acc[plane, out_rows, inner] = jnp.zeros_like(acc[plane, out_rows, inner])
            halo = unpack_planes(band[:, 2 * width :])[plane]
            for lanes, keep in (
                (slice(0, LANES), is_high[:BAND]),
                (slice(LANES + width, None), is_low[:BAND]),
            ):
                acc[plane, row : row + BAND, lanes] += jnp.where(keep, halo, 0.0)
        for block, band, on_grid, own_first in (
            (0, lefts[plane], before, False),
            (width, rights[plane], after, True),
        ):
            low_block = slice(block, block + LANES)
            high_block = slice(block + LANES, block + 2 * LANES)
            own, out = (low_block, high_block) if own_first else (high_block, low_block)
            keep_own, keep_out = (is_high, is_low) if own_first else (is_low, is_high)
            own_band = jnp.where(keep_own, band, 0.0)
            cur[plane, :extent, own] += row_gain * own_band
            acc[plane, BORDER : BORDER + tile, own] += own_band[BORDER : BORDER + tile]
            cur[plane, :extent, out] += (row_gain * on_grid) * (
                acc[plane, :extent, out] + jnp.where(keep_out, band, 0.0)
            )
            acc[plane, :extent, out] = jnp.zeros_like(acc[plane, :extent, out])
    gradient_slots(
        cur, acc, doubled, amplitudes, plan, Plan.SECOND, 0, plan[Plan.NUMBER, Plan.SECOND_STOP],
        (forth, back),
    )


def corner_slots_kernel(
    row_count, col_count,
    plan, probe, doubled, amplitudes, forth, back,
    left, right, cur_in, acc_in,
    cur, acc, to_up, to_down, to_left, to_right,
):
    tile, width = cur.shape[1] - SUBLANES - BAND, cur.shape[2] - 2 * LANES
    row_gain, _, _, before, after = grid_gains(row_count, col_count, tile, step_of(probe))
    lane = lane_iota(BAND)
    is_low, is_high = lane < BORDER, lane >= LANES - BORDER
    left, right = by_side("col", left[...], right[...])
    for block, corners, on_grid, own_first in (
        (0, left, before, False), (width, right, after, True),
    ):
        low_block = slice(block, block + LANES)
        high_block = slice(block + LANES, block + 2 * LANES)
        own, out = (low_block, high_block) if own_first else (high_block, low_block)
        keep_own, keep_out = (is_high, is_low) if own_first else (is_low, is_high)
        both = unpack_planes(corners)
        for plane in range(2):
            for row, own_at in ((0, BORDER), (tile, 0)):
                rows = slice(row, row + BAND)
                part = both[plane][:BAND] if row == 0 else both[plane][BAND:]
                own_part = jnp.where(keep_own, part, 0.0)
                gain = row_gain[rows]
                cur[plane, rows, own] += gain * own_part
                cur[plane, rows, out] += (gain * on_grid) * jnp.where(keep_out, part, 0.0)
                acc[plane, row + own_at : row + own_at + BORDER, own] += own_part[
                    own_at : own_at + BORDER
                ]
    few_slots(
        cur, acc, doubled, amplitudes, plan, Plan.CORNER,
        plan[Plan.NUMBER, Plan.CORNER_END], (forth, back),
    )
    store_rows(acc, 0, BORDER + tile, BORDER, to_up, to_down)
    to_left[...], to_right[...] = pack_side_bands(acc, to_left.shape[0])


def second_rest_kernel(
    plan, cur, doubled, amplitudes, forth, back, acc_in,
    acc,
):
    gradient_slots(
        cur, acc, doubled, amplitudes, plan, Plan.SECOND,
        plan[Plan.NUMBER, Plan.SECOND_STOP], plan[Plan.NUMBER, Plan.REST_END],
        (forth, back),
    )


def store_rows(acc, top, bottom, count, to_up, to_down):
    ups = pack_row_band(acc, top, count), pack_row_band(acc, bottom, count)
    to_up[...], to_down[...] = by_side("row", *ups)


def middle_kernel(
    probe, up, down, acc, held, estimate, correction, estimated, corrected, sems,
):
    tile, width = held.shape[1:]
    rate = step_of(probe)
    lanes = slice(LANES, width - LANES)
    up, down = by_side("row", up[...], down[...])
    for plane in range(2):
        total = acc[plane, BORDER : BORDER + tile, 2 * LANES : width]
        at = slice(plane * width + LANES, (plane + 1) * width - LANES)
        corrected[plane] = rate * jnp.concatenate(
            [
                total[:BORDER] + up[:, at],
                total[BORDER : tile - BORDER],
                total[tile - BORDER :] + down[:, at],
            ],
            axis=0,
        )
        estimated[plane] = held[plane, :, lanes] + corrected[plane]
    stores = [
        pltpu.make_async_copy(
            source, target.at[:, :, pl.ds(LANES, width - 2 * LANES)], sems.at[i]
        )
        for i, (source, target) in enumerate(((corrected, correction), (estimated, estimate)))
    ]
    for store in stores:
        store.start()
    for store in stores:
        store.wait()


def last_kernel(
    probe, up, down, left, right, acc, held, estimate_in, correction_in,
    estimate, correction, parts, sems,
):
    tile, width = held.shape[1:]
    rate = step_of(probe)
    lane = lane_iota(tile)
    rows = slice(BORDER, BORDER + tile)
    lefts, rights = map(unfold_side, by_side("col", left[...], right[...]))
    up, down = by_side("row", up[...], down[...])
    stores = []
    for side, (block, bands) in enumerate(((0, lefts), (width - LANES, rights))):
        keep = (lane < BORDER) if side == 0 else (lane >= LANES - BORDER)
        for plane in range(2):
            at = plane * width + block
            total = acc[plane, rows, LANES + block : 2 * LANES + block]
            total += jnp.where(keep, bands[plane], 0.0)
            total = jnp.concatenate(
                [
                    total[:BORDER] + up[:, at : at + LANES],
                    total[BORDER : tile - BORDER],
                    total[tile - BORDER :] + down[:, at : at + LANES],
                ],
                axis=0,
            )
            parts[0, side, plane] = rate * total
            parts[1, side, plane] = held[plane, :, block : block + LANES] + parts[0, side, plane]
            for number, target in enumerate((correction, estimate)):
                store = pltpu.make_async_copy(
                    parts.at[number, side, plane],
                    target.at[plane, :, pl.ds(block, LANES)],
                    sems.at[side, plane, number],
                )
                store.start()
                stores.append(store)
    for store in stores:
        store.wait()


VMEM = pl.BlockSpec(memory_space=pltpu.VMEM)
SMEM = pl.BlockSpec(memory_space=pltpu.SMEM)
HBM = pl.BlockSpec(memory_space=pltpu.HBM)
PARAMS = pltpu.CompilerParams(vmem_limit_bytes=32 * 1024 * 1024)


def f32(*shape):
    return pltpu.VMEM(shape, jnp.float32)


def in_hbm(array):
    return pltpu.with_memory_space_constraint(array, pltpu.HBM)


def in_smem(array):
    return pltpu.with_memory_space_constraint(array, pltpu.SMEM)


def in_vmem(array):
    return pltpu.with_memory_space_constraint(array, pltpu.VMEM)


def swap_pairs(axis, first, second):
    count = lax.axis_size(axis)

    def swap(array, begin):
        ends = [(i, i + 1) for i in range(begin, count - 1, 2)]
        return in_vmem(lax.ppermute(array, axis, ends + [(j, i) for i, j in ends]))

    first = swap(first, 0)
    second = swap(second, 1)
    return first, second


def on_device(object_field, probe_field, amplitudes, positions, counts):
    tile, width = object_field.shape[1:]
    probe = probe_field.shape[1]
    extent = tile + BAND
    padded = f32(2, extent + SUBLANES, width + 2 * LANES)
    doubled_shape = f32(2, 2 * probe, probe)
    tables = tuple(jnp.asarray(table) for table in dft_blocks(probe))
    places = positions[0, 0]
    plan_shape = pltpu.SMEM(Plan.shape(amplitudes.shape[0]), jnp.int32)
    sides = (f32(extent, LANES), f32(extent, LANES))

    def row_bands(count):
        band = f32(count, 2 * width + LANES)
        return (band, band)

    def call(kernel, scalars, arrays, outs, scratch=(), aliases=None):
        return pl.pallas_call(
            kernel,
            out_shape=outs,
            in_specs=[SMEM] * len(scalars) + [VMEM] * len(arrays),
            out_specs=jax.tree.map(lambda out: VMEM, outs),
            scratch_shapes=list(scratch),
            input_output_aliases=aliases or {},
            compiler_params=PARAMS,
        )(*scalars, *arrays)

    slots = (in_hbm(places), counts)
    strips = [
        jnp.concatenate([object_field[0, rows], object_field[1, rows]], axis=1)
        for rows in (slice(0, BORDER), slice(tile - BORDER, tile))
    ]
    table_shapes = tuple(pltpu.VMEM(table.shape, table.dtype) for table in tables)
    up, down = swap_pairs("row", *by_side("row", *strips))
    cur, acc, doubled, held, plan, *tables = pl.pallas_call(
        start_kernel,
        out_shape=(
            padded, padded, doubled_shape, f32(*amplitudes.shape), plan_shape, *table_shapes,
        ),
        in_specs=[SMEM, SMEM] + [HBM] * (3 + len(tables)),
        out_specs=(VMEM,) * 4 + (SMEM,) + (VMEM,) * len(tables),
        scratch_shapes=[pltpu.SemaphoreType.DMA((7 + len(tables),))],
        compiler_params=PARAMS,
        name="start",
    )(*slots, *map(in_hbm, (object_field, probe_field, amplitudes, *tables)))
    slots = (in_smem(plan),)
    to_left, to_right = call(
        object_pack_kernel, (), (cur, up, down),
        (f32(extent // 2, LANES),) * 2, (f32(extent, LANES),),
    )
    left, right = swap_pairs("col", to_left, to_right)
    cur, acc = call(
        side_kernel, slots, (up, down, doubled, held, *tables, cur, acc),
        (padded, padded), (), {7: 0, 8: 1},
    )
    cur, acc, to_up, to_down = call(
        outer_kernel, slots, (left, right, doubled, held, *tables, cur, acc),
        (padded, padded, *row_bands(BAND)), (), {7: 0, 8: 1},
    )
    up, down = swap_pairs("row", to_up, to_down)
    acc, to_left, to_right = call(
        outer_rest_kernel, slots, (cur, doubled, held, *tables, acc),
        (padded, *sides), (), {6: 0},
    )
    left, right = swap_pairs("col", to_left, to_right)
    cur, acc, tile_held = pl.pallas_call(
        deep_kernel,
        out_shape=(padded, padded, f32(2, tile, width)),
        in_specs=[SMEM, HBM] + [VMEM] * 7,
        out_specs=(VMEM,) * 3,
        scratch_shapes=[pltpu.SemaphoreType.DMA(())],
        input_output_aliases={7: 0, 8: 1},
        compiler_params=PARAMS,
        name="deep",
    )(*slots, in_hbm(object_field), probe_field, doubled, held, *tables, cur, acc)
    corners = (f32(2 * BAND, LANES),) * 2
    left_corners, right_corners = swap_pairs("col", *call(corner_kernel, (), (up, down, acc), corners))
    grid = (lax.axis_size("row"), lax.axis_size("col"))
    cur, acc = call(
        functools.partial(second_kernel, *grid), slots,
        (probe_field, doubled, held, *tables, up, down, left, right, cur, acc),
        (padded, padded), (), {10: 0, 11: 1},
    )
    cur, acc, to_up, to_down, to_left, to_right = call(
        functools.partial(corner_slots_kernel, *grid), slots,
        (probe_field, doubled, held, *tables, left_corners, right_corners, cur, acc),
        (padded, padded, *row_bands(BORDER), *sides), (), {8: 0, 9: 1},
    )
    up, down = swap_pairs("row", to_up, to_down)
    acc = call(
        second_rest_kernel, slots, (cur, doubled, held, *tables, acc),
        padded, (), {6: 0},
    )
    folded = f32(tile // 2, LANES)
    to_left, to_right = call(
        last_corner_kernel, (), (up, down, to_left, to_right, acc),
        (folded, folded), (f32(tile, LANES),),
    )
    left, right = swap_pairs("col", to_left, to_right)
    result = jax.ShapeDtypeStruct((2, tile, width), jnp.float32)
    middle = f32(2, tile, width - 2 * LANES)
    estimate, correction = pl.pallas_call(
        middle_kernel,
        out_shape=(result, result),
        in_specs=[VMEM] * 5,
        out_specs=(HBM, HBM),
        scratch_shapes=[middle, middle, pltpu.SemaphoreType.DMA((2,))],
        compiler_params=PARAMS,
        name="middle",
    )(probe_field, up, down, acc, tile_held)
    estimate, correction = pl.pallas_call(
        last_kernel,
        out_shape=(result, result),
        in_specs=[VMEM] * 7 + [HBM] * 2,
        out_specs=(HBM, HBM),
        scratch_shapes=[
            f32(2, 2, 2, tile, LANES), pltpu.SemaphoreType.DMA((2, 2, 2)),
        ],
        input_output_aliases={7: 0, 8: 1},
        compiler_params=PARAMS,
        name="finish",
    )(probe_field, up, down, left, right, acc, tile_held, estimate, correction)
    return estimate, correction


def solution(mesh):
    placed = (
        P(None, "row", "col"),
        P(),
        P("row", None, "col"),
        P("row", "col", None, None),
        P("row", "col"),
    )
    return jax.shard_map(
        on_device,
        mesh=mesh,
        in_specs=placed,
        out_specs=(P(None, "row", "col"), P(None, "row", "col")),
        check_vma=False,
    )
```

```python
import functools

import jax
import jax.numpy as jnp
import numpy as np
from jax import lax
from jax.experimental import pallas as pl
from jax.experimental.pallas import tpu as pltpu
from jax.sharding import PartitionSpec as P

BORDER = 32
BAND = 2 * BORDER
ITERS = 2
LANES = 128
SUBLANES = 8
LARGE, MIDDLE, SMALL = 8, 4, 2
RIGHT = 4

smoothing = 0.5
step_gain = 0.5


def split_host(table):
    high = table.astype(jnp.bfloat16)
    low = (table - high.astype(np.float64)).astype(jnp.bfloat16)
    return high, low


def dft_blocks(length):
    counter = np.arange(length)
    angles = 2.0 * np.pi * (np.outer(counter, counter) % length) / length
    real, imag = np.cos(angles) / np.sqrt(length), -np.sin(angles) / np.sqrt(length)
    blocks = []
    for sign in (1.0, -1.0):
        block = np.block([[real, sign * imag], [-sign * imag, real]])
        blocks.append(np.concatenate(split_host(block), axis=0))
    return blocks


def split(value):
    high = value.astype(jnp.bfloat16)
    low = (value - high.astype(jnp.float32)).astype(jnp.bfloat16)
    return high, low


def dot(left, right):
    return jnp.dot(left, right, preferred_element_type=jnp.float32)


def times_right(rows, block):
    high, low = split(rows)
    count = block.shape[0] // 2
    stacked = jnp.concatenate([block[:count], block], axis=0)
    return dot(jnp.concatenate([high, low, high], axis=1), stacked)


def right_groups(members, block):
    rows = members[0].shape[0]
    results = []
    count = min(RIGHT, len(members) // 2)
    for start in range(0, len(members), count):
        product = times_right(jnp.concatenate(members[start : start + count], axis=0), block[...])
        results += [product[i * rows : (i + 1) * rows] for i in range(count)]
    return results


def times_left(block, columns):
    high, low = split(columns)
    count = block.shape[0] // 2
    both = dot(block, high)
    return both[:count] + (both[count:] + dot(block[:count], low))


def lane_iota(rows):
    return lax.broadcasted_iota(jnp.int32, (rows, LANES), 1)


def edge_lanes(rows):
    lane = lane_iota(rows)
    return (lane < BORDER) | (lane >= LANES - BORDER)


def pack_planes(real, imag):
    return jnp.where(edge_lanes(real.shape[0]), real, pltpu.roll(imag, LANES // 2, 1))


def unpack_planes(packed):
    return packed, pltpu.roll(packed, LANES // 2, 1)


def slot_kinds(row, col, last):
    row_out, col_out = (row < 0) | (row > last), (col < 0) | (col > last)
    row_edge = (row < BORDER) | (row > last - BORDER)
    col_edge = (col < BORDER) | (col > last - BORDER)
    return row_out, col_out, row_edge, col_edge


def is_deep(row_out, col_out, row_edge, col_edge):
    return jnp.logical_not(row_edge | col_edge)


def is_beside(row_out, col_out, row_edge, col_edge):
    return col_out & jnp.logical_not(row_edge)


def is_beside_edge(row_out, col_out, row_edge, col_edge):
    return col_out & row_edge


def is_early(row_out, col_out, row_edge, col_edge):
    return (row_edge | col_edge) & jnp.logical_not(col_out)


def is_reaching(row_out, col_out, row_edge, col_edge):
    return (row_out | col_out) & jnp.logical_not(row_edge & col_edge)


def is_rim(row_out, col_out, row_edge, col_edge):
    return (row_edge ^ col_edge) & jnp.logical_not(row_out | col_out)


def is_reaching_corner(row_out, col_out, row_edge, col_edge):
    return (row_out | col_out) & row_edge & col_edge


def is_rim_corner(row_out, col_out, row_edge, col_edge):
    return row_edge & col_edge & jnp.logical_not(row_out | col_out)


class Plan:
    DEEP, SIDE, BESIDE, SECOND, CORNER, RIM, RIM_CORNER, BESIDE_EDGE, ROW, COL, NUMBER = range(11)
    SIDE_STOP, BAND_BEGIN, BAND_END, SECOND_DEEP, BESIDE_END, SECOND_STOP, REST_END, CORNER_END, BESIDE_EDGE_END = range(9)
    BAND_GROUPS, REST_GROUPS = 2, 2

    @staticmethod
    def shape(slot_total):
        return 11, max(slot_total + 1, 9)

    @staticmethod
    def fill(plan, positions, live, last):
        kinds = (
            (Plan.DEEP, is_deep), (Plan.SIDE, is_early), (Plan.BESIDE, is_beside),
            (Plan.SECOND, is_reaching), (Plan.RIM, is_rim), (Plan.RIM_CORNER, is_rim_corner),
            (Plan.CORNER, is_reaching_corner), (Plan.BESIDE_EDGE, is_beside_edge),
        )

        def visit(slot, found):
            row, col = positions[0, slot], positions[1, slot]
            plan[Plan.ROW, slot] = row
            plan[Plan.COL, slot] = col
            where = slot_kinds(row, col, last)
            counted = []
            for (listed, kind), number in zip(kinds, found):
                plan[listed, number] = slot
                counted.append(number + jnp.where(kind(*where), 1, 0))
            return tuple(counted)

        deep, early, beside, reaching, rim, rim_corner, corner, beside_edge = lax.fori_loop(
            0, live, visit, (0,) * len(kinds)
        )

        def extend(listed, begin, source, first, count):
            def move(index, carry):
                plan[listed, begin + index - first] = plan[source, index]
                return carry

            lax.fori_loop(first, count, move, 0)
            return begin + count - first

        side_stop = jnp.minimum(extend(Plan.SIDE, early, Plan.DEEP, 0, deep), round_up(early))
        done = side_stop - early
        second_end = extend(Plan.SECOND, reaching, Plan.RIM, 0, rim)
        second_stop = jnp.where(
            reaching <= MIDDLE, reaching, jnp.minimum(second_end, round_up(reaching))
        )

        def deep_taken(groups):
            room = (groups - (deep - done + LARGE - 1) // LARGE) * LARGE
            return jnp.minimum(deep, jnp.maximum(room, 0))

        left = second_end - second_stop + rim_corner + deep - deep_taken(Plan.BAND_GROUPS)
        crowded = left > Plan.REST_GROUPS * LARGE
        second_deep = deep_taken(Plan.BAND_GROUPS + jnp.where(crowded, 1, 0))
        end = extend(Plan.SECOND, second_end, Plan.RIM_CORNER, 0, rim_corner)
        numbers = (
            side_stop, done, deep, second_deep, beside,
            second_stop,
            extend(Plan.SECOND, end, Plan.DEEP, second_deep, deep),
            corner, beside_edge,
        )
        for index, number in enumerate(numbers):
            plan[Plan.NUMBER, index] = number


def round_up(count):
    return jnp.maximum((count + LARGE - 1) // LARGE, 1) * LARGE


def gradient_slots(cur, acc, doubled, amplitudes, plan, listed, begin, stop, tables, size=LARGE):
    right_f, right_b = tables
    left_f, left_b = right_b, right_f
    probe = doubled.shape[1] // 2
    frame = probe + SUBLANES
    lane = lane_iota(frame)
    sub = lax.broadcasted_iota(jnp.int32, (SUBLANES, LANES), 0)

    def group_body(group, carry):
        places, probes, exits = [], [], []
        for member in range(size):
            slot = begin + group * size + member
            at = plan[listed, jnp.minimum(slot, stop - 1)]
            row = plan[Plan.ROW, at] + BORDER
            col = plan[Plan.COL, at] + LANES
            row_at = pl.multiple_of(row // SUBLANES * SUBLANES, SUBLANES)
            col_at = pl.multiple_of(col // LANES * LANES, LANES)
            row_off, col_off = row - row_at, col - col_at
            from_left = lane >= col_off
            from_top = sub >= row_off
            planes, rolled = [], []
            for plane in range(2):
                wide = jnp.where(
                    from_left,
                    cur[plane, pl.ds(row_at, frame), pl.ds(col_at, LANES)],
                    cur[plane, pl.ds(row_at, frame), pl.ds(col_at + LANES, LANES)],
                )
                first = jnp.where(from_top, wide[:SUBLANES], wide[probe:])
                planes.append(jnp.concatenate([first, wide[SUBLANES:probe]], axis=0))
                shifted = doubled[plane, pl.ds(probe - row_off, probe), :]
                rolled.append(pltpu.roll(shifted, col_off, 1))
            places.append((at, slot, row_at, col_at, from_left, from_top))
            probes.append(rolled)
            exits.append(
                jnp.concatenate(
                    [
                        rolled[0] * planes[0] - rolled[1] * planes[1],
                        rolled[0] * planes[1] + rolled[1] * planes[0],
                    ],
                    axis=1,
                )
            )
        half = right_groups(exits, right_f)
        shrunk = []
        for pair in range(0, size, 2):
            first, second = half[pair], half[pair + 1]
            stacked = jnp.concatenate(
                [
                    jnp.concatenate([first[:, :probe], second[:, :probe]], axis=1),
                    jnp.concatenate([first[:, probe:], second[:, probe:]], axis=1),
                ],
                axis=0,
            )
            wave = times_left(left_f[...], stacked)
            for member in range(2):
                at = places[pair + member][0]
                real = wave[:probe, member * probe : (member + 1) * probe]
                imag = wave[probe:, member * probe : (member + 1) * probe]
                shrink = amplitudes[at] * lax.rsqrt(real * real + imag * imag + smoothing) - 1.0
                shrunk.append(jnp.concatenate([real * shrink, imag * shrink], axis=1))
        half = right_groups(shrunk, right_b)
        for pair in range(0, size, 2):
            first, second = half[pair], half[pair + 1]
            stacked = jnp.concatenate(
                [
                    jnp.concatenate([first[:, :probe], second[:, :probe]], axis=1),
                    jnp.concatenate([first[:, probe:], second[:, probe:]], axis=1),
                ],
                axis=0,
            )
            back = times_left(left_b[...], stacked)
            for member in range(2):
                at, slot, row_at, col_at, from_left, from_top = places[pair + member]
                real = back[:probe, member * probe : (member + 1) * probe]
                imag = back[probe:, member * probe : (member + 1) * probe]
                rolled = probes[pair + member]
                grads = (
                    rolled[0] * real + rolled[1] * imag,
                    rolled[0] * imag - rolled[1] * real,
                )
                is_live = slot < stop
                keep_left = from_left & is_live
                keep_right = jnp.logical_not(from_left) & is_live
                for plane in range(2):
                    grad = grads[plane]
                    frame_grad = jnp.concatenate(
                        [
                            jnp.where(from_top, grad[:SUBLANES], 0.0),
                            grad[SUBLANES:],
                            jnp.where(from_top, 0.0, grad[:SUBLANES]),
                        ],
                        axis=0,
                    )
                    rows = pl.ds(row_at, frame)
                    acc[plane, rows, pl.ds(col_at, LANES)] += jnp.where(keep_left, frame_grad, 0.0)
                    acc[plane, rows, pl.ds(col_at + LANES, LANES)] += jnp.where(
                        keep_right, frame_grad, 0.0
                    )
        return carry

    lax.fori_loop(0, (stop - begin + size - 1) // size, group_body, 0)


def few_slots(cur, acc, doubled, amplitudes, plan, listed, stop, tables):
    whole = jnp.minimum((stop + 1) // MIDDLE * MIDDLE, stop)
    gradient_slots(cur, acc, doubled, amplitudes, plan, listed, 0, whole, tables, MIDDLE)
    gradient_slots(cur, acc, doubled, amplitudes, plan, listed, whole, stop, tables, SMALL)


def step_of(probe):
    return step_gain / (jnp.max(probe[0] * probe[0] + probe[1] * probe[1]) + 1e-06)


def pack_row_band(acc, row, count):
    rows = slice(row, row + count)
    width = acc.shape[2] - 2 * LANES
    is_low = lane_iota(count) < BORDER
    halo = [
        jnp.where(is_low, acc[plane, rows, LANES + width :], acc[plane, rows, :LANES])
        for plane in range(2)
    ]
    own = [acc[plane, rows, LANES : LANES + width] for plane in range(2)]
    return jnp.concatenate([*own, pack_planes(*halo)], axis=1)


def pack_side_bands(acc, height):
    width = acc.shape[2] - 2 * LANES
    is_low = lane_iota(height) < BORDER
    return [
        pack_planes(
            *[
                jnp.where(
                    is_low,
                    acc[plane, :height, block + LANES : block + 2 * LANES],
                    acc[plane, :height, block : block + LANES],
                )
                for plane in range(2)
            ]
        )
        for block in (0, width)
    ]


def start_kernel(
    positions, counts, objects, probe_in, amplitudes, *refs
):
    table_count = (len(refs) - 6) // 2
    tables_in, refs = refs[:table_count], refs[table_count:]
    cur, acc, doubled, held, plan = refs[:5]
    tables, sems = refs[5:-1], refs[-1]
    tile, width = objects.shape[1:]
    probe = probe_in.shape[1]
    sources = list(zip(tables_in, tables))
    for plane in range(2):
        sources.append(
            (
                objects.at[plane],
                cur.at[plane, pl.ds(BORDER, tile), pl.ds(LANES, width)],
            )
        )
        for row in (0, probe):
            sources.append((probe_in.at[plane], doubled.at[plane, pl.ds(row, probe), :]))
    sources.append((amplitudes, held))
    loads = [
        pltpu.make_async_copy(source, target, sems.at[i])
        for i, (source, target) in enumerate(sources)
    ]
    for load in loads:
        load.start()
    acc[...] = jnp.zeros_like(acc)
    Plan.fill(plan, positions, counts[0, 0], tile - probe)
    for load in loads:
        load.wait()


def side_kernel(
    plan, up, down, doubled, amplitudes, forth, back, cur_in, acc_in,
    cur, acc,
):
    tile, width = cur.shape[1] - SUBLANES - BAND, cur.shape[2] - 2 * LANES
    up, down = by_side("row", up[...], down[...])
    inner = slice(LANES, LANES + width)
    for plane in range(2):
        lanes = slice(plane * width, (plane + 1) * width)
        cur[plane, :BORDER, inner] = up[:, lanes]
        cur[plane, BORDER + tile : BAND + tile, inner] = down[:, lanes]
        cur[plane, BAND + tile :, :] = jnp.zeros_like(cur[plane, BAND + tile :, :])
    gradient_slots(
        cur, acc, doubled, amplitudes, plan, Plan.SIDE, 0, plan[Plan.NUMBER, Plan.SIDE_STOP],
        (forth, back),
    )


def fold_side(whole, is_low):
    half = whole.shape[0] // 2
    low = lane_iota(half) % (LANES // 2) < BORDER
    keep = low if is_low else jnp.logical_not(low)
    return jnp.where(keep, whole[:half, :], pltpu.roll(whole[half:, :], BORDER, 1))


def unfold_side(packed):
    return unpack_planes(
        jnp.concatenate([packed, pltpu.roll(packed, LANES - BORDER, 1)], axis=0)
    )


def by_side(axis, first, second):
    even = lax.axis_index(axis) % 2 == 0
    return jnp.where(even, second, first), jnp.where(even, first, second)


def object_pack_kernel(cur, up, down, to_left, to_right, whole):
    count = up.shape[0]
    width = up.shape[1] // 2
    extent = whole.shape[0]
    rows = slice(count, extent - count)
    up, down = by_side("row", up[...], down[...])
    parts = []
    for side in range(2):
        block = side * (width - LANES)
        for row, band in ((0, up), (extent - count, down)):
            whole[row : row + count, :] = pack_planes(
                *[
                    band[:, plane * width + block : plane * width + block + LANES]
                    for plane in range(2)
                ]
            )
        lanes = slice(LANES + block, 2 * LANES + block)
        whole[rows, :] = pack_planes(cur[0, rows, lanes], cur[1, rows, lanes])
        parts.append(fold_side(whole, side == 0))
    to_left[...], to_right[...] = by_side("col", *parts)


def outer_kernel(
    plan, left, right, doubled, amplitudes, forth, back, cur_in, acc_in,
    cur, acc, to_up, to_down,
):
    extent = 2 * left.shape[0]
    tile, width = extent - BAND, cur.shape[2] - 2 * LANES
    lane = lane_iota(extent)
    lefts, rights = map(unfold_side, by_side("col", left[...], right[...]))
    for plane in range(2):
        cur[plane, :extent, :LANES] = jnp.where(lane >= LANES - BORDER, lefts[plane], 0.0)
        cur[plane, :extent, LANES + width :] = jnp.where(lane < BORDER, rights[plane], 0.0)
    few_slots(
        cur, acc, doubled, amplitudes, plan, Plan.BESIDE_EDGE,
        plan[Plan.NUMBER, Plan.BESIDE_EDGE_END], (forth, back),
    )
    store_rows(acc, 0, tile, BAND, to_up, to_down)


def outer_rest_kernel(
    plan, cur, doubled, amplitudes, forth, back, acc_in,
    acc, to_left, to_right,
):
    few_slots(
        cur, acc, doubled, amplitudes, plan, Plan.BESIDE,
        plan[Plan.NUMBER, Plan.BESIDE_END], (forth, back),
    )
    sides = pack_side_bands(acc, to_left.shape[0])
    to_left[...], to_right[...] = by_side("col", *sides)


def corner_parts(band, width):
    is_low = lane_iota(band.shape[0]) < BORDER
    halo = unpack_planes(band[:, 2 * width :])
    lefts, rights = [], []
    for plane in range(2):
        low = band[:, plane * width : plane * width + LANES]
        high = band[:, (plane + 1) * width - LANES : (plane + 1) * width]
        lefts.append(jnp.where(is_low, low, halo[plane]))
        rights.append(jnp.where(is_low, halo[plane], high))
    return pack_planes(*lefts), pack_planes(*rights)


def corner_kernel(up, down, after, to_left, to_right):
    count = up.shape[0]
    width = (up.shape[1] - LANES) // 2
    up, down = by_side("row", up[...], down[...])
    tops, bottoms = corner_parts(up, width), corner_parts(down, width)
    to_left[...], to_right[...] = by_side(
        "col", *(jnp.concatenate([tops[i], bottoms[i]], axis=0) for i in range(2))
    )


def last_corner_kernel(up, down, left, right, after, to_left, to_right, whole):
    count = up.shape[0]
    tile = left.shape[0] - BAND
    width = (up.shape[1] - LANES) // 2
    up, down = by_side("row", up[...], down[...])
    tops, bottoms = corner_parts(up, width), corner_parts(down, width)
    parts = []
    for side, source in enumerate((left, right)):
        whole[...] = source[BORDER : BORDER + tile, :]
        whole[:count, :] += tops[side]
        whole[tile - count :, :] += bottoms[side]
        parts.append(fold_side(whole, side == 1))
    to_left[...], to_right[...] = by_side("col", *parts)


def deep_kernel(
    plan, objects, probe, doubled, amplitudes, forth, back, cur_in, acc_in,
    cur, acc, tile_held, sem,
):
    load = pltpu.make_async_copy(objects, tile_held, sem)
    load.start()
    tile, width = cur.shape[1] - SUBLANES - BAND, cur.shape[2] - 2 * LANES
    rate = step_of(probe)
    middle, inner = slice(BORDER, BORDER + tile), slice(LANES, LANES + width)
    begins = (plan[Plan.NUMBER, Plan.BAND_BEGIN], 0)
    ends = (plan[Plan.NUMBER, Plan.BAND_END], plan[Plan.NUMBER, Plan.SECOND_DEEP])

    def turn(iteration, carry):
        @pl.when(iteration == 1)
        def update():
            for plane in range(2):
                cur[plane, middle, inner] += rate * acc[plane, middle, inner]

        gradient_slots(
            cur, acc, doubled, amplitudes, plan, Plan.DEEP,
            jnp.where(iteration == 0, *begins), jnp.where(iteration == 0, *ends),
            (forth, back),
        )
        return carry

    lax.fori_loop(0, ITERS, turn, 0)
    load.wait()


def grid_gains(row_count, col_count, tile, rate):
    row_at, col_at = lax.axis_index("row"), lax.axis_index("col")
    top = jnp.where(row_at > 0, 1.0, 0.0)
    bottom = jnp.where(row_at < row_count - 1, 1.0, 0.0)
    before = jnp.where(col_at > 0, 1.0, 0.0)
    after = jnp.where(col_at < col_count - 1, 1.0, 0.0)
    row_id = lax.broadcasted_iota(jnp.int32, (tile + BAND, LANES), 0)
    row_gain = rate * jnp.where(
        row_id < BORDER, top, jnp.where(row_id >= BORDER + tile, bottom, 1.0)
    )
    return row_gain, top, bottom, before, after


def second_kernel(
    row_count, col_count,
    plan, probe, doubled, amplitudes, forth, back,
    up, down, left, right, cur_in, acc_in,
    cur, acc,
):
    tile, width = cur.shape[1] - SUBLANES - BAND, cur.shape[2] - 2 * LANES
    extent = tile + BAND
    rate = step_of(probe)
    row_gain, top, bottom, before, after = grid_gains(row_count, col_count, tile, rate)
    inner = slice(LANES, LANES + width)
    lane = lane_iota(extent)
    is_low, is_high = lane < BORDER, lane >= LANES - BORDER
    lefts, rights = map(unpack_planes, by_side("col", left[...], right[...]))
    up, down = by_side("row", up[...], down[...])
    for plane in range(2):
        for row, band, on_grid in ((0, up, top), (tile, down, bottom)):
            halo_first = row == 0
            values = band[:, plane * width : (plane + 1) * width]
            own, out = (BORDER, 0) if halo_first else (0, BORDER)
            own_rows = slice(row + own, row + own + BORDER)
            out_rows = slice(row + out, row + out + BORDER)
            cur[plane, own_rows, inner] += rate * values[own : own + BORDER]
            acc[plane, own_rows, inner] += values[own : own + BORDER]
            cur[plane, out_rows, inner] += (rate * on_grid) * (
                acc[plane, out_rows, inner] + values[out : out + BORDER]
            )
            acc[plane, out_rows, inner] = jnp.zeros_like(acc[plane, out_rows, inner])
            halo = unpack_planes(band[:, 2 * width :])[plane]
            for lanes, keep in (
                (slice(0, LANES), is_high[:BAND]),
                (slice(LANES + width, None), is_low[:BAND]),
            ):
                acc[plane, row : row + BAND, lanes] += jnp.where(keep, halo, 0.0)
        for block, band, on_grid, own_first in (
            (0, lefts[plane], before, False),
            (width, rights[plane], after, True),
        ):
            low_block = slice(block, block + LANES)
            high_block = slice(block + LANES, block + 2 * LANES)
            own, out = (low_block, high_block) if own_first else (high_block, low_block)
            keep_own, keep_out = (is_high, is_low) if own_first else (is_low, is_high)
            own_band = jnp.where(keep_own, band, 0.0)
            cur[plane, :extent, own] += row_gain * own_band
            acc[plane, BORDER : BORDER + tile, own] += own_band[BORDER : BORDER + tile]
            cur[plane, :extent, out] += (row_gain * on_grid) * (
                acc[plane, :extent, out] + jnp.where(keep_out, band, 0.0)
            )
            acc[plane, :extent, out] = jnp.zeros_like(acc[plane, :extent, out])
    stop = plan[Plan.NUMBER, Plan.SECOND_STOP]
    few = jnp.where(stop <= MIDDLE, stop, 0)
    few_slots(cur, acc, doubled, amplitudes, plan, Plan.SECOND, few, (forth, back))
    gradient_slots(
        cur, acc, doubled, amplitudes, plan, Plan.SECOND, few, stop, (forth, back)
    )


def corner_slots_kernel(
    row_count, col_count,
    plan, probe, doubled, amplitudes, forth, back,
    left, right, cur_in, acc_in,
    cur, acc, to_up, to_down, to_left, to_right,
):
    tile, width = cur.shape[1] - SUBLANES - BAND, cur.shape[2] - 2 * LANES
    row_gain, _, _, before, after = grid_gains(row_count, col_count, tile, step_of(probe))
    lane = lane_iota(BAND)
    is_low, is_high = lane < BORDER, lane >= LANES - BORDER
    left, right = by_side("col", left[...], right[...])
    for block, corners, on_grid, own_first in (
        (0, left, before, False), (width, right, after, True),
    ):
        low_block = slice(block, block + LANES)
        high_block = slice(block + LANES, block + 2 * LANES)
        own, out = (low_block, high_block) if own_first else (high_block, low_block)
        keep_own, keep_out = (is_high, is_low) if own_first else (is_low, is_high)
        both = unpack_planes(corners)
        for plane in range(2):
            for row, own_at in ((0, BORDER), (tile, 0)):
                rows = slice(row, row + BAND)
                part = both[plane][:BAND] if row == 0 else both[plane][BAND:]
                own_part = jnp.where(keep_own, part, 0.0)
                gain = row_gain[rows]
                cur[plane, rows, own] += gain * own_part
                cur[plane, rows, out] += (gain * on_grid) * jnp.where(keep_out, part, 0.0)
                acc[plane, row + own_at : row + own_at + BORDER, own] += own_part[
                    own_at : own_at + BORDER
                ]
    few_slots(
        cur, acc, doubled, amplitudes, plan, Plan.CORNER,
        plan[Plan.NUMBER, Plan.CORNER_END], (forth, back),
    )
    store_rows(acc, 0, BORDER + tile, BORDER, to_up, to_down)
    to_left[...], to_right[...] = pack_side_bands(acc, to_left.shape[0])


def second_rest_kernel(
    plan, cur, doubled, amplitudes, forth, back, acc_in,
    acc,
):
    gradient_slots(
        cur, acc, doubled, amplitudes, plan, Plan.SECOND,
        plan[Plan.NUMBER, Plan.SECOND_STOP], plan[Plan.NUMBER, Plan.REST_END],
        (forth, back),
    )


def store_rows(acc, top, bottom, count, to_up, to_down):
    ups = pack_row_band(acc, top, count), pack_row_band(acc, bottom, count)
    to_up[...], to_down[...] = by_side("row", *ups)


def middle_kernel(
    probe, up, down, acc, held, estimate, correction, estimated, corrected, sems,
):
    tile, width = held.shape[1:]
    rate = step_of(probe)
    lanes = slice(LANES, width - LANES)
    up, down = by_side("row", up[...], down[...])
    for plane in range(2):
        total = acc[plane, BORDER : BORDER + tile, 2 * LANES : width]
        at = slice(plane * width + LANES, (plane + 1) * width - LANES)
        corrected[plane] = rate * jnp.concatenate(
            [
                total[:BORDER] + up[:, at],
                total[BORDER : tile - BORDER],
                total[tile - BORDER :] + down[:, at],
            ],
            axis=0,
        )
        estimated[plane] = held[plane, :, lanes] + corrected[plane]
    stores = [
        pltpu.make_async_copy(
            source, target.at[:, :, pl.ds(LANES, width - 2 * LANES)], sems.at[i]
        )
        for i, (source, target) in enumerate(((corrected, correction), (estimated, estimate)))
    ]
    for store in stores:
        store.start()
    for store in stores:
        store.wait()


def last_kernel(
    probe, up, down, left, right, acc, held, estimate_in, correction_in,
    estimate, correction, parts, sems,
):
    tile, width = held.shape[1:]
    rate = step_of(probe)
    lane = lane_iota(tile)
    rows = slice(BORDER, BORDER + tile)
    lefts, rights = map(unfold_side, by_side("col", left[...], right[...]))
    up, down = by_side("row", up[...], down[...])
    stores = []
    for side, (block, bands) in enumerate(((0, lefts), (width - LANES, rights))):
        keep = (lane < BORDER) if side == 0 else (lane >= LANES - BORDER)
        for plane in range(2):
            at = plane * width + block
            total = acc[plane, rows, LANES + block : 2 * LANES + block]
            total += jnp.where(keep, bands[plane], 0.0)
            total = jnp.concatenate(
                [
                    total[:BORDER] + up[:, at : at + LANES],
                    total[BORDER : tile - BORDER],
                    total[tile - BORDER :] + down[:, at : at + LANES],
                ],
                axis=0,
            )
            parts[0, side, plane] = rate * total
            parts[1, side, plane] = held[plane, :, block : block + LANES] + parts[0, side, plane]
            for number, target in enumerate((correction, estimate)):
                store = pltpu.make_async_copy(
                    parts.at[number, side, plane],
                    target.at[plane, :, pl.ds(block, LANES)],
                    sems.at[side, plane, number],
                )
                store.start()
                stores.append(store)
    for store in stores:
        store.wait()


VMEM = pl.BlockSpec(memory_space=pltpu.VMEM)
SMEM = pl.BlockSpec(memory_space=pltpu.SMEM)
HBM = pl.BlockSpec(memory_space=pltpu.HBM)
PARAMS = pltpu.CompilerParams(vmem_limit_bytes=32 * 1024 * 1024)


def f32(*shape):
    return pltpu.VMEM(shape, jnp.float32)


def in_hbm(array):
    return pltpu.with_memory_space_constraint(array, pltpu.HBM)


def in_smem(array):
    return pltpu.with_memory_space_constraint(array, pltpu.SMEM)


def in_vmem(array):
    return pltpu.with_memory_space_constraint(array, pltpu.VMEM)


def swap_pairs(axis, first, second):
    count = lax.axis_size(axis)

    def swap(array, begin):
        ends = [(i, i + 1) for i in range(begin, count - 1, 2)]
        return in_vmem(lax.ppermute(array, axis, ends + [(j, i) for i, j in ends]))

    first = swap(first, 0)
    second = swap(second, 1)
    return first, second


def on_device(object_field, probe_field, amplitudes, positions, counts):
    tile, width = object_field.shape[1:]
    probe = probe_field.shape[1]
    extent = tile + BAND
    padded = f32(2, extent + SUBLANES, width + 2 * LANES)
    doubled_shape = f32(2, 2 * probe, probe)
    tables = tuple(jnp.asarray(table) for table in dft_blocks(probe))
    places = positions[0, 0]
    plan_shape = pltpu.SMEM(Plan.shape(amplitudes.shape[0]), jnp.int32)
    sides = (f32(extent, LANES), f32(extent, LANES))

    def row_bands(count):
        band = f32(count, 2 * width + LANES)
        return (band, band)

    def call(kernel, scalars, arrays, outs, scratch=(), aliases=None):
        return pl.pallas_call(
            kernel,
            out_shape=outs,
            in_specs=[SMEM] * len(scalars) + [VMEM] * len(arrays),
            out_specs=jax.tree.map(lambda out: VMEM, outs),
            scratch_shapes=list(scratch),
            input_output_aliases=aliases or {},
            compiler_params=PARAMS,
        )(*scalars, *arrays)

    slots = (in_hbm(places), counts)
    strips = [
        jnp.concatenate([object_field[0, rows], object_field[1, rows]], axis=1)
        for rows in (slice(0, BORDER), slice(tile - BORDER, tile))
    ]
    table_shapes = tuple(pltpu.VMEM(table.shape, table.dtype) for table in tables)
    up, down = swap_pairs("row", *by_side("row", *strips))
    cur, acc, doubled, held, plan, *tables = pl.pallas_call(
        start_kernel,
        out_shape=(
            padded, padded, doubled_shape, f32(*amplitudes.shape), plan_shape, *table_shapes,
        ),
        in_specs=[SMEM, SMEM] + [HBM] * (3 + len(tables)),
        out_specs=(VMEM,) * 4 + (SMEM,) + (VMEM,) * len(tables),
        scratch_shapes=[pltpu.SemaphoreType.DMA((7 + len(tables),))],
        compiler_params=PARAMS,
        name="start",
    )(*slots, *map(in_hbm, (object_field, probe_field, amplitudes, *tables)))
    slots = (in_smem(plan),)
    to_left, to_right = call(
        object_pack_kernel, (), (cur, up, down),
        (f32(extent // 2, LANES),) * 2, (f32(extent, LANES),),
    )
    left, right = swap_pairs("col", to_left, to_right)
    cur, acc = call(
        side_kernel, slots, (up, down, doubled, held, *tables, cur, acc),
        (padded, padded), (), {7: 0, 8: 1},
    )
    cur, acc, to_up, to_down = call(
        outer_kernel, slots, (left, right, doubled, held, *tables, cur, acc),
        (padded, padded, *row_bands(BAND)), (), {7: 0, 8: 1},
    )
    up, down = swap_pairs("row", to_up, to_down)
    acc, to_left, to_right = call(
        outer_rest_kernel, slots, (cur, doubled, held, *tables, acc),
        (padded, *sides), (), {6: 0},
    )
    left, right = swap_pairs("col", to_left, to_right)
    cur, acc, tile_held = pl.pallas_call(
        deep_kernel,
        out_shape=(padded, padded, f32(2, tile, width)),
        in_specs=[SMEM, HBM] + [VMEM] * 7,
        out_specs=(VMEM,) * 3,
        scratch_shapes=[pltpu.SemaphoreType.DMA(())],
        input_output_aliases={7: 0, 8: 1},
        compiler_params=PARAMS,
        name="deep",
    )(*slots, in_hbm(object_field), probe_field, doubled, held, *tables, cur, acc)
    corners = (f32(2 * BAND, LANES),) * 2
    left_corners, right_corners = swap_pairs("col", *call(corner_kernel, (), (up, down, acc), corners))
    grid = (lax.axis_size("row"), lax.axis_size("col"))
    cur, acc = call(
        functools.partial(second_kernel, *grid), slots,
        (probe_field, doubled, held, *tables, up, down, left, right, cur, acc),
        (padded, padded), (), {10: 0, 11: 1},
    )
    cur, acc, to_up, to_down, to_left, to_right = call(
        functools.partial(corner_slots_kernel, *grid), slots,
        (probe_field, doubled, held, *tables, left_corners, right_corners, cur, acc),
        (padded, padded, *row_bands(BORDER), *sides), (), {8: 0, 9: 1},
    )
    up, down = swap_pairs("row", to_up, to_down)
    acc = call(
        second_rest_kernel, slots, (cur, doubled, held, *tables, acc),
        padded, (), {6: 0},
    )
    folded = f32(tile // 2, LANES)
    to_left, to_right = call(
        last_corner_kernel, (), (up, down, to_left, to_right, acc),
        (folded, folded), (f32(tile, LANES),),
    )
    left, right = swap_pairs("col", to_left, to_right)
    result = jax.ShapeDtypeStruct((2, tile, width), jnp.float32)
    middle = f32(2, tile, width - 2 * LANES)
    estimate, correction = pl.pallas_call(
        middle_kernel,
        out_shape=(result, result),
        in_specs=[VMEM] * 5,
        out_specs=(HBM, HBM),
        scratch_shapes=[middle, middle, pltpu.SemaphoreType.DMA((2,))],
        compiler_params=PARAMS,
        name="middle",
    )(probe_field, up, down, acc, tile_held)
    estimate, correction = pl.pallas_call(
        last_kernel,
        out_shape=(result, result),
        in_specs=[VMEM] * 7 + [HBM] * 2,
        out_specs=(HBM, HBM),
        scratch_shapes=[
            f32(2, 2, 2, tile, LANES), pltpu.SemaphoreType.DMA((2, 2, 2)),
        ],
        input_output_aliases={7: 0, 8: 1},
        compiler_params=PARAMS,
        name="finish",
    )(probe_field, up, down, left, right, acc, tile_held, estimate, correction)
    return estimate, correction


def solution(mesh):
    placed = (
        P(None, "row", "col"),
        P(),
        P("row", None, "col"),
        P("row", "col", None, None),
        P("row", "col"),
    )
    return jax.shard_map(
        on_device,
        mesh=mesh,
        in_specs=placed,
        out_specs=(P(None, "row", "col"), P(None, "row", "col")),
        check_vma=False,
    )
```
